32 devices in a mesh: range: 8 (over z, y), alt: 4 (over x, core), freq: 1.
Axes of the slice: x: 2, y: 2, z: 4, core: 2. Of those that a mesh axis runs over, the one named last changes fastest.
Arguments:
- freq_scale: float32 [2], P('freq'), may hold values from 1 to 2
- base_profile: float32 [1024], P('alt'), may hold values from 1.5 to 3
- perturb: float32 [32, 1024], P('range', 'alt'), may hold values from -1 to 1
- start_block: float32 [96, 1024], P(None, 'alt'), may hold values from -6 to 6
- source: float32 [2, 2, 96], P('freq'), may hold values from -6 to 6
Outputs:
- field: float32 [2, 32, 2, 1024], P('freq', 'range', None, 'alt')
The draws below stay inside these ranges and needn't reach their ends.
All inputs are finite; a program needn't handle non-finite values.
Results may differ from the reference program's by a relative error of at most 0.0003.
Values sent between devices are 32-bit elements; how exact they have to be, the bound alone decides.
No kernel may reach another device: no remote copies, remote signals or barrier semaphores. Data moves between devices by JAX's collectives and lax.ppermute only.
A program may use at most 128 MiB of HBM per device.

```python
import math
import jax
import jax.numpy as jnp
from jax import lax

ALT = 1024
MODES = 96
FREQS = 2
ITERS = 8
SEGMENTS = 32


def level_of(stream_key, extent, split, low, high):
    level, own = 1.0, jax.random.fold_in(stream_key, 6)
    for axis_at, shards_of in split:
        heights = jnp.exp(jax.random.uniform(jax.random.fold_in(own, axis_at), (shards_of,), jnp.float32, low / len(split), high / len(split)))
        level = level * jnp.repeat(heights, extent[axis_at] // shards_of).reshape([-1 if axis == axis_at else 1 for axis in range(len(extent))])
    return level


def bell_draw(rng, extent, scale, most, split=(), kind=jnp.bfloat16):
    gain = level_of(rng, extent, split, -0.22, 0.18) if split else 1.0
    entries = jax.random.normal(rng, extent, jnp.float32) * scale * gain
    return jnp.minimum(jnp.maximum(entries, -most), most).astype(kind)


def setup_inputs(seed: int = 0, part: int = 0) -> dict:
    keys = jax.random.split(jax.random.key(seed), 6)
    part_splits = jax.random.split(jax.random.fold_in(keys[5], part), 6)
    freq_scale = jnp.clip(jnp.exp(jax.random.uniform(part_splits[0], (FREQS,), jnp.float32, math.log(1.0), math.log(2.0))), 1.0, 2.0)
    base_profile = jnp.clip(1.5 + 1.5 * jax.random.uniform(keys[1], (ALT,), jnp.float32) ** level_of(keys[1], (ALT,), ((0, 4),), -0.2, 0.2), 1.5, 3.0)
    perturb = jnp.clip(jax.random.uniform(keys[2], (SEGMENTS, ALT), jnp.float32, -1.0, 1.0) * level_of(keys[2], (SEGMENTS, ALT), ((0, 8), (1, 4)), -0.4, 0.0), -1.0, 1.0)
    start_block = bell_draw(keys[3], (MODES, ALT), 1.0, 6.0, ((1, 4),), jnp.float32)
    source = bell_draw(part_splits[4], (FREQS, 2, MODES), 1.0, 6.0, (), jnp.float32)
    return dict(freq_scale=freq_scale, base_profile=base_profile, perturb=perturb, start_block=start_block, source=source)


phase_step = 0.15
relief = 0.1

def mult(left, right):
    return jnp.einsum('...ij,...jk->...ik', left, right, precision=lax.Precision.HIGHEST)

def apply_operator(block, coef):
    widths = [(0, 0)] * (block.ndim - 1) + [(1, 1)]
    padded = jnp.pad(block, widths)
    return coef * block + 0.5 * (padded[..., 2:] + padded[..., :-2])

def orthonormal(image):
    gram = jnp.einsum('...mz,...nz->...mn', image, image, precision=lax.Precision.HIGHEST)
    lower = jnp.linalg.cholesky(gram)
    return lax.linalg.triangular_solve(lower, image, left_side=True, lower=True)

def build_transfer(ritz, correlation):
    count = ritz.shape[-1]
    unit = jnp.eye(count, dtype=ritz.dtype)
    phase = phase_step * ritz
    square = mult(phase, phase)
    cosine = unit - 0.5 * square + mult(square, square) / 24.0
    sine = phase - mult(phase, square) / 6.0
    turned = mult(correlation, cosine)
    skewed = mult(correlation, sine)
    upper = jnp.concatenate([turned, -skewed], axis=-1)
    below = jnp.concatenate([skewed, turned], axis=-1)
    return jnp.concatenate([upper, below], axis=-2)

def reference(freq_scale, base_profile, perturb, start_block, source):
    coef = freq_scale[:, None, None, None] * (base_profile[None, :] * (1.0 + relief * perturb))[None, :, None, :]
    basis = jnp.broadcast_to(start_block / jnp.sqrt(float(ALT)), (FREQS, SEGMENTS, MODES, ALT))
    for step in range(ITERS):
        basis = orthonormal(apply_operator(basis, coef))
    himage = apply_operator(basis, coef)
    ritz = jnp.einsum('fsmz,fsnz->fsmn', basis, himage, precision=lax.Precision.HIGHEST)
    correlation = jnp.einsum('fsmz,fsnz->fsmn', basis[:, 1:], basis[:, :-1], precision=lax.Precision.HIGHEST)
    transfer = build_transfer(ritz[:, :-1], correlation)
    start = jnp.concatenate([source[:, 0], source[:, 1]], axis=-1)

    def advance(state, matrix):
        following = jnp.einsum('fij,fj->fi', matrix, state, precision=lax.Precision.HIGHEST)
        return (following, following)
    unused, later = lax.scan(advance, start, jnp.moveaxis(transfer, 1, 0))
    amps = jnp.concatenate([start[None], later], axis=0)
    amps = jnp.moveaxis(amps, 0, 1).reshape(FREQS, SEGMENTS, 2, MODES)
    scale = jnp.sqrt(float(ALT) / float(MODES))
    return scale * jnp.einsum('fspm,fsmz->fspz', amps, basis, precision=lax.Precision.HIGHEST)
```

```python
import functools

import jax
import jax.numpy as jnp
from jax import lax
from jax.experimental import pallas as pl
from jax.experimental.pallas import tpu as pltpu
from jax.sharding import PartitionSpec as P

ITERS = 8

phase_step = 0.15
relief = 0.1
HIGHEST = lax.Precision.HIGHEST
VMEM_LIMIT = 48 * 2**20


def mm(left, right):
    return lax.dot_general(
        left, right, (((1,), (0,)), ((), ())), precision=HIGHEST, preferred_element_type=jnp.float32
    )


def mmt(left, right):
    return lax.dot_general(
        left, right, (((1,), (1,)), ((), ())), precision=HIGHEST, preferred_element_type=jnp.float32
    )


def kernel_call(body, out_shape, args, specs, scratch=(), flops=0):
    nbytes = sum(4 * a.size for a in args) + sum(4 * o.size for o in jax.tree.leaves(out_shape))
    return pl.pallas_call(
        body,
        out_shape=out_shape,
        in_specs=specs,
        out_specs=jax.tree.map(lambda _: pl.BlockSpec(memory_space=pltpu.VMEM), out_shape),
        scratch_shapes=scratch,
        cost_estimate=pl.CostEstimate(flops=flops, bytes_accessed=nbytes, transcendentals=0),
        compiler_params=pltpu.CompilerParams(vmem_limit_bytes=VMEM_LIMIT),
    )(*args)


VM = pl.BlockSpec(memory_space=pltpu.VMEM)
SM = pl.BlockSpec(memory_space=pltpu.SMEM)


def shape(*dims):
    return jax.ShapeDtypeStruct(dims, jnp.float32)


def row_of(value, at):
    return jnp.broadcast_to(value[at : at + 1, :], value.shape)


def lane_of(value, at):
    return jnp.broadcast_to(value[:, at : at + 1], value.shape)


def inverse_factors(grams):
    blocks = len(grams[0])
    lanes = lax.broadcasted_iota(jnp.int32, (8, 128), 1)
    subs = lax.broadcasted_iota(jnp.int32, (8, 128), 0)
    works = [list(gram) for gram in grams]
    results = [[None] * blocks for _ in grams]
    for k in range(blocks):
        first = 8 * k
        panels = [
            [[lane_of(work[v], first + c) for v in range(k, blocks)] for c in range(8)]
            for work in works
        ]
        pivots = [jnp.ones((8, 128), jnp.float32) for _ in works]
        for c in range(8):
            for i, work in enumerate(works):
                panel = panels[i]
                pivot = row_of(panel[c][0], c)
                inv = pltpu.reciprocal(pivot, approx=True)
                inv = inv * (2.0 - pivot * inv)
                pivots[i] = jnp.where(subs == c, pivot, pivots[i])
                factor = [column * inv for column in panel[c]]
                factor[0] = jnp.where(subs > c, factor[0], 0.0)
                line = row_of(work[k], c) + jnp.where(lanes == first + c, 1.0, 0.0)
                for d in range(c + 1, 8):
                    weight = row_of(panel[d][0], c)
                    panel[d][0] = panel[d][0] - (panel[c][0] * weight) * inv
                    for v in range(1, blocks - k):
                        panel[d][v] = panel[d][v] - factor[v] * weight
                for v in range(blocks - k):
                    work[k + v] = work[k + v] - factor[v] * line
        for i, work in enumerate(works):
            unit = jnp.where(lanes == subs + first, 1.0, 0.0)
            results[i][k] = jnp.where(lanes < subs + first, work[k], unit) * lax.rsqrt(pivots[i])
    return results


def edge_weights(width):
    lanes = lax.broadcasted_iota(jnp.int32, (1, width), 1)
    return jnp.where(lanes == 0, 0.0, 0.5), jnp.where(lanes == width - 1, 0.0, 0.5)


def apply_rows(value, coef, from_low, from_high):
    width = value.shape[1]
    return (
        coef * value
        + from_low * pltpu.roll(value, 1, 1)
        + from_high * pltpu.roll(value, width - 1, 1)
    )


def iterate_body(n_alt, chunk, seg_count, modes, width, scale_ref, *refs):
    blocks = refs[:n_alt]
    out_refs = refs[n_alt : n_alt + chunk]
    coef_ref, image_ref, gram_ref, inv_ref = refs[n_alt + chunk :]
    place = lax.axis_index("alt")
    flat = place * chunk
    freq = flat // seg_count
    first = flat - freq * seg_count
    total = n_alt * width
    for k, block in enumerate(blocks):
        source = lax.rem(place + n_alt - k, n_alt)
        span = pl.ds(pl.multiple_of(source * width, width), width)
        start = block[0:modes, :] * (1.0 / float(total) ** 0.5)
        for i in range(chunk):
            out_refs[i][:, span] = start
            change = block[pl.ds(modes + 1 + first + i, 1), :]
            coef_ref[i : i + 1, span] = scale_ref[freq] * (
                block[modes : modes + 1, :] * (1.0 + relief * change)
            )
    from_low, from_high = edge_weights(total)
    down = 2.0**-11
    gram_ref[...] = jnp.zeros_like(gram_ref)

    def step(_, carry):
        for i in range(chunk):
            coef = coef_ref[i : i + 1, :]
            for at in range(0, modes, 8):
                image_ref[i, at : at + 8, :] = apply_rows(
                    out_refs[i][at : at + 8, :], coef, from_low, from_high
                )
            image = image_ref[i]
            gram_ref[i, :, 0:modes] = mmt(image, image) * down
        grams = [[gram_ref[i, at : at + 8, :] for at in range(0, modes, 8)] for i in range(chunk)]
        results = inverse_factors(grams)
        for i in range(chunk):
            for at in range(0, modes, 8):
                inv_ref[i, at : at + 8, :] = results[i][at // 8] * down**0.5
        for i in range(chunk):
            inv = inv_ref[i, :, 0:modes]
            for at in range(0, total, 256):
                out_refs[i][:, at : at + 256] = mm(inv, image_ref[i, :, at : at + 256])
        return carry

    lax.fori_loop(0, ITERS, step, 0)


def unit_of(modes):
    rows = lax.broadcasted_iota(jnp.int32, (modes, modes), 0)
    return jnp.where(rows == lax.broadcasted_iota(jnp.int32, (modes, modes), 1), 1.0, 0.0)


def complex_mm(left, right):
    return (
        mm(left[0], right[0]) - mm(left[1], right[1]),
        mm(left[0], right[1]) + mm(left[1], right[0]),
    )


def advance_body(modes, total, coef_ref, first_ref, second_ref, inner_ref, rest_ref, image_ref):
    from_low, from_high = edge_weights(total)
    unit = unit_of(modes)
    turns = []
    for i, ref in enumerate((first_ref, second_ref)):
        for at in range(0, modes, 8):
            image_ref[at : at + 8, :] = apply_rows(
                ref[at : at + 8, :], coef_ref[i : i + 1, :], from_low, from_high
            )
        phase = phase_step * mmt(ref[...], image_ref[...])
        square = mm(phase, phase)
        turns.append(
            (unit - 0.5 * square + mm(square, square) / 24.0, phase - mm(phase, square) / 6.0)
        )
    corr = mmt(second_ref[...], first_ref[...])
    inner = (mm(corr, turns[0][0]), mm(corr, turns[0][1]))
    rest = complex_mm(turns[1], inner)
    for part in range(2):
        inner_ref[part] = inner[part]
        rest_ref[part] = rest[part]


def product_body(next_ref, second_ref, rest_ref, out_ref):
    corr = mmt(next_ref[...], second_ref[...])
    for part in range(2):
        out_ref[part] = mm(corr, rest_ref[part])


def chain_place(halves):
    return lax.axis_index("range") * halves + lax.rem(lax.axis_index("alt"), halves)


def padded(ref, missing):
    return (ref[0] + jnp.where(missing, unit_of(ref.shape[1]), 0.0), ref[1])


def join_body(halves, back_new, back_old, new_ref, old_ref, out_ref):
    at = chain_place(halves)
    new = padded(new_ref, at < back_new) if back_new else (new_ref[0], new_ref[1])
    real, imag = complex_mm(new, padded(old_ref, at < back_old))
    out_ref[0] = real
    out_ref[1] = imag


def turn_vector(matrix, vector):
    rows = lax.broadcasted_iota(jnp.int32, vector.shape, 0)
    swapped = jnp.where(
        rows == 0, -row_of(vector, 1), jnp.where(rows == 1, row_of(vector, 0), 0.0)
    )
    return mmt(vector, matrix[0]) + mmt(swapped, matrix[1])


def source_rows(source_ref, halves):
    return source_ref[lax.axis_index("alt") // halves]


def early_body(halves, span_ref, source_ref, out_ref):
    out_ref[...] = turn_vector((span_ref[0], span_ref[1]), source_rows(source_ref, halves))


def field_body(halves, back, n_alt, width, scale, *refs):
    span_ref, early_ref, came_ref, inner_ref, first_ref, second_ref, out_ref = refs
    at = chain_place(halves)
    came = turn_vector((span_ref[0], span_ref[1]), came_ref[...])
    amp = jnp.where(at < back, early_ref[...], came)
    amps = (amp, turn_vector((inner_ref[0], inner_ref[1]), amp))
    for i, ref in enumerate((first_ref, second_ref)):
        for k in range(n_alt):
            part = mm(amps[i], ref[:, k * width : (k + 1) * width])
            out_ref[k, i] = scale * part[0:2, :]


def local(freq_scale, base_profile, perturb, start_block, source):
    freqs = freq_scale.shape[0]
    seg_count = perturb.shape[0]
    modes, width = start_block.shape
    n_alt = lax.axis_size("alt")
    n_range = lax.axis_size("range")
    total = width * n_alt
    chunk = freqs * seg_count // n_alt
    halves = seg_count // chunk
    length = n_range * halves
    assert chunk == 2 and halves * chunk == seg_count and halves * freqs == n_alt

    def along_chain(value, steps):
        pairs = []
        for freq in range(freqs):
            for at in range(max(0, -steps), min(length, length - steps)):
                ends = []
                for d in (at, at + steps):
                    ends.append(d // halves * n_alt + freq * halves + d % halves)
                pairs.append(tuple(ends))
        return lax.ppermute(value, ("range", "alt"), pairs)

    lines = [start_block, base_profile[None, :], perturb]
    filler = -(modes + 1 + seg_count) % 8
    mine = jnp.concatenate(lines + [jnp.zeros((filler, width), jnp.float32)], axis=0)
    blocks = [mine]
    for k in range(1, n_alt):
        blocks.append(lax.ppermute(mine, "alt", [(i, (i + k) % n_alt) for i in range(n_alt)]))
    flops = 2 * modes * modes * total
    first, second, coef = kernel_call(
        functools.partial(iterate_body, n_alt, chunk, seg_count, modes, width),
        [shape(modes, total)] * chunk + [shape(chunk, total)],
        [freq_scale] + blocks,
        [SM] + [VM] * n_alt,
        [pltpu.VMEM((chunk, modes, total), jnp.float32)]
        + [pltpu.VMEM((chunk, modes, 128), jnp.float32)] * 2,
        flops=2 * ITERS * chunk * flops,
    )
    following = along_chain(first, -1)
    inner, rest = kernel_call(
        functools.partial(advance_body, modes, total),
        [shape(2, modes, modes)] * 2,
        [coef, first, second],
        [VM] * 3,
        [pltpu.VMEM((modes, total), jnp.float32)],
        flops=8 * flops,
    )
    product = kernel_call(
        product_body, shape(2, modes, modes), [following, second, rest], [VM] * 3, flops=flops
    )
    reach = 2
    span = kernel_call(
        functools.partial(join_body, halves, 1, 2),
        shape(2, modes, modes),
        [along_chain(product, 1), along_chain(product, 2)],
        [VM] * 2,
        flops=flops,
    )
    while 2 * reach < length:
        span = kernel_call(
            functools.partial(join_body, halves, 0, reach),
            shape(2, modes, modes),
            [span, along_chain(span, reach)],
            [VM] * 2,
            flops=flops,
        )
        reach *= 2
    rows = jnp.concatenate([source, jnp.zeros((freqs, 6, modes), jnp.float32)], axis=1)
    early = kernel_call(
        functools.partial(early_body, halves), shape(8, modes), [span, rows], [VM] * 2
    )
    parts = kernel_call(
        functools.partial(
            field_body, halves, reach, n_alt, width, (float(total) / float(modes)) ** 0.5
        ),
        shape(n_alt, chunk, 2, width),
        [span, early, along_chain(early, reach), inner, first, second],
        [VM] * 6,
    )
    field = lax.all_to_all(parts, "alt", 0, 0)
    return field.reshape(freqs, seg_count, 2, width)


def solution(mesh):
    in_specs = (P("freq"), P("alt"), P("range", "alt"), P(None, "alt"), P("freq", None, None))
    out_specs = P("freq", "range", None, "alt")
    return jax.shard_map(local, mesh=mesh, in_specs=in_specs, out_specs=out_specs, check_vma=False)
```

```python
import functools

import jax
import jax.numpy as jnp
from jax import lax
from jax.experimental import pallas as pl
from jax.experimental.pallas import tpu as pltpu
from jax.sharding import PartitionSpec as P

ITERS = 8

phase_step = 0.15
relief = 0.1
HIGHEST = lax.Precision.HIGHEST
VMEM_LIMIT = 48 * 2**20
HALF = 48


def mm(left, right):
    return lax.dot_general(
        left, right, (((1,), (0,)), ((), ())), precision=HIGHEST, preferred_element_type=jnp.float32
    )


def mmt(left, right):
    return lax.dot_general(
        left, right, (((1,), (1,)), ((), ())), precision=HIGHEST, preferred_element_type=jnp.float32
    )


def short_mm(left, right):
    return lax.dot_general(
        left, right, (((1,), (0,)), ((), ())), preferred_element_type=jnp.float32
    )


def short_mmt(left, right):
    return lax.dot_general(
        left, right, (((1,), (1,)), ((), ())), preferred_element_type=jnp.float32
    )


def kernel_call(body, out_shape, args, specs, scratch=(), flops=0):
    nbytes = sum(4 * a.size for a in args) + sum(4 * o.size for o in jax.tree.leaves(out_shape))
    return pl.pallas_call(
        body,
        out_shape=out_shape,
        in_specs=specs,
        out_specs=jax.tree.map(lambda _: pl.BlockSpec(memory_space=pltpu.VMEM), out_shape),
        scratch_shapes=scratch,
        cost_estimate=pl.CostEstimate(flops=flops, bytes_accessed=nbytes, transcendentals=0),
        compiler_params=pltpu.CompilerParams(vmem_limit_bytes=VMEM_LIMIT),
    )(*args)


VM = pl.BlockSpec(memory_space=pltpu.VMEM)
SM = pl.BlockSpec(memory_space=pltpu.SMEM)


def shape(*dims):
    return jax.ShapeDtypeStruct(dims, jnp.float32)


def row_of(value, at):
    return jnp.broadcast_to(value[at : at + 1, :], value.shape)


def pack_pair(one, two):
    left = lax.broadcasted_iota(jnp.int32, one.shape, 1) < 64
    return [
        jnp.where(left, one, pltpu.roll(two, 64, 1)),
        jnp.where(left, pltpu.roll(one, 128 - HALF, 1), pltpu.roll(two, 64 - HALF, 1)),
    ]


def unpack_pair(low, high):
    early = lax.broadcasted_iota(jnp.int32, low.shape, 1) < HALF
    return (
        jnp.where(early, low, pltpu.roll(high, HALF, 1)),
        jnp.where(early, pltpu.roll(low, 64, 1), pltpu.roll(high, 64 + HALF, 1)),
    )


def inverse_factors(one, two):
    count = len(one)
    lanes = lax.broadcasted_iota(jnp.int32, (8, 128), 1)
    subs = lax.broadcasted_iota(jnp.int32, (8, 128), 0)
    base = jnp.where(lanes < 64, 0, 64)
    column = lanes - base
    work = [pack_pair(a, b) for a, b in zip(one, two)]
    results = []

    def place(k):
        side = 8 * k // HALF
        return side, 8 * k - side * HALF

    def spread(v, k):
        side, first = place(k)
        return [
            jnp.take_along_axis(work[v][side], base + (first + c), axis=1) for c in range(8)
        ]

    panel = spread(0, 0)
    for k in range(count):
        side, first = place(k)
        below = [spread(v, k) for v in range(k + 1, count)]
        ahead = spread(k + 1, k + 1) if k + 1 < count else None
        weights = [[None] * 8 for _ in range(8)]
        inverses, lines = [], []
        scales = jnp.ones((8, 128), jnp.float32)
        for c in range(8):
            inv = 1.0 / row_of(panel[c], c)
            inverses.append(inv)
            scales = jnp.where(subs == c, inv, scales)
            for d in range(c + 1, 8):
                weights[c][d] = row_of(panel[d], c)
                panel[d] = panel[d] - (panel[c] * weights[c][d]) * inv
            factor = jnp.where(subs > c, panel[c] * inv, 0.0)
            line = [row_of(part, c) for part in work[k]]
            line[side] = line[side] + jnp.where(column == first + c, 1.0, 0.0)
            lines.append(line)
            work[k] = [part - factor * along for part, along in zip(work[k], line)]
        for v in range(k + 1, count):
            panel = below[v - k - 1]
            for c in range(8):
                factor = panel[c] * inverses[c]
                for d in range(c + 1, 8):
                    panel[d] = panel[d] - factor * weights[c][d]
                if v == k + 1:
                    for d in range(8):
                        ahead[d] = ahead[d] - factor * row_of(panel[c], d)
                work[v] = [part - factor * along for part, along in zip(work[v], lines[c])]
        panel = ahead
        root = lax.sqrt(scales)
        unit = jnp.where(column == subs + first, 1.0, 0.0)
        own = jnp.where(column < subs + first, work[k][side], unit) * root
        other = work[k][0] * root if side else jnp.zeros((8, 128), jnp.float32)
        results.append(unpack_pair(other, own) if side else unpack_pair(own, other))
    return [pair[0] for pair in results], [pair[1] for pair in results]


def edge_weights(width):
    lanes = lax.broadcasted_iota(jnp.int32, (1, width), 1)
    return jnp.where(lanes == 0, 0.0, 0.5), jnp.where(lanes == width - 1, 0.0, 0.5)


def apply_rows(value, coef, from_low, from_high):
    width = value.shape[1]
    return (
        coef * value
        + from_low * pltpu.roll(value, 1, 1)
        + from_high * pltpu.roll(value, width - 1, 1)
    )


def iterate_body(n_alt, chunk, seg_count, modes, width, scale_ref, *refs):
    blocks = refs[:n_alt]
    out_refs = refs[n_alt : n_alt + chunk]
    coef_ref, split_ref, image_ref, gram_ref, inv_ref = refs[n_alt + chunk :]
    place = lax.axis_index("alt")
    flat = place * chunk
    freq = flat // seg_count
    first = flat - freq * seg_count
    total = n_alt * width
    for k, block in enumerate(blocks):
        source = lax.rem(place + n_alt - k, n_alt)
        span = pl.ds(pl.multiple_of(source * width, width), width)
        start = block[0:modes, :] * (1.0 / float(total) ** 0.5)
        for i in range(chunk):
            out_refs[i][:, span] = start
            change = block[pl.ds(modes + 1 + first + i, 1), :]
            coef_ref[i : i + 1, span] = scale_ref[freq] * (
                block[modes : modes + 1, :] * (1.0 + relief * change)
            )
    from_low, from_high = edge_weights(total)
    down = 2.0**-11
    gram_ref[...] = jnp.zeros_like(gram_ref)

    def factorise():
        grams = [[gram_ref[i, at : at + 8, :] for at in range(0, modes, 8)] for i in range(chunk)]
        results = inverse_factors(*grams)
        for i in range(chunk):
            for at in range(0, modes, 8):
                inv_ref[i, at : at + 8, :] = results[i][at // 8] * down**0.5

    def step(_, carry):
        for i in range(chunk):
            coef = coef_ref[i : i + 1, :]
            for at in range(0, modes, 16):
                image = apply_rows(out_refs[i][at : at + 16, :], coef, from_low, from_high)
                for part in range(3):
                    piece = image.astype(jnp.bfloat16)
                    split_ref[i, part, at : at + 16, :] = piece
                    image = image - piece.astype(jnp.float32)
            high, low = split_ref[i, 0], split_ref[i, 1]
            gram = short_mmt(high, high) + short_mmt(high, low) + short_mmt(low, high)
            gram_ref[i, :, 0:modes] = gram * down
        factorise()
        for i in range(chunk):
            inv = inv_ref[i, :, 0:modes].astype(jnp.bfloat16)
            for at in range(0, total, 256):
                out_refs[i][:, at : at + 256] = sum(
                    short_mm(inv, split_ref[i, part, :, at : at + 256]) for part in range(3)
                )
        return carry

    lax.fori_loop(0, ITERS - 1, step, 0)
    for i in range(chunk):
        for at in range(0, modes, 8):
            image_ref[i, at : at + 8, :] = apply_rows(
                out_refs[i][at : at + 8, :], coef_ref[i : i + 1, :], from_low, from_high
            )
        image = image_ref[i]
        gram_ref[i, :, 0:modes] = mmt(image, image) * down
    factorise()
    for i in range(chunk):
        inv = inv_ref[i, :, 0:modes]
        for at in range(0, total, 256):
            out_refs[i][:, at : at + 256] = mm(inv, image_ref[i, :, at : at + 256])


def unit_of(modes):
    rows = lax.broadcasted_iota(jnp.int32, (modes, modes), 0)
    return jnp.where(rows == lax.broadcasted_iota(jnp.int32, (modes, modes), 1), 1.0, 0.0)


def complex_mm(left, right):
    return (
        mm(left[0], right[0]) - mm(left[1], right[1]),
        mm(left[0], right[1]) + mm(left[1], right[0]),
    )


def advance_body(modes, total, coef_ref, first_ref, second_ref, inner_ref, rest_ref, image_ref):
    from_low, from_high = edge_weights(total)
    unit = unit_of(modes)
    turns = []
    for i, ref in enumerate((first_ref, second_ref)):
        for at in range(0, modes, 8):
            image_ref[at : at + 8, :] = apply_rows(
                ref[at : at + 8, :], coef_ref[i : i + 1, :], from_low, from_high
            )
        phase = phase_step * mmt(ref[...], image_ref[...])
        square = mm(phase, phase)
        turns.append(
            (unit - 0.5 * square + mm(square, square) / 24.0, phase - mm(phase, square) / 6.0)
        )
    corr = mmt(second_ref[...], first_ref[...])
    inner = (mm(corr, turns[0][0]), mm(corr, turns[0][1]))
    rest = complex_mm(turns[1], inner)
    for part in range(2):
        inner_ref[part] = inner[part]
        rest_ref[part] = rest[part]


def product_body(next_ref, second_ref, rest_ref, out_ref):
    corr = mmt(next_ref[...], second_ref[...])
    for part in range(2):
        out_ref[part] = mm(corr, rest_ref[part])


def chain_place(halves):
    return lax.axis_index("range") * halves + lax.rem(lax.axis_index("alt"), halves)


def padded(ref, missing):
    return (ref[0] + jnp.where(missing, unit_of(ref.shape[1]), 0.0), ref[1])


def join_body(halves, back_new, back_old, new_ref, old_ref, out_ref):
    at = chain_place(halves)
    new = padded(new_ref, at < back_new) if back_new else (new_ref[0], new_ref[1])
    real, imag = complex_mm(new, padded(old_ref, at < back_old))
    out_ref[0] = real
    out_ref[1] = imag


def turn_vector(matrix, vector):
    rows = lax.broadcasted_iota(jnp.int32, vector.shape, 0)
    swapped = jnp.where(
        rows == 0, -row_of(vector, 1), jnp.where(rows == 1, row_of(vector, 0), 0.0)
    )
    return mmt(vector, matrix[0]) + mmt(swapped, matrix[1])


def source_rows(source_ref, halves):
    return source_ref[lax.axis_index("alt") // halves]


def early_body(halves, span_ref, source_ref, out_ref):
    out_ref[...] = turn_vector((span_ref[0], span_ref[1]), source_rows(source_ref, halves))


def field_body(halves, back, n_alt, width, scale, *refs):
    span_ref, early_ref, came_ref, inner_ref, first_ref, second_ref, out_ref = refs
    at = chain_place(halves)
    came = turn_vector((span_ref[0], span_ref[1]), came_ref[...])
    amp = jnp.where(at < back, early_ref[...], came)
    amps = (amp, turn_vector((inner_ref[0], inner_ref[1]), amp))
    for i, ref in enumerate((first_ref, second_ref)):
        for k in range(n_alt):
            part = mm(amps[i], ref[:, k * width : (k + 1) * width])
            out_ref[k, i] = scale * part[0:2, :]


def local(freq_scale, base_profile, perturb, start_block, source):
    freqs = freq_scale.shape[0]
    seg_count = perturb.shape[0]
    modes, width = start_block.shape
    n_alt = lax.axis_size("alt")
    n_range = lax.axis_size("range")
    total = width * n_alt
    chunk = freqs * seg_count // n_alt
    halves = seg_count // chunk
    length = n_range * halves
    assert modes == 2 * HALF and chunk == 2 and halves * chunk == seg_count and halves * freqs == n_alt

    def along_chain(value, steps):
        pairs = []
        for freq in range(freqs):
            for at in range(max(0, -steps), min(length, length - steps)):
                ends = []
                for d in (at, at + steps):
                    ends.append(d // halves * n_alt + freq * halves + d % halves)
                pairs.append(tuple(ends))
        return lax.ppermute(value, ("range", "alt"), pairs)

    lines = [start_block, base_profile[None, :], perturb]
    filler = -(modes + 1 + seg_count) % 8
    mine = jnp.concatenate(lines + [jnp.zeros((filler, width), jnp.float32)], axis=0)
    blocks = [mine]
    for k in range(1, n_alt):
        blocks.append(lax.ppermute(mine, "alt", [(i, (i + k) % n_alt) for i in range(n_alt)]))
    flops = 2 * modes * modes * total
    first, second, coef = kernel_call(
        functools.partial(iterate_body, n_alt, chunk, seg_count, modes, width),
        [shape(modes, total)] * chunk + [shape(chunk, total)],
        [freq_scale] + blocks,
        [SM] + [VM] * n_alt,
        [pltpu.VMEM((chunk, 3, modes, total), jnp.bfloat16)]
        + [pltpu.VMEM((chunk, modes, total), jnp.float32)]
        + [pltpu.VMEM((chunk, modes, 128), jnp.float32)] * 2,
        flops=2 * ITERS * chunk * flops,
    )
    following = along_chain(first, -1)
    inner, rest = kernel_call(
        functools.partial(advance_body, modes, total),
        [shape(2, modes, modes)] * 2,
        [coef, first, second],
        [VM] * 3,
        [pltpu.VMEM((modes, total), jnp.float32)],
        flops=8 * flops,
    )
    product = kernel_call(
        product_body, shape(2, modes, modes), [following, second, rest], [VM] * 3, flops=flops
    )
    reach = 2
    span = kernel_call(
        functools.partial(join_body, halves, 1, 2),
        shape(2, modes, modes),
        [along_chain(product, 1), along_chain(product, 2)],
        [VM] * 2,
        flops=flops,
    )
    while 2 * reach < length:
        span = kernel_call(
            functools.partial(join_body, halves, 0, reach),
            shape(2, modes, modes),
            [span, along_chain(span, reach)],
            [VM] * 2,
            flops=flops,
        )
        reach *= 2
    rows = jnp.concatenate([source, jnp.zeros((freqs, 6, modes), jnp.float32)], axis=1)
    early = kernel_call(
        functools.partial(early_body, halves), shape(8, modes), [span, rows], [VM] * 2
    )
    parts = kernel_call(
        functools.partial(
            field_body, halves, reach, n_alt, width, (float(total) / float(modes)) ** 0.5
        ),
        shape(n_alt, chunk, 2, width),
        [span, early, along_chain(early, reach), inner, first, second],
        [VM] * 6,
    )
    field = lax.all_to_all(parts, "alt", 0, 0)
    return field.reshape(freqs, seg_count, 2, width)


def solution(mesh):
    in_specs = (P("freq"), P("alt"), P("range", "alt"), P(None, "alt"), P("freq", None, None))
    out_specs = P("freq", "range", None, "alt")
    return jax.shard_map(local, mesh=mesh, in_specs=in_specs, out_specs=out_specs, check_vma=False)
```

```python
import functools

import jax
import jax.numpy as jnp
from jax import lax
from jax.experimental import pallas as pl
from jax.experimental.pallas import tpu as pltpu
from jax.sharding import PartitionSpec as P

ITERS = 8

phase_step = 0.15
relief = 0.1
HIGHEST = lax.Precision.HIGHEST
VMEM_LIMIT = 48 * 2**20
HALF = 48


def mm(left, right):
    return lax.dot_general(
        left, right, (((1,), (0,)), ((), ())), precision=HIGHEST, preferred_element_type=jnp.float32
    )


def mmt(left, right):
    return lax.dot_general(
        left, right, (((1,), (1,)), ((), ())), precision=HIGHEST, preferred_element_type=jnp.float32
    )


def short_mm(left, right):
    return lax.dot_general(
        left, right, (((1,), (0,)), ((), ())), preferred_element_type=jnp.float32
    )


def short_mmt(left, right):
    return lax.dot_general(
        left, right, (((1,), (1,)), ((), ())), preferred_element_type=jnp.float32
    )


def kernel_call(body, out_shape, args, specs, scratch=(), flops=0):
    nbytes = sum(4 * a.size for a in args) + sum(4 * o.size for o in jax.tree.leaves(out_shape))
    return pl.pallas_call(
        body,
        out_shape=out_shape,
        in_specs=specs,
        out_specs=jax.tree.map(lambda _: pl.BlockSpec(memory_space=pltpu.VMEM), out_shape),
        scratch_shapes=scratch,
        cost_estimate=pl.CostEstimate(flops=flops, bytes_accessed=nbytes, transcendentals=0),
        compiler_params=pltpu.CompilerParams(vmem_limit_bytes=VMEM_LIMIT),
    )(*args)


VM = pl.BlockSpec(memory_space=pltpu.VMEM)
SM = pl.BlockSpec(memory_space=pltpu.SMEM)


def shape(*dims):
    return jax.ShapeDtypeStruct(dims, jnp.float32)


def row_of(value, at):
    return jnp.broadcast_to(value[at : at + 1, :], value.shape)


def pack_pair(one, two):
    left = lax.broadcasted_iota(jnp.int32, one.shape, 1) < 64
    return [
        jnp.where(left, one, pltpu.roll(two, 64, 1)),
        jnp.where(left, pltpu.roll(one, 128 - HALF, 1), pltpu.roll(two, 64 - HALF, 1)),
    ]


def unpack_pair(low, high):
    early = lax.broadcasted_iota(jnp.int32, low.shape, 1) < HALF
    return (
        jnp.where(early, low, pltpu.roll(high, HALF, 1)),
        jnp.where(early, pltpu.roll(low, 64, 1), pltpu.roll(high, 64 + HALF, 1)),
    )


def inverse_factors(one, two):
    count = len(one)
    lanes = lax.broadcasted_iota(jnp.int32, (8, 128), 1)
    subs = lax.broadcasted_iota(jnp.int32, (8, 128), 0)
    base = jnp.where(lanes < 64, 0, 64)
    column = lanes - base
    work = [pack_pair(a, b) for a, b in zip(one, two)]
    results = []

    def place(k):
        side = 8 * k // HALF
        return side, 8 * k - side * HALF

    def spread(v, k):
        side, first = place(k)
        return [
            jnp.take_along_axis(work[v][side], base + (first + c), axis=1) for c in range(8)
        ]

    panel = spread(0, 0)
    for k in range(count):
        side, first = place(k)
        near = spread(k + 1, k) if k + 1 < count else None
        ahead = spread(k + 1, k + 1) if k + 1 < count else None
        weights = [[None] * 8 for _ in range(8)]
        inverses, lines = [], []
        scales = jnp.ones((8, 128), jnp.float32)
        for c in range(0, 8, 2):
            corner, cross, late = (
                row_of(panel[c], c),
                row_of(panel[c + 1], c),
                row_of(panel[c + 1], c + 1),
            )
            inv = 1.0 / corner
            second = corner * (1.0 / (corner * late - cross * cross))
            ratio = cross * inv
            weights[c][c + 1] = cross
            factor = panel[c] * inv
            rest = panel[c + 1] - factor * cross
            for d in range(c + 2, 8):
                weights[c][d] = row_of(panel[d], c)
                weights[c + 1][d] = row_of(panel[d], c + 1) - ratio * weights[c][d]
                panel[d] = (panel[d] - factor * weights[c][d]) - (
                    rest * weights[c + 1][d]
                ) * second
            pair = (jnp.where(subs > c, factor, 0.0), jnp.where(subs > c + 1, rest * second, 0.0))
            for e in range(2):
                inverses.append((inv, second)[e])
                scales = jnp.where(subs == c + e, inverses[-1], scales)
                line = [row_of(part, c + e) for part in work[k]]
                line[side] = line[side] + jnp.where(column == first + c + e, 1.0, 0.0)
                lines.append(line)
                work[k] = [part - pair[e] * along for part, along in zip(work[k], line)]
        if near is not None:
            for c in range(8):
                factor = near[c] * inverses[c]
                for d in range(c + 1, 8):
                    near[d] = near[d] - factor * weights[c][d]
                for d in range(8):
                    ahead[d] = ahead[d] - factor * row_of(near[c], d)
                work[k + 1] = [
                    part - factor * along for part, along in zip(work[k + 1], lines[c])
                ]
        panel = ahead
        scaled = [[part * inv for part in line] for line, inv in zip(lines, inverses)]
        for v in range(k + 2, count):
            there, at = place(v)
            for c in range(8):
                factor = jnp.take_along_axis(scaled[c][there], base + subs + at, axis=1)
                work[v] = [part - factor * along for part, along in zip(work[v], lines[c])]
        root = lax.sqrt(scales)
        unit = jnp.where(column == subs + first, 1.0, 0.0)
        own = jnp.where(column < subs + first, work[k][side], unit) * root
        other = work[k][0] * root if side else jnp.zeros((8, 128), jnp.float32)
        results.append(unpack_pair(other, own) if side else unpack_pair(own, other))
    return [pair[0] for pair in results], [pair[1] for pair in results]


def edge_weights(width):
    lanes = lax.broadcasted_iota(jnp.int32, (1, width), 1)
    return jnp.where(lanes == 0, 0.0, 0.5), jnp.where(lanes == width - 1, 0.0, 0.5)


def apply_rows(value, coef, from_low, from_high):
    width = value.shape[1]
    return (
        coef * value
        + from_low * pltpu.roll(value, 1, 1)
        + from_high * pltpu.roll(value, width - 1, 1)
    )


def iterate_body(n_alt, chunk, seg_count, modes, width, scale_ref, *refs):
    starts, profiles = refs[:n_alt], refs[n_alt : 2 * n_alt]
    out_refs = refs[2 * n_alt : 2 * n_alt + chunk]
    coef_ref, split_ref, image_ref, gram_ref, inv_ref = refs[2 * n_alt + chunk :]
    place = lax.axis_index("alt")
    flat = place * chunk
    freq = flat // seg_count
    first = flat - freq * seg_count
    total = n_alt * width
    for k in range(n_alt):
        source = lax.rem(place + n_alt - k, n_alt)
        span = pl.ds(pl.multiple_of(source * width, width), width)
        start = starts[k][...] * (1.0 / float(total) ** 0.5)
        for i in range(chunk):
            out_refs[i][:, span] = start
            change = profiles[k][pl.ds(1 + first + i, 1), :]
            coef_ref[i : i + 1, span] = scale_ref[freq] * (
                profiles[k][0:1, :] * (1.0 + relief * change)
            )
    from_low, from_high = edge_weights(total)
    down = 2.0**-11
    gram_ref[...] = jnp.zeros_like(gram_ref)

    def factorise():
        grams = [[gram_ref[i, at : at + 8, :] for at in range(0, modes, 8)] for i in range(chunk)]
        results = inverse_factors(*grams)
        for i in range(chunk):
            for at in range(0, modes, 8):
                inv_ref[i, at : at + 8, :] = results[i][at // 8] * down**0.5

    def step(_, carry):
        for i in range(chunk):
            coef = coef_ref[i : i + 1, :]
            for at in range(0, modes, 16):
                image = apply_rows(out_refs[i][at : at + 16, :], coef, from_low, from_high)
                for part in range(3):
                    piece = image.astype(jnp.bfloat16)
                    split_ref[i, part, at : at + 16, :] = piece
                    image = image - piece.astype(jnp.float32)
            high, low = split_ref[i, 0], split_ref[i, 1]
            gram = short_mmt(high, high) + short_mmt(high, low) + short_mmt(low, high)
            gram_ref[i, :, 0:modes] = gram * down
        factorise()
        for i in range(chunk):
            inv = inv_ref[i, :, 0:modes].astype(jnp.bfloat16)
            for at in range(0, total, 256):
                out_refs[i][:, at : at + 256] = sum(
                    short_mm(inv, split_ref[i, part, :, at : at + 256]) for part in range(3)
                )
        return carry

    lax.fori_loop(0, ITERS - 1, step, 0)
    for i in range(chunk):
        for at in range(0, modes, 8):
            image_ref[i, at : at + 8, :] = apply_rows(
                out_refs[i][at : at + 8, :], coef_ref[i : i + 1, :], from_low, from_high
            )
        image = image_ref[i]
        gram_ref[i, :, 0:modes] = mmt(image, image) * down
    factorise()
    for i in range(chunk):
        inv = inv_ref[i, :, 0:modes]
        for at in range(0, total, 256):
            out_refs[i][:, at : at + 256] = mm(inv, image_ref[i, :, at : at + 256])


def unit_of(modes):
    rows = lax.broadcasted_iota(jnp.int32, (modes, modes), 0)
    return jnp.where(rows == lax.broadcasted_iota(jnp.int32, (modes, modes), 1), 1.0, 0.0)


def complex_mm(left, right):
    return (
        mm(left[0], right[0]) - mm(left[1], right[1]),
        mm(left[0], right[1]) + mm(left[1], right[0]),
    )


def advance_body(modes, total, coef_ref, first_ref, second_ref, inner_ref, rest_ref, image_ref):
    from_low, from_high = edge_weights(total)
    unit = unit_of(modes)
    turns = []
    for i, ref in enumerate((first_ref, second_ref)):
        for at in range(0, modes, 8):
            image_ref[at : at + 8, :] = apply_rows(
                ref[at : at + 8, :], coef_ref[i : i + 1, :], from_low, from_high
            )
        phase = phase_step * mmt(ref[...], image_ref[...])
        square = mm(phase, phase)
        turns.append(
            (unit - 0.5 * square + mm(square, square) / 24.0, phase - mm(phase, square) / 6.0)
        )
    corr = mmt(second_ref[...], first_ref[...])
    inner = (mm(corr, turns[0][0]), mm(corr, turns[0][1]))
    rest = complex_mm(turns[1], inner)
    for part in range(2):
        inner_ref[part] = inner[part]
        rest_ref[part] = rest[part]


def chain_place(halves):
    return lax.axis_index("range") * halves + lax.rem(lax.axis_index("alt"), halves)


def with_start(halves, back, ref):
    missing = chain_place(halves) < back
    return (ref[0] + jnp.where(missing, unit_of(ref.shape[1]), 0.0), ref[1])


def product_body(halves, first_ref, before_ref, rest_ref, out_ref):
    corr = mmt(first_ref[...], before_ref[...])
    missing = chain_place(halves) < 1
    out_ref[0] = mm(corr, rest_ref[0]) + jnp.where(missing, unit_of(out_ref.shape[1]), 0.0)
    out_ref[1] = mm(corr, rest_ref[1])


def join_body(halves, back, new_ref, old_ref, *refs):
    out_ref = refs[1] if len(refs) > 1 else refs[0]
    joined = complex_mm((new_ref[0], new_ref[1]), with_start(halves, back, old_ref))
    out_ref[0], out_ref[1] = joined
    if len(refs) > 1:
        source = refs[0][lax.axis_index("alt") // halves]
        refs[2][...] = turn_vector(joined, source)


def turn_vector(matrix, vector):
    rows = lax.broadcasted_iota(jnp.int32, vector.shape, 0)
    swapped = jnp.where(
        rows == 0, -row_of(vector, 1), jnp.where(rows == 1, row_of(vector, 0), 0.0)
    )
    return mmt(vector, matrix[0]) + mmt(swapped, matrix[1])


def field_body(halves, back, n_alt, width, scale, *refs):
    span_ref, early_ref, came_ref, inner_ref, first_ref, second_ref = refs[:6]
    place = lax.axis_index("alt")
    came = turn_vector((span_ref[0], span_ref[1]), came_ref[...])
    amp = jnp.where(chain_place(halves) < back, early_ref[...], came)
    amps = (amp, turn_vector((inner_ref[0], inner_ref[1]), amp))
    for k, out_ref in enumerate(refs[6:]):
        target = lax.rem(place + k, n_alt)
        span = pl.ds(pl.multiple_of(target * width, width), width)
        for i, ref in enumerate((first_ref, second_ref)):
            out_ref[i] = scale * mm(amps[i], ref[:, span])[0:2, :]


def settle_body(halves, n_alt, *refs):
    place = lax.axis_index("alt")
    out_ref = refs[n_alt]
    for k, part_ref in enumerate(refs[:n_alt]):
        source = lax.rem(place + n_alt - k, n_alt)
        chunk = part_ref.shape[0]
        freq, half = source // halves, lax.rem(source, halves)
        for i in range(chunk):
            out_ref[freq, half * chunk + i] = part_ref[i]


def local(freq_scale, base_profile, perturb, start_block, source):
    freqs = freq_scale.shape[0]
    seg_count = perturb.shape[0]
    modes, width = start_block.shape
    n_alt = lax.axis_size("alt")
    n_range = lax.axis_size("range")
    total = width * n_alt
    chunk = freqs * seg_count // n_alt
    halves = seg_count // chunk
    length = n_range * halves
    assert modes == 2 * HALF and chunk == 2 and halves * chunk == seg_count and halves * freqs == n_alt

    def along_chain(value, steps):
        pairs = []
        for freq in range(freqs):
            for at in range(max(0, -steps), min(length, length - steps)):
                ends = []
                for d in (at, at + steps):
                    ends.append(d // halves * n_alt + freq * halves + d % halves)
                pairs.append(tuple(ends))
        return lax.ppermute(value, ("range", "alt"), pairs)

    def around(value, k):
        return lax.ppermute(value, "alt", [(i, (i + k) % n_alt) for i in range(n_alt)])

    filler = jnp.zeros((-(1 + seg_count) % 8, width), jnp.float32)
    profile = jnp.concatenate([base_profile[None, :], perturb, filler], axis=0)
    starts = [start_block] + [around(start_block, k) for k in range(1, n_alt)]
    profiles = [profile] + [around(profile, k) for k in range(1, n_alt)]
    flops = 2 * modes * modes * total
    first, second, coef = kernel_call(
        functools.partial(iterate_body, n_alt, chunk, seg_count, modes, width),
        [shape(modes, total)] * chunk + [shape(chunk, total)],
        [freq_scale] + starts + profiles,
        [SM] + [VM] * (2 * n_alt),
        [pltpu.VMEM((chunk, 3, modes, total), jnp.bfloat16)]
        + [pltpu.VMEM((chunk, modes, total), jnp.float32)]
        + [pltpu.VMEM((chunk, modes, 128), jnp.float32)] * 2,
        flops=2 * ITERS * chunk * flops,
    )
    before = along_chain(second, 1)
    inner, rest = kernel_call(
        functools.partial(advance_body, modes, total),
        [shape(2, modes, modes)] * 2,
        [coef, first, second],
        [VM] * 3,
        [pltpu.VMEM((modes, total), jnp.float32)],
        flops=8 * flops,
    )
    span = kernel_call(
        functools.partial(product_body, halves),
        shape(2, modes, modes),
        [first, before, along_chain(rest, 1)],
        [VM] * 3,
        flops=flops,
    )
    rows = jnp.concatenate([source, jnp.zeros((freqs, 6, modes), jnp.float32)], axis=1)
    reach = 1
    while 2 * reach < length:
        last = 4 * reach >= length
        out = [shape(2, modes, modes)] + [shape(8, modes)] * last
        results = kernel_call(
            functools.partial(join_body, halves, reach),
            out,
            [span, along_chain(span, reach)] + [rows] * last,
            [VM] * (2 + last),
            flops=flops,
        )
        span = results[0]
        reach *= 2
    early = results[1]
    parts = kernel_call(
        functools.partial(
            field_body, halves, reach, n_alt, width, (float(total) / float(modes)) ** 0.5
        ),
        [shape(chunk, 2, width)] * n_alt,
        [span, early, along_chain(early, reach), inner, first, second],
        [VM] * 6,
    )
    parts = [parts[0]] + [around(parts[k], k) for k in range(1, n_alt)]
    return kernel_call(
        functools.partial(settle_body, halves, n_alt),
        shape(freqs, seg_count, 2, width),
        parts,
        [VM] * n_alt,
    )


def solution(mesh):
    in_specs = (P("freq"), P("alt"), P("range", "alt"), P(None, "alt"), P("freq", None, None))
    out_specs = P("freq", "range", None, "alt")
    return jax.shard_map(local, mesh=mesh, in_specs=in_specs, out_specs=out_specs, check_vma=False)
```

```python
import functools

import jax
import jax.numpy as jnp
from jax import lax
from jax.experimental import pallas as pl
from jax.experimental.pallas import tpu as pltpu
from jax.sharding import PartitionSpec as P

ITERS = 8

phase_step = 0.15
relief = 0.1
HIGHEST = lax.Precision.HIGHEST
VMEM_LIMIT = 48 * 2**20
HALF = 48


def mm(left, right):
    return lax.dot_general(
        left, right, (((1,), (0,)), ((), ())), precision=HIGHEST, preferred_element_type=jnp.float32
    )


def mmt(left, right):
    return lax.dot_general(
        left, right, (((1,), (1,)), ((), ())), precision=HIGHEST, preferred_element_type=jnp.float32
    )


def short_mm(left, right):
    return lax.dot_general(
        left, right, (((1,), (0,)), ((), ())), preferred_element_type=jnp.float32
    )


def short_mmt(left, right):
    return lax.dot_general(
        left, right, (((1,), (1,)), ((), ())), preferred_element_type=jnp.float32
    )


def kernel_call(body, out_shape, args, specs, scratch=(), flops=0):
    nbytes = sum(4 * a.size for a in args) + sum(4 * o.size for o in jax.tree.leaves(out_shape))
    return pl.pallas_call(
        body,
        out_shape=out_shape,
        in_specs=specs,
        out_specs=jax.tree.map(lambda _: pl.BlockSpec(memory_space=pltpu.VMEM), out_shape),
        scratch_shapes=scratch,
        cost_estimate=pl.CostEstimate(flops=flops, bytes_accessed=nbytes, transcendentals=0),
        compiler_params=pltpu.CompilerParams(vmem_limit_bytes=VMEM_LIMIT),
    )(*args)


VM = pl.BlockSpec(memory_space=pltpu.VMEM)
SM = pl.BlockSpec(memory_space=pltpu.SMEM)


def shape(*dims):
    return jax.ShapeDtypeStruct(dims, jnp.float32)


def row_of(value, at):
    return jnp.broadcast_to(value[at : at + 1, :], value.shape)


def pack_pair(one, two):
    left = lax.broadcasted_iota(jnp.int32, one.shape, 1) < 64
    return [
        jnp.where(left, one, pltpu.roll(two, 64, 1)),
        jnp.where(left, pltpu.roll(one, 128 - HALF, 1), pltpu.roll(two, 64 - HALF, 1)),
    ]


def unpack_pair(low, high):
    early = lax.broadcasted_iota(jnp.int32, low.shape, 1) < HALF
    return (
        jnp.where(early, low, pltpu.roll(high, HALF, 1)),
        jnp.where(early, pltpu.roll(low, 64, 1), pltpu.roll(high, 64 + HALF, 1)),
    )


def inverse_factors(one, two):
    count = len(one)
    lanes = lax.broadcasted_iota(jnp.int32, (8, 128), 1)
    subs = lax.broadcasted_iota(jnp.int32, (8, 128), 0)
    base = jnp.where(lanes < 64, 0, 64)
    column = lanes - base
    work = [pack_pair(a, b) for a, b in zip(one, two)]
    results = []

    def place(k):
        side = 8 * k // HALF
        return side, 8 * k - side * HALF

    def spread(v, k):
        side, first = place(k)
        return [
            jnp.take_along_axis(work[v][side], base + (first + c), axis=1) for c in range(8)
        ]

    panel = spread(0, 0)
    for k in range(count):
        side, first = place(k)
        near = spread(k + 1, k) if k + 1 < count else None
        ahead = spread(k + 1, k + 1) if k + 1 < count else None
        weights = [[None] * 8 for _ in range(8)]
        inverses, lines = [], []
        scales = jnp.ones((8, 128), jnp.float32)
        for c in range(0, 8, 2):
            corner, cross, late = (
                row_of(panel[c], c),
                row_of(panel[c + 1], c),
                row_of(panel[c + 1], c + 1),
            )
            inv = 1.0 / corner
            second = corner * (1.0 / (corner * late - cross * cross))
            ratio = cross * inv
            weights[c][c + 1] = cross
            factor = panel[c] * inv
            rest = panel[c + 1] - factor * cross
            for d in range(c + 2, 8):
                weights[c][d] = row_of(panel[d], c)
                weights[c + 1][d] = row_of(panel[d], c + 1) - ratio * weights[c][d]
                panel[d] = (panel[d] - factor * weights[c][d]) - (
                    rest * weights[c + 1][d]
                ) * second
            pair = (jnp.where(subs > c, factor, 0.0), jnp.where(subs > c + 1, rest * second, 0.0))
            for e in range(2):
                inverses.append((inv, second)[e])
                scales = jnp.where(subs == c + e, inverses[-1], scales)
                line = [row_of(part, c + e) for part in work[k]]
                line[side] = line[side] + jnp.where(column == first + c + e, 1.0, 0.0)
                lines.append(line)
                work[k] = [part - pair[e] * along for part, along in zip(work[k], line)]
        if near is not None:
            for c in range(8):
                factor = near[c] * inverses[c]
                for d in range(c + 1, 8):
                    near[d] = near[d] - factor * weights[c][d]
                for d in range(8):
                    ahead[d] = ahead[d] - factor * row_of(near[c], d)
                work[k + 1] = [
                    part - factor * along for part, along in zip(work[k + 1], lines[c])
                ]
        panel = ahead
        scaled = [[part * inv for part in line] for line, inv in zip(lines, inverses)]
        for v in range(k + 2, count):
            there, at = place(v)
            for c in range(8):
                factor = jnp.take_along_axis(scaled[c][there], base + subs + at, axis=1)
                work[v] = [part - factor * along for part, along in zip(work[v], lines[c])]
        root = lax.sqrt(scales)
        unit = jnp.where(column == subs + first, 1.0, 0.0)
        own = jnp.where(column < subs + first, work[k][side], unit) * root
        other = work[k][0] * root if side else jnp.zeros((8, 128), jnp.float32)
        results.append(unpack_pair(other, own) if side else unpack_pair(own, other))
    return [pair[0] for pair in results], [pair[1] for pair in results]


def edge_weights(width):
    lanes = lax.broadcasted_iota(jnp.int32, (1, width), 1)
    return jnp.where(lanes == 0, 0.0, 0.5), jnp.where(lanes == width - 1, 0.0, 0.5)


def apply_rows(value, coef, from_low, from_high):
    width = value.shape[1]
    return (
        coef * value
        + from_low * pltpu.roll(value, 1, 1)
        + from_high * pltpu.roll(value, width - 1, 1)
    )


def iterate_body(n_alt, chunk, seg_count, modes, width, scale_ref, *refs):
    blocks, out_refs = refs[:n_alt], refs[n_alt : n_alt + chunk]
    coef_ref, split_ref, image_ref, gram_ref, inv_ref = refs[n_alt + chunk :]
    place = lax.axis_index("alt")
    flat = place * chunk
    freq = flat // seg_count
    first = flat - freq * seg_count
    total = n_alt * width
    for k, block in enumerate(blocks):
        source = lax.rem(place + n_alt - k, n_alt)
        span = pl.ds(pl.multiple_of(source * width, width), width)
        start = block[0:modes, :] * (1.0 / float(total) ** 0.5)
        for i in range(chunk):
            out_refs[i][:, span] = start
            change = block[pl.ds(modes + 1 + first + i, 1), :]
            coef_ref[i : i + 1, span] = scale_ref[freq] * (
                block[modes : modes + 1, :] * (1.0 + relief * change)
            )
    from_low, from_high = edge_weights(total)
    down = 2.0**-11
    gram_ref[...] = jnp.zeros_like(gram_ref)

    def factorise():
        grams = [[gram_ref[i, at : at + 8, :] for at in range(0, modes, 8)] for i in range(chunk)]
        results = inverse_factors(*grams)
        for i in range(chunk):
            for at in range(0, modes, 8):
                inv_ref[i, at : at + 8, :] = results[i][at // 8] * down**0.5

    def step(_, carry):
        for i in range(chunk):
            coef = coef_ref[i : i + 1, :]
            for at in range(0, modes, 16):
                image = apply_rows(out_refs[i][at : at + 16, :], coef, from_low, from_high)
                for part in range(3):
                    piece = image.astype(jnp.bfloat16)
                    split_ref[i, part, at : at + 16, :] = piece
                    image = image - piece.astype(jnp.float32)
            high, low = split_ref[i, 0], split_ref[i, 1]
            gram = short_mmt(high, high) + short_mmt(high, low) + short_mmt(low, high)
            gram_ref[i, :, 0:modes] = gram * down
        factorise()
        for i in range(chunk):
            inv = inv_ref[i, :, 0:modes].astype(jnp.bfloat16)
            for at in range(0, total, 256):
                out_refs[i][:, at : at + 256] = sum(
                    short_mm(inv, split_ref[i, part, :, at : at + 256]) for part in range(3)
                )
        return carry

    lax.fori_loop(0, ITERS - 1, step, 0)
    for i in range(chunk):
        for at in range(0, modes, 8):
            image_ref[i, at : at + 8, :] = apply_rows(
                out_refs[i][at : at + 8, :], coef_ref[i : i + 1, :], from_low, from_high
            )
        image = image_ref[i]
        gram_ref[i, :, 0:modes] = mmt(image, image) * down
    factorise()
    for i in range(chunk):
        inv = inv_ref[i, :, 0:modes]
        for at in range(0, total, 256):
            out_refs[i][:, at : at + 256] = mm(inv, image_ref[i, :, at : at + 256])


def unit_of(modes):
    rows = lax.broadcasted_iota(jnp.int32, (modes, modes), 0)
    return jnp.where(rows == lax.broadcasted_iota(jnp.int32, (modes, modes), 1), 1.0, 0.0)


def complex_mm(left, right):
    return (
        mm(left[0], right[0]) - mm(left[1], right[1]),
        mm(left[0], right[1]) + mm(left[1], right[0]),
    )


def advance_body(modes, total, coef_ref, first_ref, second_ref, inner_ref, rest_ref, image_ref):
    from_low, from_high = edge_weights(total)
    unit = unit_of(modes)
    turns = []
    for i, ref in enumerate((first_ref, second_ref)):
        for at in range(0, modes, 8):
            image_ref[at : at + 8, :] = apply_rows(
                ref[at : at + 8, :], coef_ref[i : i + 1, :], from_low, from_high
            )
        phase = phase_step * mmt(ref[...], image_ref[...])
        square = mm(phase, phase)
        turns.append(
            (unit - 0.5 * square + mm(square, square) / 24.0, phase - mm(phase, square) / 6.0)
        )
    corr = mmt(second_ref[...], first_ref[...])
    inner = (mm(corr, turns[0][0]), mm(corr, turns[0][1]))
    rest = complex_mm(turns[1], inner)
    for part in range(2):
        inner_ref[part] = inner[part]
        rest_ref[part] = rest[part]


def chain_place(halves):
    return lax.axis_index("range") * halves + lax.rem(lax.axis_index("alt"), halves)


def product_body(next_ref, second_ref, rest_ref, out_ref):
    corr = mmt(next_ref[...], second_ref[...])
    for part in range(2):
        out_ref[part] = mm(corr, rest_ref[part])


def join_body(halves, backs, *refs):
    at = chain_place(halves)
    spans = []
    for back, ref in zip(backs, refs):
        missing = jnp.where(at < back, unit_of(ref.shape[1]), 0.0)
        spans.append((ref[0] + missing, ref[1]) if back else (ref[0], ref[1]))
    while len(spans) > 1:
        pairs = [complex_mm(*spans[i : i + 2]) for i in range(0, len(spans) - 1, 2)]
        spans = pairs + spans[len(pairs) * 2 :]
    refs[-1][0], refs[-1][1] = spans[0]


def turn_vector(matrix, vector):
    rows = lax.broadcasted_iota(jnp.int32, vector.shape, 0)
    swapped = jnp.where(
        rows == 0, -row_of(vector, 1), jnp.where(rows == 1, row_of(vector, 0), 0.0)
    )
    return mmt(vector, matrix[0]) + mmt(swapped, matrix[1])


def field_body(halves, backs, n_alt, width, scale, source_ref, *refs):
    count = len(backs)
    inner_ref, first_ref, second_ref = refs[count : count + 3]
    place = lax.axis_index("alt")
    amp = source_ref[place // halves]
    for back, ref in reversed(list(zip(backs, refs))):
        moved = turn_vector((ref[0], ref[1]), amp)
        amp = jnp.where(chain_place(halves) < back, amp, moved)
    amps = (amp, turn_vector((inner_ref[0], inner_ref[1]), amp))
    for k, out_ref in enumerate(refs[count + 3 :]):
        target = lax.rem(place + k, n_alt)
        span = pl.ds(pl.multiple_of(target * width, width), width)
        for i, ref in enumerate((first_ref, second_ref)):
            out_ref[i] = scale * mm(amps[i], ref[:, span])[0:2, :]


def settle_body(halves, n_alt, *refs):
    place = lax.axis_index("alt")
    out_ref = refs[n_alt]
    for k, part_ref in enumerate(refs[:n_alt]):
        source = lax.rem(place + n_alt - k, n_alt)
        chunk = part_ref.shape[0]
        freq, half = source // halves, lax.rem(source, halves)
        for i in range(chunk):
            out_ref[freq, half * chunk + i] = part_ref[i]


def local(freq_scale, base_profile, perturb, start_block, source):
    freqs = freq_scale.shape[0]
    seg_count = perturb.shape[0]
    modes, width = start_block.shape
    n_alt = lax.axis_size("alt")
    n_range = lax.axis_size("range")
    total = width * n_alt
    chunk = freqs * seg_count // n_alt
    halves = seg_count // chunk
    length = n_range * halves
    assert modes == 2 * HALF and chunk == 2 and halves * chunk == seg_count and halves * freqs == n_alt

    def along_chain(value, steps):
        pairs = []
        for freq in range(freqs):
            for at in range(max(0, -steps), min(length, length - steps)):
                ends = []
                for d in (at, at + steps):
                    ends.append(d // halves * n_alt + freq * halves + d % halves)
                pairs.append(tuple(ends))
        return lax.ppermute(value, ("range", "alt"), pairs)

    def around(value, k):
        return lax.ppermute(value, "alt", [(i, (i + k) % n_alt) for i in range(n_alt)])

    lines = [start_block, base_profile[None, :], perturb]
    filler = jnp.zeros((-(modes + 1 + seg_count) % 8, width), jnp.float32)
    mine = jnp.concatenate(lines + [filler], axis=0)
    blocks = [mine] + [around(mine, k) for k in range(1, n_alt)]
    flops = 2 * modes * modes * total
    first, second, coef = kernel_call(
        functools.partial(iterate_body, n_alt, chunk, seg_count, modes, width),
        [shape(modes, total)] * chunk + [shape(chunk, total)],
        [freq_scale] + blocks,
        [SM] + [VM] * n_alt,
        [pltpu.VMEM((chunk, 3, modes, total), jnp.bfloat16)]
        + [pltpu.VMEM((chunk, modes, total), jnp.float32)]
        + [pltpu.VMEM((chunk, modes, 128), jnp.float32)] * 2,
        flops=2 * ITERS * chunk * flops,
    )
    following = along_chain(first, -1)
    inner, rest = kernel_call(
        functools.partial(advance_body, modes, total),
        [shape(2, modes, modes)] * 2,
        [coef, first, second],
        [VM] * 3,
        [pltpu.VMEM((modes, total), jnp.float32)],
        flops=8 * flops,
    )
    product = kernel_call(
        product_body, shape(2, modes, modes), [following, second, rest], [VM] * 3, flops=flops
    )

    def join(spans, backs):
        return kernel_call(
            functools.partial(join_body, halves, backs),
            shape(2, modes, modes),
            spans,
            [VM] * len(spans),
            flops=flops,
        )

    reach = min(4, length)
    backs = range(1, reach + 1)
    span = join([along_chain(product, back) for back in backs], backs)
    while length > 4 * reach:
        backs = range(0, 4 * reach, reach)
        span = join([span] + [along_chain(span, back) for back in backs[1:]], backs)
        reach *= 4
    rows = jnp.concatenate([source, jnp.zeros((freqs, 6, modes), jnp.float32)], axis=1)
    backs = range(0, length, reach)
    parts = kernel_call(
        functools.partial(
            field_body, halves, backs, n_alt, width, (float(total) / float(modes)) ** 0.5
        ),
        [shape(chunk, 2, width)] * n_alt,
        [rows, span] + [along_chain(span, back) for back in backs[1:]] + [inner, first, second],
        [VM] * (4 + len(backs)),
    )
    parts = [parts[0]] + [around(parts[k], k) for k in range(1, n_alt)]
    return kernel_call(
        functools.partial(settle_body, halves, n_alt),
        shape(freqs, seg_count, 2, width),
        parts,
        [VM] * n_alt,
    )


def solution(mesh):
    in_specs = (P("freq"), P("alt"), P("range", "alt"), P(None, "alt"), P("freq", None, None))
    out_specs = P("freq", "range", None, "alt")
    return jax.shard_map(local, mesh=mesh, in_specs=in_specs, out_specs=out_specs, check_vma=False)
```

```python
import functools

import jax
import jax.numpy as jnp
from jax import lax
from jax.experimental import pallas as pl
from jax.experimental.pallas import tpu as pltpu
from jax.sharding import PartitionSpec as P

ITERS = 8

phase_step = 0.15
relief = 0.1
HIGHEST = lax.Precision.HIGHEST
VMEM_LIMIT = 48 * 2**20
HALF = 48


def mm(left, right):
    return lax.dot_general(
        left, right, (((1,), (0,)), ((), ())), precision=HIGHEST, preferred_element_type=jnp.float32
    )


def mmt(left, right):
    return lax.dot_general(
        left, right, (((1,), (1,)), ((), ())), precision=HIGHEST, preferred_element_type=jnp.float32
    )


def short_mm(left, right):
    return lax.dot_general(
        left, right, (((1,), (0,)), ((), ())), preferred_element_type=jnp.float32
    )


def short_mmt(left, right):
    return lax.dot_general(
        left, right, (((1,), (1,)), ((), ())), preferred_element_type=jnp.float32
    )


def kernel_call(body, out_shape, args, specs, scratch=(), flops=0):
    nbytes = sum(4 * a.size for a in args) + sum(4 * o.size for o in jax.tree.leaves(out_shape))
    return pl.pallas_call(
        body,
        out_shape=out_shape,
        in_specs=specs,
        out_specs=jax.tree.map(lambda _: pl.BlockSpec(memory_space=pltpu.VMEM), out_shape),
        scratch_shapes=scratch,
        cost_estimate=pl.CostEstimate(flops=flops, bytes_accessed=nbytes, transcendentals=0),
        compiler_params=pltpu.CompilerParams(vmem_limit_bytes=VMEM_LIMIT),
    )(*args)


VM = pl.BlockSpec(memory_space=pltpu.VMEM)
SM = pl.BlockSpec(memory_space=pltpu.SMEM)


def shape(*dims):
    return jax.ShapeDtypeStruct(dims, jnp.float32)


def row_of(value, at):
    return jnp.broadcast_to(value[at : at + 1, :], value.shape)


def pack_pair(one, two):
    left = lax.broadcasted_iota(jnp.int32, one.shape, 1) < 64
    return [
        jnp.where(left, one, pltpu.roll(two, 64, 1)),
        jnp.where(left, pltpu.roll(one, 128 - HALF, 1), pltpu.roll(two, 64 - HALF, 1)),
    ]


def unpack_pair(low, high):
    early = lax.broadcasted_iota(jnp.int32, low.shape, 1) < HALF
    return (
        jnp.where(early, low, pltpu.roll(high, HALF, 1)),
        jnp.where(early, pltpu.roll(low, 64, 1), pltpu.roll(high, 64 + HALF, 1)),
    )


def inverse_factors(one, two):
    count = len(one)
    lanes = lax.broadcasted_iota(jnp.int32, (8, 128), 1)
    subs = lax.broadcasted_iota(jnp.int32, (8, 128), 0)
    base = jnp.where(lanes < 64, 0, 64)
    column = lanes - base
    work = [pack_pair(a, b) for a, b in zip(one, two)]
    results = []

    def place(k):
        side = 8 * k // HALF
        return side, 8 * k - side * HALF

    def spread(v, k):
        side, first = place(k)
        return [
            jnp.take_along_axis(work[v][side], base + (first + c), axis=1) for c in range(8)
        ]

    panel = spread(0, 0)
    for k in range(count):
        side, first = place(k)
        near = spread(k + 1, k) if k + 1 < count else None
        ahead = spread(k + 1, k + 1) if k + 1 < count else None
        weights = [[None] * 8 for _ in range(8)]
        inverses, lines = [], []
        scales = jnp.ones((8, 128), jnp.float32)
        for c in range(0, 8, 2):
            corner, cross, late = (
                row_of(panel[c], c),
                row_of(panel[c + 1], c),
                row_of(panel[c + 1], c + 1),
            )
            inv = 1.0 / corner
            second = corner * (1.0 / (corner * late - cross * cross))
            ratio = cross * inv
            weights[c][c + 1] = cross
            factor = panel[c] * inv
            rest = panel[c + 1] - factor * cross
            for d in range(c + 2, 8):
                weights[c][d] = row_of(panel[d], c)
                weights[c + 1][d] = row_of(panel[d], c + 1) - ratio * weights[c][d]
                panel[d] = (panel[d] - factor * weights[c][d]) - (
                    rest * weights[c + 1][d]
                ) * second
            pair = (jnp.where(subs > c, factor, 0.0), jnp.where(subs > c + 1, rest * second, 0.0))
            for e in range(2):
                inverses.append((inv, second)[e])
                scales = jnp.where(subs == c + e, inverses[-1], scales)
                line = [row_of(part, c + e) for part in work[k]]
                line[side] = line[side] + jnp.where(column == first + c + e, 1.0, 0.0)
                lines.append(line)
                work[k] = [part - pair[e] * along for part, along in zip(work[k], line)]
        if near is not None:
            for c in range(8):
                factor = near[c] * inverses[c]
                for d in range(c + 1, 8):
                    near[d] = near[d] - factor * weights[c][d]
                for d in range(8):
                    ahead[d] = ahead[d] - factor * row_of(near[c], d)
                work[k + 1] = [
                    part - factor * along for part, along in zip(work[k + 1], lines[c])
                ]
        panel = ahead
        scaled = [[part * inv for part in line] for line, inv in zip(lines, inverses)]
        for v in range(k + 2, count):
            there, at = place(v)
            for c in range(8):
                factor = jnp.take_along_axis(scaled[c][there], base + subs + at, axis=1)
                work[v] = [part - factor * along for part, along in zip(work[v], lines[c])]
        root = lax.sqrt(scales)
        unit = jnp.where(column == subs + first, 1.0, 0.0)
        own = jnp.where(column < subs + first, work[k][side], unit) * root
        other = work[k][0] * root if side else jnp.zeros((8, 128), jnp.float32)
        results.append(unpack_pair(other, own) if side else unpack_pair(own, other))
    return [pair[0] for pair in results], [pair[1] for pair in results]


def edge_weights(width):
    lanes = lax.broadcasted_iota(jnp.int32, (1, width), 1)
    return jnp.where(lanes == 0, 0.0, 0.5), jnp.where(lanes == width - 1, 0.0, 0.5)


def apply_rows(value, coef, from_low, from_high):
    width = value.shape[1]
    return (
        coef * value
        + from_low * pltpu.roll(value, 1, 1)
        + from_high * pltpu.roll(value, width - 1, 1)
    )


def iterate_body(n_alt, chunk, seg_count, modes, width, scale_ref, *refs):
    blocks, out_refs = refs[:n_alt], refs[n_alt : n_alt + chunk]
    coef_ref, split_ref, image_ref, gram_ref, inv_ref = refs[n_alt + chunk :]
    place = lax.axis_index("alt")
    flat = place * chunk
    freq = flat // seg_count
    first = flat - freq * seg_count
    total = n_alt * width
    for k, block in enumerate(blocks):
        source = lax.rem(place + n_alt - k, n_alt)
        span = pl.ds(pl.multiple_of(source * width, width), width)
        start = block[0:modes, :] * (1.0 / float(total) ** 0.5)
        for i in range(chunk):
            out_refs[i][:, span] = start
            change = block[pl.ds(modes + 1 + first + i, 1), :]
            coef_ref[i : i + 1, span] = scale_ref[freq] * (
                block[modes : modes + 1, :] * (1.0 + relief * change)
            )
    from_low, from_high = edge_weights(total)
    down = 2.0**-11
    gram_ref[...] = jnp.zeros_like(gram_ref)

    def factorise():
        grams = [[gram_ref[i, at : at + 8, :] for at in range(0, modes, 8)] for i in range(chunk)]
        results = inverse_factors(*grams)
        for i in range(chunk):
            for at in range(0, modes, 8):
                inv_ref[i, at : at + 8, :] = results[i][at // 8] * down**0.5

    def step(_, carry):
        for i in range(chunk):
            coef = coef_ref[i : i + 1, :]
            for at in range(0, modes, 16):
                image = apply_rows(out_refs[i][at : at + 16, :], coef, from_low, from_high)
                for part in range(3):
                    piece = image.astype(jnp.bfloat16)
                    split_ref[i, part, at : at + 16, :] = piece
                    image = image - piece.astype(jnp.float32)
            high, low = split_ref[i, 0], split_ref[i, 1]
            gram = short_mmt(high, high) + short_mmt(high, low) + short_mmt(low, high)
            gram_ref[i, :, 0:modes] = gram * down
        factorise()
        for i in range(chunk):
            inv = inv_ref[i, :, 0:modes].astype(jnp.bfloat16)
            for at in range(0, total, 256):
                out_refs[i][:, at : at + 256] = sum(
                    short_mm(inv, split_ref[i, part, :, at : at + 256]) for part in range(3)
                )
        return carry

    lax.fori_loop(0, ITERS - 1, step, 0)
    for i in range(chunk):
        for at in range(0, modes, 8):
            image_ref[i, at : at + 8, :] = apply_rows(
                out_refs[i][at : at + 8, :], coef_ref[i : i + 1, :], from_low, from_high
            )
        image = image_ref[i]
        gram_ref[i, :, 0:modes] = mmt(image, image) * down
    factorise()
    for i in range(chunk):
        inv = inv_ref[i, :, 0:modes]
        for at in range(0, total, 256):
            out_refs[i][:, at : at + 256] = mm(inv, image_ref[i, :, at : at + 256])


def unit_of(modes):
    rows = lax.broadcasted_iota(jnp.int32, (modes, modes), 0)
    return jnp.where(rows == lax.broadcasted_iota(jnp.int32, (modes, modes), 1), 1.0, 0.0)


def complex_mm(left, right):
    return (
        mm(left[0], right[0]) - mm(left[1], right[1]),
        mm(left[0], right[1]) + mm(left[1], right[0]),
    )


def advance_body(modes, total, coef_ref, first_ref, second_ref, inner_ref, rest_ref, image_ref):
    from_low, from_high = edge_weights(total)
    unit = unit_of(modes)
    turns = []
    for i, ref in enumerate((first_ref, second_ref)):
        for at in range(0, modes, 8):
            image_ref[at : at + 8, :] = apply_rows(
                ref[at : at + 8, :], coef_ref[i : i + 1, :], from_low, from_high
            )
        phase = phase_step * mmt(ref[...], image_ref[...])
        square = mm(phase, phase)
        turns.append(
            (unit - 0.5 * square + mm(square, square) / 24.0, phase - mm(phase, square) / 6.0)
        )
    corr = mmt(second_ref[...], first_ref[...])
    inner = (mm(corr, turns[0][0]), mm(corr, turns[0][1]))
    rest = complex_mm(turns[1], inner)
    for part in range(2):
        inner_ref[part] = inner[part]
        rest_ref[part] = rest[part]


def chain_place(halves):
    return lax.axis_index("range") * halves + lax.rem(lax.axis_index("alt"), halves)


def product_body(next_ref, second_ref, rest_ref, out_ref):
    corr = mmt(next_ref[...], second_ref[...])
    for part in range(2):
        out_ref[part] = mm(corr, rest_ref[part])


def group_body(halves, group, *refs):
    at = lax.rem(chain_place(halves), group)
    sorted_ref, out_ref = refs[group:]
    for k, ref in enumerate(refs[:group]):
        sorted_ref[lax.rem(at + group - k, group)] = ref[...]
    spans = [(sorted_ref[j, 0], sorted_ref[j, 1]) for j in reversed(range(group))]
    out_ref[0], out_ref[1] = fold(spans)


def fold(spans):
    while len(spans) > 1:
        pairs = [complex_mm(*spans[i : i + 2]) for i in range(0, len(spans) - 1, 2)]
        spans = pairs + spans[len(pairs) * 2 :]
    return spans[0]


def inside_body(halves, group, sorted_ref, inner_ref, out_ref):
    at = lax.rem(chain_place(halves), group)
    unit = unit_of(inner_ref.shape[1])
    spans = []
    for j in reversed(range(group - 1)):
        real = jnp.where(j < at, sorted_ref[j, 0], unit)
        spans.append((real, jnp.where(j < at, sorted_ref[j, 1], 0.0)))
    reached = fold(spans)
    following = complex_mm((inner_ref[0], inner_ref[1]), reached)
    for part in range(2):
        out_ref[0, part] = reached[part]
        out_ref[1, part] = following[part]


def join_body(halves, group, backs, *refs):
    at = chain_place(halves) // group
    spans = []
    for back, ref in zip(backs, refs):
        missing = jnp.where(at < back, unit_of(ref.shape[1]), 0.0)
        spans.append((ref[0] + missing, ref[1]) if back else (ref[0], ref[1]))
    refs[-1][0], refs[-1][1] = fold(spans)


def turn_vector(matrix, vector):
    rows = lax.broadcasted_iota(jnp.int32, vector.shape, 0)
    swapped = jnp.where(
        rows == 0, -row_of(vector, 1), jnp.where(rows == 1, row_of(vector, 0), 0.0)
    )
    return mmt(vector, matrix[0]) + mmt(swapped, matrix[1])


def field_body(halves, group, backs, n_alt, width, scale, source_ref, *refs):
    count = len(backs)
    inside_ref, first_ref, second_ref = refs[count : count + 3]
    place = lax.axis_index("alt")
    amp = source_ref[place // halves]
    for back, ref in reversed(list(zip(backs, refs))):
        moved = turn_vector((ref[0], ref[1]), amp)
        amp = jnp.where(chain_place(halves) // group < back, amp, moved)
    amps = [turn_vector((inside_ref[i, 0], inside_ref[i, 1]), amp) for i in range(2)]
    for k, out_ref in enumerate(refs[count + 3 :]):
        target = lax.rem(place + k, n_alt)
        span = pl.ds(pl.multiple_of(target * width, width), width)
        for i, ref in enumerate((first_ref, second_ref)):
            out_ref[i] = scale * mm(amps[i], ref[:, span])[0:2, :]


def settle_body(halves, n_alt, *refs):
    place = lax.axis_index("alt")
    out_ref = refs[n_alt]
    for k, part_ref in enumerate(refs[:n_alt]):
        source = lax.rem(place + n_alt - k, n_alt)
        chunk = part_ref.shape[0]
        freq, half = source // halves, lax.rem(source, halves)
        for i in range(chunk):
            out_ref[freq, half * chunk + i] = part_ref[i]


def local(freq_scale, base_profile, perturb, start_block, source):
    freqs = freq_scale.shape[0]
    seg_count = perturb.shape[0]
    modes, width = start_block.shape
    n_alt = lax.axis_size("alt")
    n_range = lax.axis_size("range")
    total = width * n_alt
    chunk = freqs * seg_count // n_alt
    halves = seg_count // chunk
    length = n_range * halves
    assert modes == 2 * HALF and chunk == 2 and halves * chunk == seg_count and halves * freqs == n_alt

    def device(freq, at):
        return at // halves * n_alt + freq * halves + at % halves

    def along_chain(value, steps):
        pairs = []
        for freq in range(freqs):
            for at in range(max(0, -steps), min(length, length - steps)):
                pairs.append((device(freq, at), device(freq, at + steps)))
        return lax.ppermute(value, ("range", "alt"), pairs)

    def around(value, k):
        return lax.ppermute(value, "alt", [(i, (i + k) % n_alt) for i in range(n_alt)])

    lines = [start_block, base_profile[None, :], perturb]
    filler = jnp.zeros((-(modes + 1 + seg_count) % 8, width), jnp.float32)
    mine = jnp.concatenate(lines + [filler], axis=0)
    blocks = [mine] + [around(mine, k) for k in range(1, n_alt)]
    flops = 2 * modes * modes * total
    first, second, coef = kernel_call(
        functools.partial(iterate_body, n_alt, chunk, seg_count, modes, width),
        [shape(modes, total)] * chunk + [shape(chunk, total)],
        [freq_scale] + blocks,
        [SM] + [VM] * n_alt,
        [pltpu.VMEM((chunk, 3, modes, total), jnp.bfloat16)]
        + [pltpu.VMEM((chunk, modes, total), jnp.float32)]
        + [pltpu.VMEM((chunk, modes, 128), jnp.float32)] * 2,
        flops=2 * ITERS * chunk * flops,
    )
    following = along_chain(first, -1)
    inner, rest = kernel_call(
        functools.partial(advance_body, modes, total),
        [shape(2, modes, modes)] * 2,
        [coef, first, second],
        [VM] * 3,
        [pltpu.VMEM((modes, total), jnp.float32)],
        flops=8 * flops,
    )
    product = kernel_call(
        product_body, shape(2, modes, modes), [following, second, rest], [VM] * 3, flops=flops
    )

    group = 4
    groups = length // group
    assert groups * group == length

    def turned(k):
        pairs = []
        for freq in range(freqs):
            for at in range(length):
                goal = at // group * group + (at + k) % group
                pairs.append((device(freq, at), device(freq, goal)))
        return lax.ppermute(product, ("range", "alt"), pairs)

    ordered, span = kernel_call(
        functools.partial(group_body, halves, group),
        [shape(group, 2, modes, modes), shape(2, modes, modes)],
        [product] + [turned(k) for k in range(1, group)],
        [VM] * group,
        flops=flops,
    )

    def join(spans, backs):
        return kernel_call(
            functools.partial(join_body, halves, group, backs),
            shape(2, modes, modes),
            spans,
            [VM] * len(spans),
            flops=flops,
        )

    def from_back(backs):
        return [along_chain(span, group * back) if back else span for back in backs]

    backs = range(1, groups)
    if groups > 4:
        backs = range(1, 5)
        span = join(from_back(backs), backs)
        reach = 4
        while groups > 4 * reach:
            backs = range(0, 4 * reach, reach)
            span = join(from_back(backs), backs)
            reach *= 4
        backs = range(0, groups, reach)
    came = from_back(backs)
    inside = kernel_call(
        functools.partial(inside_body, halves, group),
        shape(2, 2, modes, modes),
        [ordered, inner],
        [VM] * 2,
        flops=flops,
    )
    rows = jnp.concatenate([source, jnp.zeros((freqs, 6, modes), jnp.float32)], axis=1)
    parts = kernel_call(
        functools.partial(
            field_body, halves, group, backs, n_alt, width, (float(total) / float(modes)) ** 0.5
        ),
        [shape(chunk, 2, width)] * n_alt,
        [rows] + came + [inside, first, second],
        [VM] * (4 + len(came)),
    )
    parts = [parts[0]] + [around(parts[k], k) for k in range(1, n_alt)]
    return kernel_call(
        functools.partial(settle_body, halves, n_alt),
        shape(freqs, seg_count, 2, width),
        parts,
        [VM] * n_alt,
    )


def solution(mesh):
    in_specs = (P("freq"), P("alt"), P("range", "alt"), P(None, "alt"), P("freq", None, None))
    out_specs = P("freq", "range", None, "alt")
    return jax.shard_map(local, mesh=mesh, in_specs=in_specs, out_specs=out_specs, check_vma=False)
```

```python
import functools

import jax
import jax.numpy as jnp
from jax import lax
from jax.experimental import pallas as pl
from jax.experimental.pallas import tpu as pltpu
from jax.sharding import PartitionSpec as P

ITERS = 8

phase_step = 0.15
relief = 0.1
HIGHEST = lax.Precision.HIGHEST
VMEM_LIMIT = 48 * 2**20
HALF = 48


def mm(left, right):
    return lax.dot_general(
        left, right, (((1,), (0,)), ((), ())), precision=HIGHEST, preferred_element_type=jnp.float32
    )


def mmt(left, right):
    return lax.dot_general(
        left, right, (((1,), (1,)), ((), ())), precision=HIGHEST, preferred_element_type=jnp.float32
    )


def short_mm(left, right):
    return lax.dot_general(
        left, right, (((1,), (0,)), ((), ())), preferred_element_type=jnp.float32
    )


def short_mmt(left, right):
    return lax.dot_general(
        left, right, (((1,), (1,)), ((), ())), preferred_element_type=jnp.float32
    )


def kernel_call(body, out_shape, args, specs, scratch=(), flops=0):
    nbytes = sum(4 * a.size for a in args) + sum(4 * o.size for o in jax.tree.leaves(out_shape))
    return pl.pallas_call(
        body,
        out_shape=out_shape,
        in_specs=specs,
        out_specs=jax.tree.map(lambda _: pl.BlockSpec(memory_space=pltpu.VMEM), out_shape),
        scratch_shapes=scratch,
        cost_estimate=pl.CostEstimate(flops=flops, bytes_accessed=nbytes, transcendentals=0),
        compiler_params=pltpu.CompilerParams(vmem_limit_bytes=VMEM_LIMIT),
    )(*args)


VM = pl.BlockSpec(memory_space=pltpu.VMEM)
SM = pl.BlockSpec(memory_space=pltpu.SMEM)


def shape(*dims):
    return jax.ShapeDtypeStruct(dims, jnp.float32)


def row_of(value, at):
    return jnp.broadcast_to(value[at : at + 1, :], value.shape)


def pack_pair(one, two):
    left = lax.broadcasted_iota(jnp.int32, one.shape, 1) < 64
    return [
        jnp.where(left, one, pltpu.roll(two, 64, 1)),
        jnp.where(left, pltpu.roll(one, 128 - HALF, 1), pltpu.roll(two, 64 - HALF, 1)),
    ]


def unpack_pair(low, high):
    early = lax.broadcasted_iota(jnp.int32, low.shape, 1) < HALF
    return (
        jnp.where(early, low, pltpu.roll(high, HALF, 1)),
        jnp.where(early, pltpu.roll(low, 64, 1), pltpu.roll(high, 64 + HALF, 1)),
    )


def inverse_factors(work):
    work = [list(pair) for pair in work]
    count = len(work)
    lanes = lax.broadcasted_iota(jnp.int32, (8, 128), 1)
    subs = lax.broadcasted_iota(jnp.int32, (8, 128), 0)
    base = jnp.where(lanes < 64, 0, 64)
    column = lanes - base
    results = []

    def place(k):
        side = 8 * k // HALF
        return side, 8 * k - side * HALF

    def spread(v, k):
        side, first = place(k)
        return [
            jnp.take_along_axis(work[v][side], base + (first + c), axis=1) for c in range(8)
        ]

    panel = spread(0, 0)
    for k in range(count):
        side, first = place(k)
        near = spread(k + 1, k) if k + 1 < count else None
        ahead = spread(k + 1, k + 1) if k + 1 < count else None
        weights = [[None] * 8 for _ in range(8)]
        inverses, lines = [], []
        scales = jnp.ones((8, 128), jnp.float32)
        for c in range(0, 8, 2):
            corner, cross, late = (
                row_of(panel[c], c),
                row_of(panel[c + 1], c),
                row_of(panel[c + 1], c + 1),
            )
            inv = 1.0 / corner
            second = corner * (1.0 / (corner * late - cross * cross))
            ratio = cross * inv
            weights[c][c + 1] = cross
            factor = panel[c] * inv
            rest = panel[c + 1] - factor * cross
            for d in range(c + 2, 8):
                weights[c][d] = row_of(panel[d], c)
                weights[c + 1][d] = row_of(panel[d], c + 1) - ratio * weights[c][d]
                panel[d] = (panel[d] - factor * weights[c][d]) - (
                    rest * weights[c + 1][d]
                ) * second
            pair = (jnp.where(subs > c, factor, 0.0), jnp.where(subs > c + 1, rest * second, 0.0))
            for e in range(2):
                inverses.append((inv, second)[e])
                scales = jnp.where(subs == c + e, inverses[-1], scales)
                line = [row_of(part, c + e) for part in work[k]]
                line[side] = line[side] + jnp.where(column == first + c + e, 1.0, 0.0)
                lines.append(line)
                work[k] = [part - pair[e] * along for part, along in zip(work[k], line)]
        if near is not None:
            for c in range(8):
                factor = near[c] * inverses[c]
                for d in range(c + 1, 8):
                    near[d] = near[d] - factor * weights[c][d]
                for d in range(8):
                    ahead[d] = ahead[d] - factor * row_of(near[c], d)
                work[k + 1] = [
                    part - factor * along for part, along in zip(work[k + 1], lines[c])
                ]
        panel = ahead
        scaled = [[part * inv for part in line] for line, inv in zip(lines, inverses)]
        for v in range(k + 2, count):
            there, at = place(v)
            for c in range(8):
                factor = jnp.take_along_axis(scaled[c][there], base + subs + at, axis=1)
                work[v] = [part - factor * along for part, along in zip(work[v], lines[c])]
        root = lax.sqrt(scales)
        unit = jnp.where(column == subs + first, 1.0, 0.0)
        own = jnp.where(column < subs + first, work[k][side], unit) * root
        other = work[k][0] * root if side else jnp.zeros((8, 128), jnp.float32)
        results.append((other, own) if side else (own, other))
    return results


def doubled_operator(value, coef):
    width = value.shape[1]
    lanes = lax.broadcasted_iota(jnp.int32, (value.shape[0], 128), 1)
    below, above = pltpu.roll(value, 1, 1), pltpu.roll(value, width - 1, 1)
    below = jnp.concatenate(
        [jnp.where(lanes == 0, 0.0, below[:, :128]), below[:, 128:]], axis=1
    )
    above = jnp.concatenate(
        [above[:, :-128], jnp.where(lanes == 127, 0.0, above[:, -128:])], axis=1
    )
    return coef * value + (below + above)


DOWN = 2.0**-13


def iterate_body(n_alt, chunk, seg_count, modes, width, scale_ref, *refs):
    blocks, image_refs = refs[:n_alt], refs[n_alt : n_alt + chunk]
    coef_ref, basis_ref, split_ref, gram_ref, inv_ref = refs[n_alt + chunk :]
    place = lax.axis_index("alt")
    flat = place * chunk
    freq = flat // seg_count
    first = flat - freq * seg_count
    total = n_alt * width
    for k, block in enumerate(blocks):
        source = lax.rem(place + n_alt - k, n_alt)
        span = pl.ds(pl.multiple_of(source * width, width), width)
        start = block[0:modes, :] * (1.0 / float(total) ** 0.5)
        for i in range(chunk):
            basis_ref[i, :, span] = start
            change = block[pl.ds(modes + 1 + first + i, 1), :]
            coef_ref[i : i + 1, span] = (2.0 * scale_ref[freq]) * (
                block[modes : modes + 1, :] * (1.0 + relief * change)
            )
    split_ref[...] = jnp.zeros_like(split_ref)
    left = lax.broadcasted_iota(jnp.int32, (8, 128), 1) < 64

    def packed_row(i, at):
        return at // HALF * 128 + i * 64 + at % HALF

    def step(_, carry):
        for i in range(chunk):
            coef = coef_ref[i : i + 1, :]
            for at in range(0, modes, 16):
                image = doubled_operator(basis_ref[i, at : at + 16, :], coef)
                row = packed_row(i, at)
                for part in range(3):
                    piece = image.astype(jnp.bfloat16)
                    split_ref[part, row : row + 16, :] = piece
                    image = image - piece.astype(jnp.float32)
        gram_ref[...] = short_mmt(split_ref[0], split_ref[0]) * DOWN
        work = []
        for at in range(0, modes, 8):
            one, two = packed_row(0, at), packed_row(1, at)
            work.append(
                [
                    jnp.where(
                        left,
                        gram_ref[one : one + 8, side : side + 128],
                        gram_ref[two : two + 8, side : side + 128],
                    )
                    for side in (0, 128)
                ]
            )
        rows = inverse_factors(work)
        for at in range(0, modes, 16):
            for half in range(2):
                part = jnp.concatenate([rows[at // 8][half], rows[at // 8 + 1][half]], axis=0)
                part = part * DOWN**0.5
                here = lax.broadcasted_iota(jnp.int32, part.shape, 1) < 64
                span = slice(half * 128, half * 128 + 128)
                inv_ref[0, at : at + 16, span] = jnp.where(here, part, 0.0).astype(jnp.bfloat16)
                inv_ref[1, at : at + 16, span] = jnp.where(here, 0.0, part).astype(jnp.bfloat16)
        for i in range(chunk):
            for at in range(0, total, 256):
                basis_ref[i, :, at : at + 256] = sum(
                    short_mm(inv_ref[i], split_ref[part, :, at : at + 256]) for part in range(3)
                )
        return carry

    lax.fori_loop(0, ITERS - 1, step, 0)
    for i in range(chunk):
        for at in range(0, modes, 8):
            image_refs[i][at : at + 8, :] = doubled_operator(
                basis_ref[i, at : at + 8, :], coef_ref[i : i + 1, :]
            )


def unit_of(modes):
    rows = lax.broadcasted_iota(jnp.int32, (modes, modes), 0)
    return jnp.where(rows == lax.broadcasted_iota(jnp.int32, (modes, modes), 1), 1.0, 0.0)


def complex_mm(left, right):
    return (
        mm(left[0], right[0]) - mm(left[1], right[1]),
        mm(left[0], right[1]) + mm(left[1], right[0]),
    )


def finish_body(halves, modes, total, coef_ref, *refs):
    image_refs, basis_refs = refs[0:2], refs[2:4]
    turn_ref, inner_ref, rest_ref, gram_ref, double_ref = refs[4:]
    unit = unit_of(modes)
    gram_ref[...] = jnp.zeros_like(gram_ref)
    for i in range(2):
        image = image_refs[i][...]
        gram_ref[i, :, 0:modes] = mmt(image, image) * DOWN
    grams = [gram_ref[i, at : at + 8, :] for at in range(0, modes, 8) for i in range(2)]
    rows = inverse_factors([pack_pair(*grams[i : i + 2]) for i in range(0, len(grams), 2)])
    for k, pair in enumerate(rows):
        for i, part in enumerate(unpack_pair(*pair)):
            gram_ref[i, 8 * k : 8 * k + 8, :] = part * DOWN**0.5
    turns = []
    for i in range(2):
        inv = gram_ref[i, :, 0:modes]
        for at in range(0, total, 256):
            basis_refs[i][:, at : at + 256] = mm(inv, image_refs[i][:, at : at + 256])
    for i, ref in enumerate(basis_refs):
        for at in range(0, modes, 8):
            double_ref[at : at + 8, :] = doubled_operator(
                ref[at : at + 8, :], coef_ref[i : i + 1, :]
            )
        phase = (0.5 * phase_step) * mmt(ref[...], double_ref[...])
        square = mm(phase, phase)
        turns.append(
            (unit - 0.5 * square + mm(square, square) / 24.0, phase - mm(phase, square) / 6.0)
        )
    corr = mmt(basis_refs[1][...], basis_refs[0][...])
    inner = (mm(corr, turns[0][0]), mm(corr, turns[0][1]))
    turn = jnp.where(chain_place(halves) == 0, unit, gram_ref[0, :, 0:modes])
    turn_ref[...] = turn
    rest = complex_mm(turns[1], (mm(inner[0], turn), mm(inner[1], turn)))
    for part in range(2):
        inner_ref[part] = inner[part]
        rest_ref[part] = rest[part]


def chain_place(halves):
    return lax.axis_index("range") * halves + lax.rem(lax.axis_index("alt"), halves)


def product_body(next_ref, second_ref, rest_ref, out_ref):
    corr = mmt(next_ref[...], second_ref[...])
    for part in range(2):
        out_ref[part] = mm(corr, rest_ref[part])


def group_body(halves, group, *refs):
    at = lax.rem(chain_place(halves), group)
    sorted_ref, out_ref = refs[group:]
    for k, ref in enumerate(refs[:group]):
        sorted_ref[lax.rem(at + group - k, group)] = ref[...]
    spans = [(sorted_ref[j, 0], sorted_ref[j, 1]) for j in reversed(range(group))]
    out_ref[0], out_ref[1] = fold(spans)


def fold(spans):
    while len(spans) > 1:
        pairs = [complex_mm(*spans[i : i + 2]) for i in range(0, len(spans) - 1, 2)]
        spans = pairs + spans[len(pairs) * 2 :]
    return spans[0]


def inside_body(halves, group, sorted_ref, turn_ref, inner_ref, out_ref):
    at = lax.rem(chain_place(halves), group)
    unit = unit_of(inner_ref.shape[1])
    spans = []
    for j in reversed(range(group - 1)):
        real = jnp.where(j < at, sorted_ref[j, 0], unit)
        spans.append((real, jnp.where(j < at, sorted_ref[j, 1], 0.0)))
    reached = fold(spans)
    reached = (mm(turn_ref[...], reached[0]), mm(turn_ref[...], reached[1]))
    following = complex_mm((inner_ref[0], inner_ref[1]), reached)
    for part in range(2):
        out_ref[0, part] = reached[part]
        out_ref[1, part] = following[part]


def join_body(halves, group, backs, *refs):
    at = chain_place(halves) // group
    spans = []
    for back, ref in zip(backs, refs):
        missing = jnp.where(at < back, unit_of(ref.shape[1]), 0.0)
        spans.append((ref[0] + missing, ref[1]) if back else (ref[0], ref[1]))
    refs[-1][0], refs[-1][1] = fold(spans)


def turn_vector(matrix, vector):
    rows = lax.broadcasted_iota(jnp.int32, vector.shape, 0)
    swapped = jnp.where(
        rows == 0, -row_of(vector, 1), jnp.where(rows == 1, row_of(vector, 0), 0.0)
    )
    return mmt(vector, matrix[0]) + mmt(swapped, matrix[1])


def field_body(halves, group, backs, n_alt, width, scale, source_ref, *refs):
    count = len(backs)
    inside_ref, first_ref, second_ref = refs[count : count + 3]
    place = lax.axis_index("alt")
    amp = source_ref[place // halves]
    for back, ref in reversed(list(zip(backs, refs))):
        moved = turn_vector((ref[0], ref[1]), amp)
        amp = jnp.where(chain_place(halves) // group < back, amp, moved)
    amps = [turn_vector((inside_ref[i, 0], inside_ref[i, 1]), amp) for i in range(2)]
    for k, out_ref in enumerate(refs[count + 3 :]):
        target = lax.rem(place + k, n_alt)
        span = pl.ds(pl.multiple_of(target * width, width), width)
        for i, ref in enumerate((first_ref, second_ref)):
            out_ref[i] = scale * mm(amps[i], ref[:, span])[0:2, :]


def settle_body(halves, n_alt, *refs):
    place = lax.axis_index("alt")
    out_ref = refs[n_alt]
    for k, part_ref in enumerate(refs[:n_alt]):
        source = lax.rem(place + n_alt - k, n_alt)
        chunk = part_ref.shape[0]
        freq, half = source // halves, lax.rem(source, halves)
        for i in range(chunk):
            out_ref[freq, half * chunk + i] = part_ref[i]


def local(freq_scale, base_profile, perturb, start_block, source):
    freqs = freq_scale.shape[0]
    seg_count = perturb.shape[0]
    modes, width = start_block.shape
    n_alt = lax.axis_size("alt")
    n_range = lax.axis_size("range")
    total = width * n_alt
    chunk = freqs * seg_count // n_alt
    halves = seg_count // chunk
    length = n_range * halves
    assert modes == 2 * HALF and chunk == 2 and halves * chunk == seg_count and halves * freqs == n_alt

    def device(freq, at):
        return at // halves * n_alt + freq * halves + at % halves

    def along_chain(value, steps):
        pairs = []
        for freq in range(freqs):
            for at in range(max(0, -steps), min(length, length - steps)):
                pairs.append((device(freq, at), device(freq, at + steps)))
        return lax.ppermute(value, ("range", "alt"), pairs)

    def around(value, k):
        return lax.ppermute(value, "alt", [(i, (i + k) % n_alt) for i in range(n_alt)])

    lines = [start_block, base_profile[None, :], perturb]
    filler = jnp.zeros((-(modes + 1 + seg_count) % 8, width), jnp.float32)
    mine = jnp.concatenate(lines + [filler], axis=0)
    blocks = [mine] + [around(mine, k) for k in range(1, n_alt)]
    flops = 2 * modes * modes * total
    image, other, coef = kernel_call(
        functools.partial(iterate_body, n_alt, chunk, seg_count, modes, width),
        [shape(modes, total)] * chunk + [shape(chunk, total)],
        [freq_scale] + blocks,
        [SM] + [VM] * n_alt,
        [
            pltpu.VMEM((chunk, modes, total), jnp.float32),
            pltpu.VMEM((3, 256, total), jnp.bfloat16),
            pltpu.VMEM((256, 256), jnp.float32),
            pltpu.VMEM((chunk, modes, 256), jnp.bfloat16),
        ],
        flops=2 * ITERS * chunk * flops,
    )
    following = along_chain(image, -1)
    first, second, turn, inner, rest = kernel_call(
        functools.partial(finish_body, halves, modes, total),
        [shape(modes, total)] * 2 + [shape(modes, modes)] + [shape(2, modes, modes)] * 2,
        [coef, image, other],
        [VM] * 3,
        [pltpu.VMEM((2, modes, 128), jnp.float32), pltpu.VMEM((modes, total), jnp.float32)],
        flops=16 * flops,
    )
    product = kernel_call(
        product_body, shape(2, modes, modes), [following, second, rest], [VM] * 3, flops=flops
    )

    group = 4
    groups = length // group
    assert groups * group == length

    def turned(value, size, k):
        pairs = []
        for freq in range(freqs):
            for at in range(length):
                goal = at // size * size + (at + k) % size
                pairs.append((device(freq, at), device(freq, goal)))
        return lax.ppermute(value, ("range", "alt"), pairs)

    ordered, span = kernel_call(
        functools.partial(group_body, halves, group),
        [shape(group, 2, modes, modes), shape(2, modes, modes)],
        [product] + [turned(product, group, k) for k in range(1, group)],
        [VM] * group,
        flops=flops,
    )

    def join(spans, backs):
        return kernel_call(
            functools.partial(join_body, halves, group, backs),
            shape(2, modes, modes),
            spans,
            [VM] * len(spans),
            flops=flops,
        )

    def from_back(backs):
        return [along_chain(span, group * back) if back else span for back in backs]

    if groups <= 4:
        backs = range(1, groups)
        came = [turned(span, length, group * back) for back in backs]
    else:
        backs = range(1, 5)
        span = join(from_back(backs), backs)
        reach = 4
        while groups > 4 * reach:
            backs = range(0, 4 * reach, reach)
            span = join(from_back(backs), backs)
            reach *= 4
        backs = range(0, groups, reach)
        came = from_back(backs)
    inside = kernel_call(
        functools.partial(inside_body, halves, group),
        shape(2, 2, modes, modes),
        [ordered, turn, inner],
        [VM] * 3,
        flops=flops,
    )
    rows = jnp.concatenate([source, jnp.zeros((freqs, 6, modes), jnp.float32)], axis=1)
    parts = kernel_call(
        functools.partial(
            field_body, halves, group, backs, n_alt, width, (float(total) / float(modes)) ** 0.5
        ),
        [shape(chunk, 2, width)] * n_alt,
        [rows] + came + [inside, first, second],
        [VM] * (4 + len(came)),
    )
    parts = [parts[0]] + [around(parts[k], k) for k in range(1, n_alt)]
    return kernel_call(
        functools.partial(settle_body, halves, n_alt),
        shape(freqs, seg_count, 2, width),
        parts,
        [VM] * n_alt,
    )


def solution(mesh):
    in_specs = (P("freq"), P("alt"), P("range", "alt"), P(None, "alt"), P("freq", None, None))
    out_specs = P("freq", "range", None, "alt")
    return jax.shard_map(local, mesh=mesh, in_specs=in_specs, out_specs=out_specs, check_vma=False)
```

```python
import functools

import jax
import jax.numpy as jnp
from jax import lax
from jax.experimental import pallas as pl
from jax.experimental.pallas import tpu as pltpu
from jax.sharding import PartitionSpec as P

ITERS = 8

phase_step = 0.15
relief = 0.1
HIGHEST = lax.Precision.HIGHEST
VMEM_LIMIT = 48 * 2**20
HALF = 48


def mm(left, right):
    return lax.dot_general(
        left, right, (((1,), (0,)), ((), ())), precision=HIGHEST, preferred_element_type=jnp.float32
    )


def mmt(left, right):
    return lax.dot_general(
        left, right, (((1,), (1,)), ((), ())), precision=HIGHEST, preferred_element_type=jnp.float32
    )


def short_mm(left, right):
    return lax.dot_general(
        left, right, (((1,), (0,)), ((), ())), preferred_element_type=jnp.float32
    )


def short_mmt(left, right):
    return lax.dot_general(
        left, right, (((1,), (1,)), ((), ())), preferred_element_type=jnp.float32
    )


def kernel_call(body, out_shape, args, specs, scratch=(), flops=0):
    nbytes = sum(4 * a.size for a in args) + sum(4 * o.size for o in jax.tree.leaves(out_shape))
    return pl.pallas_call(
        body,
        out_shape=out_shape,
        in_specs=specs,
        out_specs=jax.tree.map(lambda _: pl.BlockSpec(memory_space=pltpu.VMEM), out_shape),
        scratch_shapes=scratch,
        cost_estimate=pl.CostEstimate(flops=flops, bytes_accessed=nbytes, transcendentals=0),
        compiler_params=pltpu.CompilerParams(vmem_limit_bytes=VMEM_LIMIT),
    )(*args)


VM = pl.BlockSpec(memory_space=pltpu.VMEM)
SM = pl.BlockSpec(memory_space=pltpu.SMEM)


def shape(*dims):
    return jax.ShapeDtypeStruct(dims, jnp.float32)


def row_of(value, at):
    return jnp.broadcast_to(value[at : at + 1, :], value.shape)


def pack_pair(one, two):
    left = lax.broadcasted_iota(jnp.int32, one.shape, 1) < 64
    return [
        jnp.where(left, one, pltpu.roll(two, 64, 1)),
        jnp.where(left, pltpu.roll(one, 128 - HALF, 1), pltpu.roll(two, 64 - HALF, 1)),
    ]


def unpack_pair(low, high):
    early = lax.broadcasted_iota(jnp.int32, low.shape, 1) < HALF
    return (
        jnp.where(early, low, pltpu.roll(high, HALF, 1)),
        jnp.where(early, pltpu.roll(low, 64, 1), pltpu.roll(high, 64 + HALF, 1)),
    )


def inverse_factors(work):
    work = [list(pair) for pair in work]
    count = len(work)
    lanes = lax.broadcasted_iota(jnp.int32, (8, 128), 1)
    subs = lax.broadcasted_iota(jnp.int32, (8, 128), 0)
    base = jnp.where(lanes < 64, 0, 64)
    column = lanes - base
    results = []

    def place(k):
        side = 8 * k // HALF
        return side, 8 * k - side * HALF

    def spread(v, k):
        side, first = place(k)
        return [
            jnp.take_along_axis(work[v][side], base + (first + c), axis=1) for c in range(8)
        ]

    panel = spread(0, 0)
    for k in range(count):
        side, first = place(k)
        near = spread(k + 1, k) if k + 1 < count else None
        ahead = spread(k + 1, k + 1) if k + 1 < count else None
        weights = [[None] * 8 for _ in range(8)]
        inverses, lines = [], []
        scales = jnp.ones((8, 128), jnp.float32)
        for c in range(0, 8, 2):
            corner, cross, late = (
                row_of(panel[c], c),
                row_of(panel[c + 1], c),
                row_of(panel[c + 1], c + 1),
            )
            inv = 1.0 / corner
            second = corner * (1.0 / (corner * late - cross * cross))
            ratio = cross * inv
            weights[c][c + 1] = cross
            factor = panel[c] * inv
            rest = panel[c + 1] - factor * cross
            for d in range(c + 2, 8):
                weights[c][d] = row_of(panel[d], c)
                weights[c + 1][d] = row_of(panel[d], c + 1) - ratio * weights[c][d]
                panel[d] = (panel[d] - factor * weights[c][d]) - (
                    rest * weights[c + 1][d]
                ) * second
            pair = (jnp.where(subs > c, factor, 0.0), jnp.where(subs > c + 1, rest * second, 0.0))
            for e in range(2):
                inverses.append((inv, second)[e])
                scales = jnp.where(subs == c + e, inverses[-1], scales)
                line = [row_of(part, c + e) for part in work[k]]
                line[side] = line[side] + jnp.where(column == first + c + e, 1.0, 0.0)
                lines.append(line)
                work[k] = [part - pair[e] * along for part, along in zip(work[k], line)]
        if near is not None:
            for c in range(8):
                factor = near[c] * inverses[c]
                for d in range(c + 1, 8):
                    near[d] = near[d] - factor * weights[c][d]
                for d in range(8):
                    ahead[d] = ahead[d] - factor * row_of(near[c], d)
                work[k + 1] = [
                    part - factor * along for part, along in zip(work[k + 1], lines[c])
                ]
        panel = ahead
        scaled = [[part * inv for part in line] for line, inv in zip(lines, inverses)]
        for v in range(k + 2, count):
            there, at = place(v)
            for c in range(8):
                factor = jnp.take_along_axis(scaled[c][there], base + subs + at, axis=1)
                work[v] = [part - factor * along for part, along in zip(work[v], lines[c])]
        root = lax.sqrt(scales)
        unit = jnp.where(column == subs + first, 1.0, 0.0)
        own = jnp.where(column < subs + first, work[k][side], unit) * root
        other = work[k][0] * root if side else jnp.zeros((8, 128), jnp.float32)
        results.append((other, own) if side else (own, other))
    return results


def doubled_operator(value, coef):
    width = value.shape[1]
    lanes = lax.broadcasted_iota(jnp.int32, (value.shape[0], 128), 1)
    below, above = pltpu.roll(value, 1, 1), pltpu.roll(value, width - 1, 1)
    below = jnp.concatenate(
        [jnp.where(lanes == 0, 0.0, below[:, :128]), below[:, 128:]], axis=1
    )
    above = jnp.concatenate(
        [above[:, :-128], jnp.where(lanes == 127, 0.0, above[:, -128:])], axis=1
    )
    return coef * value + (below + above)


DOWN = 2.0**-13


def pack_body(modes, seg_count, start_ref, base_ref, perturb_ref, out_ref):
    out_ref[0:modes, :] = start_ref[...]
    out_ref[modes : modes + 1, :] = base_ref[...]
    out_ref[modes + 1 : modes + 1 + seg_count, :] = perturb_ref[...]
    rest = out_ref.shape[0] - (modes + 1 + seg_count)
    if rest:
        out_ref[modes + 1 + seg_count :, :] = jnp.zeros((rest, out_ref.shape[1]), jnp.float32)


def iterate_body(n_alt, chunk, seg_count, modes, width, scale_ref, *refs):
    blocks, image_refs = refs[:n_alt], refs[n_alt : n_alt + chunk]
    coef_ref, basis_ref, split_ref, gram_ref, inv_ref = refs[n_alt + chunk :]
    place = lax.axis_index("alt")
    flat = place * chunk
    freq = flat // seg_count
    first = flat - freq * seg_count
    total = n_alt * width
    for k, block in enumerate(blocks):
        source = place ^ k
        span = pl.ds(pl.multiple_of(source * width, width), width)
        start = block[0:modes, :] * (1.0 / float(total) ** 0.5)
        for i in range(chunk):
            basis_ref[i, :, span] = start
            change = block[pl.ds(modes + 1 + first + i, 1), :]
            coef_ref[i : i + 1, span] = (2.0 * scale_ref[freq]) * (
                block[modes : modes + 1, :] * (1.0 + relief * change)
            )
    split_ref[...] = jnp.zeros_like(split_ref)
    left = lax.broadcasted_iota(jnp.int32, (8, 128), 1) < 64

    def packed_row(i, at):
        return at // HALF * 128 + i * 64 + at % HALF

    def step(_, carry):
        for i in range(chunk):
            coef = coef_ref[i : i + 1, :]
            for at in range(0, modes, 16):
                image = doubled_operator(basis_ref[i, at : at + 16, :], coef)
                row = packed_row(i, at)
                for part in range(3):
                    piece = image.astype(jnp.bfloat16)
                    split_ref[part, row : row + 16, :] = piece
                    image = image - piece.astype(jnp.float32)
        gram_ref[...] = short_mmt(split_ref[0], split_ref[0]) * DOWN
        work = []
        for at in range(0, modes, 8):
            one, two = packed_row(0, at), packed_row(1, at)
            work.append(
                [
                    jnp.where(
                        left,
                        gram_ref[one : one + 8, side : side + 128],
                        gram_ref[two : two + 8, side : side + 128],
                    )
                    for side in (0, 128)
                ]
            )
        rows = inverse_factors(work)
        for at in range(0, modes, 16):
            for half in range(2):
                part = jnp.concatenate([rows[at // 8][half], rows[at // 8 + 1][half]], axis=0)
                part = part * DOWN**0.5
                here = lax.broadcasted_iota(jnp.int32, part.shape, 1) < 64
                span = slice(half * 128, half * 128 + 128)
                inv_ref[0, at : at + 16, span] = jnp.where(here, part, 0.0).astype(jnp.bfloat16)
                inv_ref[1, at : at + 16, span] = jnp.where(here, 0.0, part).astype(jnp.bfloat16)
        for i in range(chunk):
            for at in range(0, total, 256):
                basis_ref[i, :, at : at + 256] = sum(
                    short_mm(inv_ref[i], split_ref[part, :, at : at + 256]) for part in range(3)
                )
        return carry

    lax.fori_loop(0, ITERS - 1, step, 0)
    for i in range(chunk):
        for at in range(0, modes, 8):
            image_refs[i][at : at + 8, :] = doubled_operator(
                basis_ref[i, at : at + 8, :], coef_ref[i : i + 1, :]
            )


def unit_of(modes):
    rows = lax.broadcasted_iota(jnp.int32, (modes, modes), 0)
    return jnp.where(rows == lax.broadcasted_iota(jnp.int32, (modes, modes), 1), 1.0, 0.0)


def complex_mm(left, right):
    return (
        mm(left[0], right[0]) - mm(left[1], right[1]),
        mm(left[0], right[1]) + mm(left[1], right[0]),
    )


def finish_body(halves, modes, total, coef_ref, *refs):
    image_refs, basis_refs = refs[0:2], refs[2:4]
    turn_ref, inner_ref, rest_ref, gram_ref, double_ref = refs[4:]
    unit = unit_of(modes)
    gram_ref[...] = jnp.zeros_like(gram_ref)
    for i in range(2):
        image = image_refs[i][...]
        gram_ref[i, :, 0:modes] = mmt(image, image) * DOWN
    grams = [gram_ref[i, at : at + 8, :] for at in range(0, modes, 8) for i in range(2)]
    rows = inverse_factors([pack_pair(*grams[i : i + 2]) for i in range(0, len(grams), 2)])
    for k, pair in enumerate(rows):
        for i, part in enumerate(unpack_pair(*pair)):
            gram_ref[i, 8 * k : 8 * k + 8, :] = part * DOWN**0.5
    turns = []
    for i in range(2):
        inv = gram_ref[i, :, 0:modes]
        for at in range(0, total, 256):
            basis_refs[i][:, at : at + 256] = mm(inv, image_refs[i][:, at : at + 256])
    for i, ref in enumerate(basis_refs):
        for at in range(0, modes, 8):
            double_ref[at : at + 8, :] = doubled_operator(
                ref[at : at + 8, :], coef_ref[i : i + 1, :]
            )
        phase = (0.5 * phase_step) * mmt(ref[...], double_ref[...])
        square = mm(phase, phase)
        turns.append(
            (unit - 0.5 * square + mm(square, square) / 24.0, phase - mm(phase, square) / 6.0)
        )
    corr = mmt(basis_refs[1][...], basis_refs[0][...])
    inner = (mm(corr, turns[0][0]), mm(corr, turns[0][1]))
    turn = jnp.where(chain_place(halves) == 0, unit, gram_ref[0, :, 0:modes])
    turn_ref[...] = turn
    late = (mm(turns[1][0], corr), mm(turns[1][1], corr))
    rest = complex_mm(late, (mm(turns[0][0], turn), mm(turns[0][1], turn)))
    for part in range(2):
        inner_ref[part] = inner[part]
        rest_ref[part] = rest[part]


def chain_place(halves):
    return lax.axis_index("range") * halves + lax.rem(lax.axis_index("alt"), halves)


def product_body(next_ref, second_ref, rest_ref, out_ref):
    corr = mmt(next_ref[...], second_ref[...])
    for part in range(2):
        out_ref[part] = mm(corr, rest_ref[part])


def group_body(halves, group, *refs):
    at = lax.rem(chain_place(halves), group)
    sorted_ref, out_ref = refs[group:]
    for k, ref in enumerate(refs[:group]):
        sorted_ref[lax.rem(at + group - k, group)] = ref[...]
    spans = [(sorted_ref[j, 0], sorted_ref[j, 1]) for j in reversed(range(group))]
    out_ref[0], out_ref[1] = fold(spans)


def fold(spans):
    while len(spans) > 1:
        pairs = [complex_mm(*spans[i : i + 2]) for i in range(0, len(spans) - 1, 2)]
        spans = pairs + spans[len(pairs) * 2 :]
    return spans[0]


def inside_body(halves, group, sorted_ref, turn_ref, inner_ref, out_ref):
    at = lax.rem(chain_place(halves), group)
    unit = unit_of(inner_ref.shape[1])
    spans = []
    for j in reversed(range(group - 1)):
        real = jnp.where(j < at, sorted_ref[j, 0], unit)
        spans.append((real, jnp.where(j < at, sorted_ref[j, 1], 0.0)))
    reached = fold(spans)
    reached = (mm(turn_ref[...], reached[0]), mm(turn_ref[...], reached[1]))
    following = complex_mm((inner_ref[0], inner_ref[1]), reached)
    for part in range(2):
        out_ref[0, part] = reached[part]
        out_ref[1, part] = following[part]


def join_body(halves, group, backs, *refs):
    at = chain_place(halves) // group
    spans = []
    for back, ref in zip(backs, refs):
        missing = jnp.where(at < back, unit_of(ref.shape[1]), 0.0)
        spans.append((ref[0] + missing, ref[1]) if back else (ref[0], ref[1]))
    refs[-1][0], refs[-1][1] = fold(spans)


def turn_vector(matrix, vector):
    rows = lax.broadcasted_iota(jnp.int32, vector.shape, 0)
    swapped = jnp.where(
        rows == 0, -row_of(vector, 1), jnp.where(rows == 1, row_of(vector, 0), 0.0)
    )
    return mmt(vector, matrix[0]) + mmt(swapped, matrix[1])


def field_body(halves, group, backs, n_alt, width, scale, source_ref, *refs):
    count = len(backs)
    inside_ref, first_ref, second_ref = refs[count : count + 3]
    place = lax.axis_index("alt")
    amp = source_ref[place // halves]
    for back, ref in reversed(list(zip(backs, refs))):
        moved = turn_vector((ref[0], ref[1]), amp)
        amp = jnp.where(chain_place(halves) // group < back, amp, moved)
    amps = [turn_vector((inside_ref[i, 0], inside_ref[i, 1]), amp) for i in range(2)]
    for k, out_ref in enumerate(refs[count + 3 :]):
        target = lax.rem(place + k, n_alt)
        span = pl.ds(pl.multiple_of(target * width, width), width)
        for i, ref in enumerate((first_ref, second_ref)):
            out_ref[i] = scale * mm(amps[i], ref[:, span])[0:2, :]


def settle_body(halves, n_alt, *refs):
    place = lax.axis_index("alt")
    out_ref = refs[n_alt]
    for k, part_ref in enumerate(refs[:n_alt]):
        source = lax.rem(place + n_alt - k, n_alt)
        chunk = part_ref.shape[0]
        freq, half = source // halves, lax.rem(source, halves)
        for i in range(chunk):
            out_ref[freq, half * chunk + i] = part_ref[i]


def local(freq_scale, base_profile, perturb, start_block, source):
    freqs = freq_scale.shape[0]
    seg_count = perturb.shape[0]
    modes, width = start_block.shape
    n_alt = lax.axis_size("alt")
    n_range = lax.axis_size("range")
    total = width * n_alt
    chunk = freqs * seg_count // n_alt
    halves = seg_count // chunk
    length = n_range * halves
    assert n_alt & (n_alt - 1) == 0 and modes == 2 * HALF and chunk == 2 and halves * chunk == seg_count and halves * freqs == n_alt

    def device(freq, at):
        return at // halves * n_alt + freq * halves + at % halves

    def along_chain(value, steps):
        pairs = []
        for freq in range(freqs):
            for at in range(max(0, -steps), min(length, length - steps)):
                pairs.append((device(freq, at), device(freq, at + steps)))
        return lax.ppermute(value, ("range", "alt"), pairs)

    def around(value, k):
        return lax.ppermute(value, "alt", [(i, (i + k) % n_alt) for i in range(n_alt)])

    mine = kernel_call(
        functools.partial(pack_body, modes, seg_count),
        shape(-(-(modes + 1 + seg_count) // 8) * 8, width),
        [start_block, base_profile[None, :], perturb],
        [VM] * 3,
    )
    found, bit = {0: mine}, n_alt
    while bit > 1:
        bit //= 2
        pairs = [(i, i ^ bit) for i in range(n_alt)]
        for key in list(found):
            found[key ^ bit] = lax.ppermute(found[key], "alt", pairs)
    blocks = [found[k] for k in range(n_alt)]
    flops = 2 * modes * modes * total
    image, other, coef = kernel_call(
        functools.partial(iterate_body, n_alt, chunk, seg_count, modes, width),
        [shape(modes, total)] * chunk + [shape(chunk, total)],
        [freq_scale] + blocks,
        [SM] + [VM] * n_alt,
        [
            pltpu.VMEM((chunk, modes, total), jnp.float32),
            pltpu.VMEM((3, 256, total), jnp.bfloat16),
            pltpu.VMEM((256, 256), jnp.float32),
            pltpu.VMEM((chunk, modes, 256), jnp.bfloat16),
        ],
        flops=2 * ITERS * chunk * flops,
    )
    following = along_chain(image, -1)
    first, second, turn, inner, rest = kernel_call(
        functools.partial(finish_body, halves, modes, total),
        [shape(modes, total)] * 2 + [shape(modes, modes)] + [shape(2, modes, modes)] * 2,
        [coef, image, other],
        [VM] * 3,
        [pltpu.VMEM((2, modes, 128), jnp.float32), pltpu.VMEM((modes, total), jnp.float32)],
        flops=16 * flops,
    )
    product = kernel_call(
        product_body, shape(2, modes, modes), [following, second, rest], [VM] * 3, flops=flops
    )

    group = 4
    groups = length // group
    assert groups * group == length

    def turned(value, size, k):
        pairs = []
        for freq in range(freqs):
            for at in range(length):
                goal = at // size * size + (at + k) % size
                pairs.append((device(freq, at), device(freq, goal)))
        return lax.ppermute(value, ("range", "alt"), pairs)

    ordered, span = kernel_call(
        functools.partial(group_body, halves, group),
        [shape(group, 2, modes, modes), shape(2, modes, modes)],
        [product] + [turned(product, group, k) for k in range(1, group)],
        [VM] * group,
        flops=flops,
    )

    def join(spans, backs):
        return kernel_call(
            functools.partial(join_body, halves, group, backs),
            shape(2, modes, modes),
            spans,
            [VM] * len(spans),
            flops=flops,
        )

    def from_back(backs):
        return [along_chain(span, group * back) if back else span for back in backs]

    if groups <= 4:
        backs = range(1, groups)
        came = [turned(span, length, group * back) for back in backs]
    else:
        backs = range(1, 5)
        span = join(from_back(backs), backs)
        reach = 4
        while groups > 4 * reach:
            backs = range(0, 4 * reach, reach)
            span = join(from_back(backs), backs)
            reach *= 4
        backs = range(0, groups, reach)
        came = from_back(backs)
    inside = kernel_call(
        functools.partial(inside_body, halves, group),
        shape(2, 2, modes, modes),
        [ordered, turn, inner],
        [VM] * 3,
        flops=flops,
    )
    rows = jnp.concatenate([source, jnp.zeros((freqs, 6, modes), jnp.float32)], axis=1)
    parts = kernel_call(
        functools.partial(
            field_body, halves, group, backs, n_alt, width, (float(total) / float(modes)) ** 0.5
        ),
        [shape(chunk, 2, width)] * n_alt,
        [rows] + came + [inside, first, second],
        [VM] * (4 + len(came)),
    )
    parts = [parts[0]] + [around(parts[k], k) for k in range(1, n_alt)]
    return kernel_call(
        functools.partial(settle_body, halves, n_alt),
        shape(freqs, seg_count, 2, width),
        parts,
        [VM] * n_alt,
    )


def solution(mesh):
    in_specs = (P("freq"), P("alt"), P("range", "alt"), P(None, "alt"), P("freq", None, None))
    out_specs = P("freq", "range", None, "alt")
    return jax.shard_map(local, mesh=mesh, in_specs=in_specs, out_specs=out_specs, check_vma=False)
```

```python
import functools

import jax
import jax.numpy as jnp
from jax import lax
from jax.experimental import pallas as pl
from jax.experimental.pallas import tpu as pltpu
from jax.sharding import PartitionSpec as P

ITERS = 8

phase_step = 0.15
relief = 0.1
HIGHEST = lax.Precision.HIGHEST
VMEM_LIMIT = 48 * 2**20
HALF = 48


def mm(left, right):
    return lax.dot_general(
        left, right, (((1,), (0,)), ((), ())), precision=HIGHEST, preferred_element_type=jnp.float32
    )


def mmt(left, right):
    return lax.dot_general(
        left, right, (((1,), (1,)), ((), ())), precision=HIGHEST, preferred_element_type=jnp.float32
    )


def short_mm(left, right):
    return lax.dot_general(
        left, right, (((1,), (0,)), ((), ())), preferred_element_type=jnp.float32
    )


def short_mmt(left, right):
    return lax.dot_general(
        left, right, (((1,), (1,)), ((), ())), preferred_element_type=jnp.float32
    )


def kernel_call(body, out_shape, args, specs, scratch=(), flops=0):
    nbytes = sum(4 * a.size for a in args) + sum(4 * o.size for o in jax.tree.leaves(out_shape))
    return pl.pallas_call(
        body,
        out_shape=out_shape,
        in_specs=specs,
        out_specs=jax.tree.map(lambda _: pl.BlockSpec(memory_space=pltpu.VMEM), out_shape),
        scratch_shapes=scratch,
        cost_estimate=pl.CostEstimate(flops=flops, bytes_accessed=nbytes, transcendentals=0),
        compiler_params=pltpu.CompilerParams(vmem_limit_bytes=VMEM_LIMIT),
    )(*args)


VM = pl.BlockSpec(memory_space=pltpu.VMEM)
SM = pl.BlockSpec(memory_space=pltpu.SMEM)


def shape(*dims):
    return jax.ShapeDtypeStruct(dims, jnp.float32)


def row_of(value, at):
    return jnp.broadcast_to(value[at : at + 1, :], value.shape)


def pack_pair(one, two):
    left = lax.broadcasted_iota(jnp.int32, one.shape, 1) < 64
    return [
        jnp.where(left, one, pltpu.roll(two, 64, 1)),
        jnp.where(left, pltpu.roll(one, 128 - HALF, 1), pltpu.roll(two, 64 - HALF, 1)),
    ]


def unpack_pair(low, high):
    early = lax.broadcasted_iota(jnp.int32, low.shape, 1) < HALF
    return (
        jnp.where(early, low, pltpu.roll(high, HALF, 1)),
        jnp.where(early, pltpu.roll(low, 64, 1), pltpu.roll(high, 64 + HALF, 1)),
    )


def inverse_factors(work):
    work = [list(pair) for pair in work]
    count = len(work)
    lanes = lax.broadcasted_iota(jnp.int32, (8, 128), 1)
    subs = lax.broadcasted_iota(jnp.int32, (8, 128), 0)
    base = jnp.where(lanes < 64, 0, 64)
    column = lanes - base
    results = []

    def place(k):
        side = 8 * k // HALF
        return side, 8 * k - side * HALF

    def spread(v, k):
        side, first = place(k)
        return [
            jnp.take_along_axis(work[v][side], base + (first + c), axis=1) for c in range(8)
        ]

    panel = spread(0, 0)
    for k in range(count):
        side, first = place(k)
        near = spread(k + 1, k) if k + 1 < count else None
        ahead = spread(k + 1, k + 1) if k + 1 < count else None
        weights = [[None] * 8 for _ in range(8)]
        inverses, lines = [], []
        scales = jnp.ones((8, 128), jnp.float32)
        for c in range(0, 8, 2):
            corner, cross, late = (
                row_of(panel[c], c),
                row_of(panel[c + 1], c),
                row_of(panel[c + 1], c + 1),
            )
            inv = 1.0 / corner
            second = corner * (1.0 / (corner * late - cross * cross))
            ratio = cross * inv
            weights[c][c + 1] = cross
            factor = panel[c] * inv
            rest = panel[c + 1] - factor * cross
            for d in range(c + 2, 8):
                weights[c][d] = row_of(panel[d], c)
                weights[c + 1][d] = row_of(panel[d], c + 1) - ratio * weights[c][d]
                panel[d] = (panel[d] - factor * weights[c][d]) - (
                    rest * weights[c + 1][d]
                ) * second
            pair = (jnp.where(subs > c, factor, 0.0), jnp.where(subs > c + 1, rest * second, 0.0))
            for e in range(2):
                inverses.append((inv, second)[e])
                scales = jnp.where(subs == c + e, inverses[-1], scales)
                line = [row_of(part, c + e) for part in work[k]]
                line[side] = line[side] + jnp.where(column == first + c + e, 1.0, 0.0)
                lines.append(line)
                work[k] = [part - pair[e] * along for part, along in zip(work[k], line)]
        if near is not None:
            for c in range(8):
                factor = near[c] * inverses[c]
                for d in range(c + 1, 8):
                    near[d] = near[d] - factor * weights[c][d]
                for d in range(8):
                    ahead[d] = ahead[d] - factor * row_of(near[c], d)
                work[k + 1] = [
                    part - factor * along for part, along in zip(work[k + 1], lines[c])
                ]
        panel = ahead
        scaled = [[part * inv for part in line] for line, inv in zip(lines, inverses)]
        for v in range(k + 2, count):
            there, at = place(v)
            for c in range(8):
                factor = jnp.take_along_axis(scaled[c][there], base + subs + at, axis=1)
                work[v] = [part - factor * along for part, along in zip(work[v], lines[c])]
        root = lax.sqrt(scales)
        unit = jnp.where(column == subs + first, 1.0, 0.0)
        own = jnp.where(column < subs + first, work[k][side], unit) * root
        other = work[k][0] * root if side else jnp.zeros((8, 128), jnp.float32)
        results.append((other, own) if side else (own, other))
    return results


def doubled_operator(value, coef):
    width = value.shape[1]
    lanes = lax.broadcasted_iota(jnp.int32, (value.shape[0], 128), 1)
    below, above = pltpu.roll(value, 1, 1), pltpu.roll(value, width - 1, 1)
    below = jnp.concatenate(
        [jnp.where(lanes == 0, 0.0, below[:, :128]), below[:, 128:]], axis=1
    )
    above = jnp.concatenate(
        [above[:, :-128], jnp.where(lanes == 127, 0.0, above[:, -128:])], axis=1
    )
    return coef * value + (below + above)


DOWN = 2.0**-13


def pack_body(modes, start_ref, base_ref, perturb_ref, out_ref, base_buf, perturb_buf, sems):
    copies = [
        pltpu.make_async_copy(source, target, sems.at[i])
        for i, (source, target) in enumerate(
            (
                (start_ref, out_ref.at[0:modes]),
                (base_ref, base_buf),
                (perturb_ref, perturb_buf),
            )
        )
    ]
    for copy in copies:
        copy.start()
    copies[1].wait()
    copies[2].wait()
    seg_count = perturb_ref.shape[0]
    rest = out_ref.shape[0] - modes - 1 - seg_count
    lines = [base_buf[...], perturb_buf[...]]
    if rest:
        lines.append(jnp.zeros((rest, out_ref.shape[1]), jnp.float32))
    out_ref[modes:, :] = jnp.concatenate(lines, axis=0)
    copies[0].wait()


def iterate_body(n_alt, chunk, seg_count, modes, width, scale_ref, *refs):
    blocks, image_refs = refs[:n_alt], refs[n_alt : n_alt + chunk]
    coef_ref, basis_ref, split_ref, gram_ref, inv_ref = refs[n_alt + chunk :]
    place = lax.axis_index("alt")
    flat = place * chunk
    freq = flat // seg_count
    first = flat - freq * seg_count
    total = n_alt * width
    for k, block in enumerate(blocks):
        source = place ^ k
        span = pl.ds(pl.multiple_of(source * width, width), width)
        start = block[0:modes, :] * (1.0 / float(total) ** 0.5)
        for i in range(chunk):
            basis_ref[i, :, span] = start
            change = block[pl.ds(modes + 1 + first + i, 1), :]
            coef_ref[i : i + 1, span] = (2.0 * scale_ref[freq]) * (
                block[modes : modes + 1, :] * (1.0 + relief * change)
            )
    split_ref[...] = jnp.zeros_like(split_ref)
    left = lax.broadcasted_iota(jnp.int32, (8, 128), 1) < 64

    def packed_row(i, at):
        return at // HALF * 128 + i * 64 + at % HALF

    def step(_, carry):
        for i in range(chunk):
            coef = coef_ref[i : i + 1, :]
            for at in range(0, modes, 16):
                image = doubled_operator(basis_ref[i, at : at + 16, :], coef)
                row = packed_row(i, at)
                for part in range(3):
                    piece = image.astype(jnp.bfloat16)
                    split_ref[part, row : row + 16, :] = piece
                    image = image - piece.astype(jnp.float32)
        gram_ref[...] = short_mmt(split_ref[0], split_ref[0]) * DOWN
        work = []
        for at in range(0, modes, 8):
            one, two = packed_row(0, at), packed_row(1, at)
            work.append(
                [
                    jnp.where(
                        left,
                        gram_ref[one : one + 8, side : side + 128],
                        gram_ref[two : two + 8, side : side + 128],
                    )
                    for side in (0, 128)
                ]
            )
        rows = inverse_factors(work)
        for at in range(0, modes, 16):
            for half in range(2):
                part = jnp.concatenate([rows[at // 8][half], rows[at // 8 + 1][half]], axis=0)
                part = part * DOWN**0.5
                here = lax.broadcasted_iota(jnp.int32, part.shape, 1) < 64
                span = slice(half * 128, half * 128 + 128)
                inv_ref[0, at : at + 16, span] = jnp.where(here, part, 0.0).astype(jnp.bfloat16)
                inv_ref[1, at : at + 16, span] = jnp.where(here, 0.0, part).astype(jnp.bfloat16)
        for i in range(chunk):
            for at in range(0, total, 256):
                basis_ref[i, :, at : at + 256] = sum(
                    short_mm(inv_ref[i], split_ref[part, :, at : at + 256]) for part in range(3)
                )
        return carry

    lax.fori_loop(0, ITERS - 1, step, 0)
    for i in range(chunk):
        for at in range(0, modes, 8):
            image_refs[i][at : at + 8, :] = doubled_operator(
                basis_ref[i, at : at + 8, :], coef_ref[i : i + 1, :]
            )


def unit_of(modes):
    rows = lax.broadcasted_iota(jnp.int32, (modes, modes), 0)
    return jnp.where(rows == lax.broadcasted_iota(jnp.int32, (modes, modes), 1), 1.0, 0.0)


def complex_mm(left, right):
    return (
        mm(left[0], right[0]) - mm(left[1], right[1]),
        mm(left[0], right[1]) + mm(left[1], right[0]),
    )


def finish_body(halves, modes, total, coef_ref, *refs):
    image_refs, basis_refs = refs[0:2], refs[2:4]
    turn_ref, inner_ref, rest_ref, gram_ref, double_ref = refs[4:]
    unit = unit_of(modes)
    gram_ref[...] = jnp.zeros_like(gram_ref)
    for i in range(2):
        image = image_refs[i][...]
        gram_ref[i, :, 0:modes] = mmt(image, image) * DOWN
    grams = [gram_ref[i, at : at + 8, :] for at in range(0, modes, 8) for i in range(2)]
    rows = inverse_factors([pack_pair(*grams[i : i + 2]) for i in range(0, len(grams), 2)])
    for k, pair in enumerate(rows):
        for i, part in enumerate(unpack_pair(*pair)):
            gram_ref[i, 8 * k : 8 * k + 8, :] = part * DOWN**0.5
    turns = []
    for i in range(2):
        inv = gram_ref[i, :, 0:modes]
        for at in range(0, total, 256):
            basis_refs[i][:, at : at + 256] = mm(inv, image_refs[i][:, at : at + 256])
    for i, ref in enumerate(basis_refs):
        for at in range(0, modes, 8):
            double_ref[at : at + 8, :] = doubled_operator(
                ref[at : at + 8, :], coef_ref[i : i + 1, :]
            )
        phase = (0.5 * phase_step) * mmt(ref[...], double_ref[...])
        square = mm(phase, phase)
        turns.append(
            (unit - 0.5 * square + mm(square, square) / 24.0, phase - mm(phase, square) / 6.0)
        )
    corr = mmt(basis_refs[1][...], basis_refs[0][...])
    inner = (mm(corr, turns[0][0]), mm(corr, turns[0][1]))
    turn = jnp.where(chain_place(halves) == 0, unit, gram_ref[0, :, 0:modes])
    turn_ref[...] = turn
    late = (mm(turns[1][0], corr), mm(turns[1][1], corr))
    rest = complex_mm(late, (mm(turns[0][0], turn), mm(turns[0][1], turn)))
    for part in range(2):
        inner_ref[part] = inner[part]
        rest_ref[part] = rest[part]


def chain_place(halves):
    return lax.axis_index("range") * halves + lax.rem(lax.axis_index("alt"), halves)


def product_body(next_ref, second_ref, rest_ref, out_ref):
    corr = mmt(next_ref[...], second_ref[...])
    for part in range(2):
        out_ref[part] = mm(corr, rest_ref[part])


def group_body(halves, group, *refs):
    at = lax.rem(chain_place(halves), group)
    sorted_ref, out_ref = refs[group:]
    for k, ref in enumerate(refs[:group]):
        sorted_ref[lax.rem(at + group - k, group)] = ref[...]
    spans = [(sorted_ref[j, 0], sorted_ref[j, 1]) for j in reversed(range(group))]
    out_ref[0], out_ref[1] = fold(spans)


def fold(spans):
    while len(spans) > 1:
        pairs = [complex_mm(*spans[i : i + 2]) for i in range(0, len(spans) - 1, 2)]
        spans = pairs + spans[len(pairs) * 2 :]
    return spans[0]


def inside_body(halves, group, sorted_ref, turn_ref, inner_ref, out_ref):
    at = lax.rem(chain_place(halves), group)
    unit = unit_of(inner_ref.shape[1])
    spans = []
    for j in reversed(range(group - 1)):
        real = jnp.where(j < at, sorted_ref[j, 0], unit)
        spans.append((real, jnp.where(j < at, sorted_ref[j, 1], 0.0)))
    reached = fold(spans)
    reached = (mm(turn_ref[...], reached[0]), mm(turn_ref[...], reached[1]))
    following = complex_mm((inner_ref[0], inner_ref[1]), reached)
    for part in range(2):
        out_ref[0, part] = reached[part]
        out_ref[1, part] = following[part]


def join_body(halves, group, backs, *refs):
    at = chain_place(halves) // group
    spans = []
    for back, ref in zip(backs, refs):
        missing = jnp.where(at < back, unit_of(ref.shape[1]), 0.0)
        spans.append((ref[0] + missing, ref[1]) if back else (ref[0], ref[1]))
    refs[-1][0], refs[-1][1] = fold(spans)


def group_span(halves, group, back, ref):
    there = chain_place(halves) // group >= back
    return jnp.where(there, ref[0], unit_of(ref.shape[1])), jnp.where(there, ref[1], 0.0)


def merge_body(halves, group, back, last, inside_ref, span_ref, out_ref):
    span = group_span(halves, group, back, span_ref)
    for i in range(2):
        merged = complex_mm((inside_ref[i, 0], inside_ref[i, 1]), span)
        for part in range(2):
            out_ref[i, part] = merged[part].T if last else merged[part]


def field_body(halves, group, back, n_alt, width, scale, source_ref, *refs):
    span_ref, inside_ref, first_ref, second_ref = refs[:4]
    place = lax.axis_index("alt")
    source = source_ref[place // halves]
    real, imag = source[0:1, :], source[1:2, :]
    left, right = group_span(halves, group, back, span_ref)
    came = (
        jnp.sum(left * real - right * imag, axis=1, keepdims=True),
        jnp.sum(left * imag + right * real, axis=1, keepdims=True),
    )
    rows = lax.broadcasted_iota(jnp.int32, source.shape, 0)
    amps = []
    for i in range(2):
        left, right = inside_ref[i, 0], inside_ref[i, 1]
        amp = (
            jnp.sum(left * came[0] - right * came[1], axis=0, keepdims=True),
            jnp.sum(left * came[1] + right * came[0], axis=0, keepdims=True),
        )
        amps.append(jnp.where(rows == 0, amp[0], jnp.where(rows == 1, amp[1], 0.0)))
    for k, out_ref in enumerate(refs[4:]):
        target = lax.rem(place + k, n_alt)
        span = pl.ds(pl.multiple_of(target * width, width), width)
        for i, ref in enumerate((first_ref, second_ref)):
            out_ref[i] = scale * mm(amps[i], ref[:, span])[0:2, :]


def settle_body(halves, n_alt, *refs):
    place = lax.axis_index("alt")
    out_ref = refs[n_alt]
    for k, part_ref in enumerate(refs[:n_alt]):
        source = lax.rem(place + n_alt - k, n_alt)
        chunk = part_ref.shape[0]
        freq, half = source // halves, lax.rem(source, halves)
        for i in range(chunk):
            out_ref[freq, half * chunk + i] = part_ref[i]


def local(freq_scale, base_profile, perturb, start_block, source):
    freqs = freq_scale.shape[0]
    seg_count = perturb.shape[0]
    modes, width = start_block.shape
    n_alt = lax.axis_size("alt")
    n_range = lax.axis_size("range")
    total = width * n_alt
    chunk = freqs * seg_count // n_alt
    halves = seg_count // chunk
    length = n_range * halves
    assert n_alt & (n_alt - 1) == 0 and modes == 2 * HALF
    assert chunk == 2 and halves * chunk == seg_count and halves * freqs == n_alt

    def device(freq, at):
        return at // halves * n_alt + freq * halves + at % halves

    def along_chain(value, steps):
        pairs = []
        for freq in range(freqs):
            for at in range(max(0, -steps), min(length, length - steps)):
                pairs.append((device(freq, at), device(freq, at + steps)))
        return lax.ppermute(value, ("range", "alt"), pairs)

    def around(value, k):
        return lax.ppermute(value, "alt", [(i, (i + k) % n_alt) for i in range(n_alt)])

    mine = kernel_call(
        functools.partial(pack_body, modes),
        shape(-(-(modes + 1 + seg_count) // 8) * 8, width),
        [start_block, base_profile[None, :], perturb],
        [pl.BlockSpec(memory_space=pl.ANY)] * 3,
        [
            pltpu.VMEM((1, width), jnp.float32),
            pltpu.VMEM((seg_count, width), jnp.float32),
            pltpu.SemaphoreType.DMA((3,)),
        ],
    )
    found, bit = {0: mine}, n_alt
    while bit > 1:
        bit //= 2
        pairs = [(i, i ^ bit) for i in range(n_alt)]
        for key in list(found):
            found[key ^ bit] = lax.ppermute(found[key], "alt", pairs)
    blocks = [found[k] for k in range(n_alt)]
    flops = 2 * modes * modes * total
    image, other, coef = kernel_call(
        functools.partial(iterate_body, n_alt, chunk, seg_count, modes, width),
        [shape(modes, total)] * chunk + [shape(chunk, total)],
        [freq_scale] + blocks,
        [SM] + [VM] * n_alt,
        [
            pltpu.VMEM((chunk, modes, total), jnp.float32),
            pltpu.VMEM((3, 256, total), jnp.bfloat16),
            pltpu.VMEM((256, 256), jnp.float32),
            pltpu.VMEM((chunk, modes, 256), jnp.bfloat16),
        ],
        flops=2 * ITERS * chunk * flops,
    )
    following = along_chain(image, -1)
    first, second, turn, inner, rest = kernel_call(
        functools.partial(finish_body, halves, modes, total),
        [shape(modes, total)] * 2 + [shape(modes, modes)] + [shape(2, modes, modes)] * 2,
        [coef, image, other],
        [VM] * 3,
        [pltpu.VMEM((2, modes, 128), jnp.float32), pltpu.VMEM((modes, total), jnp.float32)],
        flops=16 * flops,
    )
    product = kernel_call(
        product_body, shape(2, modes, modes), [following, second, rest], [VM] * 3, flops=flops
    )

    group = 4
    groups = length // group
    assert groups * group == length and groups > 2

    def turned(value, size, k):
        pairs = []
        for freq in range(freqs):
            for at in range(length):
                goal = at // size * size + (at + k) % size
                pairs.append((device(freq, at), device(freq, goal)))
        return lax.ppermute(value, ("range", "alt"), pairs)

    ordered, span = kernel_call(
        functools.partial(group_body, halves, group),
        [shape(group, 2, modes, modes), shape(2, modes, modes)],
        [product] + [turned(product, group, k) for k in range(1, group)],
        [VM] * group,
        flops=flops,
    )

    def join(spans, backs):
        return kernel_call(
            functools.partial(join_body, halves, group, backs),
            shape(2, modes, modes),
            spans,
            [VM] * len(spans),
            flops=flops,
        )

    def from_back(backs):
        return [along_chain(span, group * back) if back else span for back in backs]

    if groups <= 4:
        backs = range(1, groups)
        came = [turned(span, length, group * back) for back in backs]
    else:
        backs = range(1, 5)
        span = join(from_back(backs), backs)
        reach = 4
        while groups > 4 * reach:
            backs = range(0, 4 * reach, reach)
            span = join(from_back(backs), backs)
            reach *= 4
        backs = range(0, groups, reach)
        came = from_back(backs)
    inside = kernel_call(
        functools.partial(inside_body, halves, group),
        shape(2, 2, modes, modes),
        [ordered, turn, inner],
        [VM] * 3,
        flops=flops,
    )
    rows = jnp.concatenate([source, jnp.zeros((freqs, 6, modes), jnp.float32)], axis=1)
    for at, back in enumerate(backs[:-1]):
        inside = kernel_call(
            functools.partial(merge_body, halves, group, back, at == len(backs) - 2),
            shape(2, 2, modes, modes),
            [inside, came[at]],
            [VM] * 2,
            flops=flops,
        )
    parts = kernel_call(
        functools.partial(
            field_body,
            halves,
            group,
            backs[-1],
            n_alt,
            width,
            (float(total) / float(modes)) ** 0.5,
        ),
        [shape(chunk, 2, width)] * n_alt,
        [rows, came[-1], inside, first, second],
        [VM] * 5,
    )
    parts = [parts[0]] + [around(parts[k], k) for k in range(1, n_alt)]
    return kernel_call(
        functools.partial(settle_body, halves, n_alt),
        shape(freqs, seg_count, 2, width),
        parts,
        [VM] * n_alt,
    )


def solution(mesh):
    in_specs = (P("freq"), P("alt"), P("range", "alt"), P(None, "alt"), P("freq", None, None))
    out_specs = P("freq", "range", None, "alt")
    return jax.shard_map(local, mesh=mesh, in_specs=in_specs, out_specs=out_specs, check_vma=False)
```

```python
import functools

import jax
import jax.numpy as jnp
from jax import lax
from jax.experimental import pallas as pl
from jax.experimental.pallas import tpu as pltpu
from jax.sharding import PartitionSpec as P

ITERS = 8

phase_step = 0.15
relief = 0.1
HIGHEST = lax.Precision.HIGHEST
VMEM_LIMIT = 48 * 2**20
HALF = 48


def mm(left, right):
    return lax.dot_general(
        left, right, (((1,), (0,)), ((), ())), precision=HIGHEST, preferred_element_type=jnp.float32
    )


def mmt(left, right):
    return lax.dot_general(
        left, right, (((1,), (1,)), ((), ())), precision=HIGHEST, preferred_element_type=jnp.float32
    )


def short_mm(left, right):
    return lax.dot_general(
        left, right, (((1,), (0,)), ((), ())), preferred_element_type=jnp.float32
    )


def short_mmt(left, right):
    return lax.dot_general(
        left, right, (((1,), (1,)), ((), ())), preferred_element_type=jnp.float32
    )


def kernel_call(body, out_shape, args, specs, scratch=(), flops=0):
    nbytes = sum(4 * a.size for a in args) + sum(4 * o.size for o in jax.tree.leaves(out_shape))
    return pl.pallas_call(
        body,
        out_shape=out_shape,
        in_specs=specs,
        out_specs=jax.tree.map(lambda _: pl.BlockSpec(memory_space=pltpu.VMEM), out_shape),
        scratch_shapes=scratch,
        cost_estimate=pl.CostEstimate(flops=flops, bytes_accessed=nbytes, transcendentals=0),
        compiler_params=pltpu.CompilerParams(vmem_limit_bytes=VMEM_LIMIT),
    )(*args)


VM = pl.BlockSpec(memory_space=pltpu.VMEM)
SM = pl.BlockSpec(memory_space=pltpu.SMEM)


def shape(*dims):
    return jax.ShapeDtypeStruct(dims, jnp.float32)


def row_of(value, at):
    return jnp.broadcast_to(value[at : at + 1, :], value.shape)


def pack_pair(one, two):
    left = lax.broadcasted_iota(jnp.int32, one.shape, 1) < 64
    return [
        jnp.where(left, one, pltpu.roll(two, 64, 1)),
        jnp.where(left, pltpu.roll(one, 128 - HALF, 1), pltpu.roll(two, 64 - HALF, 1)),
    ]


def unpack_pair(low, high):
    early = lax.broadcasted_iota(jnp.int32, low.shape, 1) < HALF
    return (
        jnp.where(early, low, pltpu.roll(high, HALF, 1)),
        jnp.where(early, pltpu.roll(low, 64, 1), pltpu.roll(high, 64 + HALF, 1)),
    )


def inverse_factors(work):
    work = [list(pair) for pair in work]
    count = len(work)
    lanes = lax.broadcasted_iota(jnp.int32, (8, 128), 1)
    subs = lax.broadcasted_iota(jnp.int32, (8, 128), 0)
    base = jnp.where(lanes < 64, 0, 64)
    column = lanes - base
    results = []

    def place(k):
        side = 8 * k // HALF
        return side, 8 * k - side * HALF

    def spread(v, k):
        side, first = place(k)
        return [
            jnp.take_along_axis(work[v][side], base + (first + c), axis=1) for c in range(8)
        ]

    panel = spread(0, 0)
    for k in range(count):
        side, first = place(k)
        near = spread(k + 1, k) if k + 1 < count else None
        ahead = spread(k + 1, k + 1) if k + 1 < count else None
        weights = [[None] * 8 for _ in range(8)]
        inverses, lines = [], []
        scales = jnp.ones((8, 128), jnp.float32)
        for c in range(0, 8, 2):
            corner, cross, late = (
                row_of(panel[c], c),
                row_of(panel[c + 1], c),
                row_of(panel[c + 1], c + 1),
            )
            inv = 1.0 / corner
            second = corner * (1.0 / (corner * late - cross * cross))
            ratio = cross * inv
            weights[c][c + 1] = cross
            factor = panel[c] * inv
            rest = panel[c + 1] - factor * cross
            for d in range(c + 2, 8):
                weights[c][d] = row_of(panel[d], c)
                weights[c + 1][d] = row_of(panel[d], c + 1) - ratio * weights[c][d]
                panel[d] = (panel[d] - factor * weights[c][d]) - (
                    rest * weights[c + 1][d]
                ) * second
            pair = (jnp.where(subs > c, factor, 0.0), jnp.where(subs > c + 1, rest * second, 0.0))
            for e in range(2):
                inverses.append((inv, second)[e])
                scales = jnp.where(subs == c + e, inverses[-1], scales)
                line = [row_of(part, c + e) for part in work[k]]
                line[side] = line[side] + jnp.where(column == first + c + e, 1.0, 0.0)
                lines.append(line)
                work[k] = [part - pair[e] * along for part, along in zip(work[k], line)]
        if near is not None:
            for c in range(8):
                factor = near[c] * inverses[c]
                for d in range(c + 1, 8):
                    near[d] = near[d] - factor * weights[c][d]
                for d in range(8):
                    ahead[d] = ahead[d] - factor * row_of(near[c], d)
                work[k + 1] = [
                    part - factor * along for part, along in zip(work[k + 1], lines[c])
                ]
        panel = ahead
        scaled = [[part * inv for part in line] for line, inv in zip(lines, inverses)]
        for v in range(k + 2, count):
            there, at = place(v)
            for c in range(8):
                factor = jnp.take_along_axis(scaled[c][there], base + subs + at, axis=1)
                work[v] = [part - factor * along for part, along in zip(work[v], lines[c])]
        root = lax.sqrt(scales)
        unit = jnp.where(column == subs + first, 1.0, 0.0)
        own = jnp.where(column < subs + first, work[k][side], unit) * root
        other = work[k][0] * root if side else jnp.zeros((8, 128), jnp.float32)
        results.append((other, own) if side else (own, other))
    return results


def doubled_operator(value, coef):
    width = value.shape[1]
    lanes = lax.broadcasted_iota(jnp.int32, (value.shape[0], 128), 1)
    below, above = pltpu.roll(value, 1, 1), pltpu.roll(value, width - 1, 1)
    below = jnp.concatenate(
        [jnp.where(lanes == 0, 0.0, below[:, :128]), below[:, 128:]], axis=1
    )
    above = jnp.concatenate(
        [above[:, :-128], jnp.where(lanes == 127, 0.0, above[:, -128:])], axis=1
    )
    return coef * value + (below + above)


DOWN = 2.0**-13


def pack_body(modes, start_ref, base_ref, perturb_ref, out_ref, base_buf, perturb_buf, sems):
    copies = [
        pltpu.make_async_copy(source, target, sems.at[i])
        for i, (source, target) in enumerate(
            (
                (start_ref, out_ref.at[0:modes]),
                (base_ref, base_buf),
                (perturb_ref, perturb_buf),
            )
        )
    ]
    for copy in copies:
        copy.start()
    copies[1].wait()
    copies[2].wait()
    seg_count = perturb_ref.shape[0]
    rest = out_ref.shape[0] - modes - 1 - seg_count
    lines = [base_buf[...], perturb_buf[...]]
    if rest:
        lines.append(jnp.zeros((rest, out_ref.shape[1]), jnp.float32))
    out_ref[modes:, :] = jnp.concatenate(lines, axis=0)
    copies[0].wait()


def iterate_body(n_alt, chunk, seg_count, modes, width, scale_ref, *refs):
    blocks, image_refs = refs[:n_alt], refs[n_alt : n_alt + chunk]
    coef_ref, basis_ref, split_ref, gram_ref, inv_ref = refs[n_alt + chunk :]
    place = lax.axis_index("alt")
    flat = place * chunk
    freq = flat // seg_count
    first = flat - freq * seg_count
    total = n_alt * width
    for k, block in enumerate(blocks):
        source = place ^ k
        span = pl.ds(pl.multiple_of(source * width, width), width)
        start = block[0:modes, :] * (1.0 / float(total) ** 0.5)
        for i in range(chunk):
            basis_ref[i, :, span] = start
            change = block[pl.ds(modes + 1 + first + i, 1), :]
            coef_ref[i : i + 1, span] = (2.0 * scale_ref[freq]) * (
                block[modes : modes + 1, :] * (1.0 + relief * change)
            )
    split_ref[...] = jnp.zeros_like(split_ref)
    left = lax.broadcasted_iota(jnp.int32, (8, 128), 1) < 64

    def packed_row(i, at):
        return at // HALF * 128 + i * 64 + at % HALF

    def step(_, carry):
        for i in range(chunk):
            coef = coef_ref[i : i + 1, :]
            for at in range(0, modes, 16):
                image = doubled_operator(basis_ref[i, at : at + 16, :], coef)
                row = packed_row(i, at)
                for part in range(3):
                    piece = image.astype(jnp.bfloat16)
                    split_ref[part, row : row + 16, :] = piece
                    image = image - piece.astype(jnp.float32)
        gram_ref[...] = short_mmt(split_ref[0], split_ref[0]) * DOWN
        work = []
        for at in range(0, modes, 8):
            one, two = packed_row(0, at), packed_row(1, at)
            work.append(
                [
                    jnp.where(
                        left,
                        gram_ref[one : one + 8, side : side + 128],
                        gram_ref[two : two + 8, side : side + 128],
                    )
                    for side in (0, 128)
                ]
            )
        rows = inverse_factors(work)
        for at in range(0, modes, 16):
            for half in range(2):
                part = jnp.concatenate([rows[at // 8][half], rows[at // 8 + 1][half]], axis=0)
                part = part * DOWN**0.5
                here = lax.broadcasted_iota(jnp.int32, part.shape, 1) < 64
                span = slice(half * 128, half * 128 + 128)
                inv_ref[0, at : at + 16, span] = jnp.where(here, part, 0.0).astype(jnp.bfloat16)
                inv_ref[1, at : at + 16, span] = jnp.where(here, 0.0, part).astype(jnp.bfloat16)
        for i in range(chunk):
            for at in range(0, total, 256):
                basis_ref[i, :, at : at + 256] = sum(
                    short_mm(inv_ref[i], split_ref[part, :, at : at + 256]) for part in range(3)
                )
        return carry

    lax.fori_loop(0, ITERS - 1, step, 0)
    for i in range(chunk):
        for at in range(0, modes, 8):
            image_refs[i][at : at + 8, :] = doubled_operator(
                basis_ref[i, at : at + 8, :], coef_ref[i : i + 1, :]
            )


def unit_of(modes):
    rows = lax.broadcasted_iota(jnp.int32, (modes, modes), 0)
    return jnp.where(rows == lax.broadcasted_iota(jnp.int32, (modes, modes), 1), 1.0, 0.0)


def complex_mm(left, right):
    return (
        mm(left[0], right[0]) - mm(left[1], right[1]),
        mm(left[0], right[1]) + mm(left[1], right[0]),
    )


def finish_body(halves, modes, total, coef_ref, *refs):
    image_refs, basis_refs = refs[0:2], refs[2:4]
    turn_ref, inner_ref, rest_ref, gram_ref, double_ref = refs[4:]
    unit = unit_of(modes)
    gram_ref[...] = jnp.zeros_like(gram_ref)
    for i in range(2):
        image = image_refs[i][...]
        gram_ref[i, :, 0:modes] = mmt(image, image) * DOWN
    grams = [gram_ref[i, at : at + 8, :] for at in range(0, modes, 8) for i in range(2)]
    rows = inverse_factors([pack_pair(*grams[i : i + 2]) for i in range(0, len(grams), 2)])
    for k, pair in enumerate(rows):
        for i, part in enumerate(unpack_pair(*pair)):
            gram_ref[i, 8 * k : 8 * k + 8, :] = part * DOWN**0.5
    turns = []
    for i in range(2):
        inv = gram_ref[i, :, 0:modes]
        for at in range(0, total, 256):
            basis_refs[i][:, at : at + 256] = mm(inv, image_refs[i][:, at : at + 256])
    for i, ref in enumerate(basis_refs):
        for at in range(0, modes, 8):
            double_ref[at : at + 8, :] = doubled_operator(
                ref[at : at + 8, :], coef_ref[i : i + 1, :]
            )
        phase = (0.5 * phase_step) * mmt(ref[...], double_ref[...])
        square = mm(phase, phase)
        turns.append(
            (unit - 0.5 * square + mm(square, square) / 24.0, phase - mm(phase, square) / 6.0)
        )
    corr = mmt(basis_refs[1][...], basis_refs[0][...])
    inner = (mm(corr, turns[0][0]), mm(corr, turns[0][1]))
    turn = jnp.where(chain_place(halves) == 0, unit, gram_ref[0, :, 0:modes])
    turn_ref[...] = turn
    late = (mm(turns[1][0], corr), mm(turns[1][1], corr))
    rest = complex_mm(late, (mm(turns[0][0], turn), mm(turns[0][1], turn)))
    for part in range(2):
        inner_ref[part] = inner[part]
        rest_ref[part] = rest[part]


def chain_place(halves):
    return lax.axis_index("range") * halves + lax.rem(lax.axis_index("alt"), halves)


def product_body(next_ref, second_ref, rest_ref, out_ref):
    corr = mmt(next_ref[...], second_ref[...])
    for part in range(2):
        out_ref[part] = mm(corr, rest_ref[part])


def later_half(halves, bit):
    return lax.rem(chain_place(halves) // bit, 2) == 1


def pair_body(halves, bit, own_ref, other_ref, out_ref):
    later = later_half(halves, bit)
    own, other = (own_ref[0], own_ref[1]), (other_ref[0], other_ref[1])
    pairs = list(zip(own, other))
    out_ref[0], out_ref[1] = complex_mm(
        [jnp.where(later, a, b) for a, b in pairs], [jnp.where(later, b, a) for a, b in pairs]
    )


def fold(spans):
    while len(spans) > 1:
        pairs = [complex_mm(*spans[i : i + 2]) for i in range(0, len(spans) - 1, 2)]
        spans = pairs + spans[len(pairs) * 2 :]
    return spans[0]


def inside_body(halves, bits, *refs):
    turn_ref, inner_ref, out_ref = refs[len(bits) :]
    unit = unit_of(inner_ref.shape[1])
    spans = []
    for bit, ref in zip(bits, refs):
        later = later_half(halves, bit)
        spans.append((jnp.where(later, ref[0], unit), jnp.where(later, ref[1], 0.0)))
    reached = fold(spans)
    reached = (mm(turn_ref[...], reached[0]), mm(turn_ref[...], reached[1]))
    following = complex_mm((inner_ref[0], inner_ref[1]), reached)
    for part in range(2):
        out_ref[0, part] = reached[part]
        out_ref[1, part] = following[part]


def join_body(halves, group, backs, *refs):
    at = chain_place(halves) // group
    spans = []
    for back, ref in zip(backs, refs):
        missing = jnp.where(at < back, unit_of(ref.shape[1]), 0.0)
        spans.append((ref[0] + missing, ref[1]) if back else (ref[0], ref[1]))
    refs[-1][0], refs[-1][1] = fold(spans)


def group_span(halves, group, back, ref):
    there = chain_place(halves) // group >= back
    return jnp.where(there, ref[0], unit_of(ref.shape[1])), jnp.where(there, ref[1], 0.0)


def merge_body(halves, group, back, last, inside_ref, span_ref, out_ref):
    span = group_span(halves, group, back, span_ref)
    for i in range(2):
        merged = complex_mm((inside_ref[i, 0], inside_ref[i, 1]), span)
        for part in range(2):
            out_ref[i, part] = merged[part].T if last else merged[part]


def field_body(halves, group, back, n_alt, width, scale, source_ref, *refs):
    span_ref, inside_ref, first_ref, second_ref = refs[:4]
    place = lax.axis_index("alt")
    source = source_ref[place // halves]
    real, imag = source[0:1, :], source[1:2, :]
    left, right = group_span(halves, group, back, span_ref)
    came = (
        jnp.sum(left * real - right * imag, axis=1, keepdims=True),
        jnp.sum(left * imag + right * real, axis=1, keepdims=True),
    )
    rows = lax.broadcasted_iota(jnp.int32, source.shape, 0)
    amps = []
    for i in range(2):
        left, right = inside_ref[i, 0], inside_ref[i, 1]
        amp = (
            jnp.sum(left * came[0] - right * came[1], axis=0, keepdims=True),
            jnp.sum(left * came[1] + right * came[0], axis=0, keepdims=True),
        )
        amps.append(jnp.where(rows == 0, amp[0], jnp.where(rows == 1, amp[1], 0.0)))
    for k, out_ref in enumerate(refs[4:]):
        target = lax.rem(place + k, n_alt)
        span = pl.ds(pl.multiple_of(target * width, width), width)
        for i, ref in enumerate((first_ref, second_ref)):
            out_ref[i] = scale * mm(amps[i], ref[:, span])[0:2, :]


def settle_body(halves, n_alt, *refs):
    place = lax.axis_index("alt")
    out_ref = refs[n_alt]
    for k, part_ref in enumerate(refs[:n_alt]):
        source = lax.rem(place + n_alt - k, n_alt)
        chunk = part_ref.shape[0]
        freq, half = source // halves, lax.rem(source, halves)
        for i in range(chunk):
            out_ref[freq, half * chunk + i] = part_ref[i]


def local(freq_scale, base_profile, perturb, start_block, source):
    freqs = freq_scale.shape[0]
    seg_count = perturb.shape[0]
    modes, width = start_block.shape
    n_alt = lax.axis_size("alt")
    n_range = lax.axis_size("range")
    total = width * n_alt
    chunk = freqs * seg_count // n_alt
    halves = seg_count // chunk
    length = n_range * halves
    assert n_alt & (n_alt - 1) == 0 and modes == 2 * HALF
    assert chunk == 2 and halves * chunk == seg_count and halves * freqs == n_alt

    def device(freq, at):
        return at // halves * n_alt + freq * halves + at % halves

    def along_chain(value, steps):
        pairs = []
        for freq in range(freqs):
            for at in range(max(0, -steps), min(length, length - steps)):
                pairs.append((device(freq, at), device(freq, at + steps)))
        return lax.ppermute(value, ("range", "alt"), pairs)

    def around(value, k):
        return lax.ppermute(value, "alt", [(i, (i + k) % n_alt) for i in range(n_alt)])

    mine = kernel_call(
        functools.partial(pack_body, modes),
        shape(-(-(modes + 1 + seg_count) // 8) * 8, width),
        [start_block, base_profile[None, :], perturb],
        [pl.BlockSpec(memory_space=pltpu.HBM)] * 3,
        [
            pltpu.VMEM((1, width), jnp.float32),
            pltpu.VMEM((seg_count, width), jnp.float32),
            pltpu.SemaphoreType.DMA((3,)),
        ],
    )
    found, bit = {0: mine}, n_alt
    while bit > 1:
        bit //= 2
        pairs = [(i, i ^ bit) for i in range(n_alt)]
        for key in list(found):
            found[key ^ bit] = lax.ppermute(found[key], "alt", pairs)
    blocks = [found[k] for k in range(n_alt)]
    flops = 2 * modes * modes * total
    image, other, coef = kernel_call(
        functools.partial(iterate_body, n_alt, chunk, seg_count, modes, width),
        [shape(modes, total)] * chunk + [shape(chunk, total)],
        [freq_scale] + blocks,
        [SM] + [VM] * n_alt,
        [
            pltpu.VMEM((chunk, modes, total), jnp.float32),
            pltpu.VMEM((3, 256, total), jnp.bfloat16),
            pltpu.VMEM((256, 256), jnp.float32),
            pltpu.VMEM((chunk, modes, 256), jnp.bfloat16),
        ],
        flops=2 * ITERS * chunk * flops,
    )
    following = along_chain(image, -1)
    first, second, turn, inner, rest = kernel_call(
        functools.partial(finish_body, halves, modes, total),
        [shape(modes, total)] * 2 + [shape(modes, modes)] + [shape(2, modes, modes)] * 2,
        [coef, image, other],
        [VM] * 3,
        [pltpu.VMEM((2, modes, 128), jnp.float32), pltpu.VMEM((modes, total), jnp.float32)],
        flops=16 * flops,
    )
    product = kernel_call(
        product_body, shape(2, modes, modes), [following, second, rest], [VM] * 3, flops=flops
    )

    group = 4
    groups = length // group
    assert groups * group == length and groups > 2

    def turned(value, size, k):
        pairs = []
        for freq in range(freqs):
            for at in range(length):
                goal = at // size * size + (at + k) % size
                pairs.append((device(freq, at), device(freq, goal)))
        return lax.ppermute(value, ("range", "alt"), pairs)

    span, beside, bits = product, [], (1, 2)
    for bit in bits:
        pairs = [
            (device(freq, at), device(freq, at ^ bit))
            for freq in range(freqs)
            for at in range(length)
        ]
        beside.append(lax.ppermute(span, ("range", "alt"), pairs))
        span = kernel_call(
            functools.partial(pair_body, halves, bit),
            shape(2, modes, modes),
            [span, beside[-1]],
            [VM] * 2,
            flops=flops,
        )

    def join(spans, backs):
        return kernel_call(
            functools.partial(join_body, halves, group, backs),
            shape(2, modes, modes),
            spans,
            [VM] * len(spans),
            flops=flops,
        )

    def from_back(backs):
        return [along_chain(span, group * back) if back else span for back in backs]

    if groups <= 4:
        backs = range(1, groups)
        came = [turned(span, length, group * back) for back in backs]
    else:
        backs = range(1, 5)
        span = join(from_back(backs), backs)
        reach = 4
        while groups > 4 * reach:
            backs = range(0, 4 * reach, reach)
            span = join(from_back(backs), backs)
            reach *= 4
        backs = range(0, groups, reach)
        came = from_back(backs)
    inside = kernel_call(
        functools.partial(inside_body, halves, bits),
        shape(2, 2, modes, modes),
        beside + [turn, inner],
        [VM] * 4,
        flops=flops,
    )
    rows = jnp.concatenate([source, jnp.zeros((freqs, 6, modes), jnp.float32)], axis=1)
    for at, back in enumerate(backs[:-1]):
        inside = kernel_call(
            functools.partial(merge_body, halves, group, back, at == len(backs) - 2),
            shape(2, 2, modes, modes),
            [inside, came[at]],
            [VM] * 2,
            flops=flops,
        )
    parts = kernel_call(
        functools.partial(
            field_body,
            halves,
            group,
            backs[-1],
            n_alt,
            width,
            (float(total) / float(modes)) ** 0.5,
        ),
        [shape(chunk, 2, width)] * n_alt,
        [rows, came[-1], inside, first, second],
        [VM] * 5,
    )
    parts = [parts[0]] + [around(parts[k], k) for k in range(1, n_alt)]
    return kernel_call(
        functools.partial(settle_body, halves, n_alt),
        shape(freqs, seg_count, 2, width),
        parts,
        [VM] * n_alt,
    )


def solution(mesh):
    in_specs = (P("freq"), P("alt"), P("range", "alt"), P(None, "alt"), P("freq", None, None))
    out_specs = P("freq", "range", None, "alt")
    return jax.shard_map(local, mesh=mesh, in_specs=in_specs, out_specs=out_specs, check_vma=False)
```

```python
import functools

import jax
import jax.numpy as jnp
from jax import lax
from jax.experimental import pallas as pl
from jax.experimental.pallas import tpu as pltpu
from jax.sharding import PartitionSpec as P

ITERS = 8

phase_step = 0.15
relief = 0.1
HIGHEST = lax.Precision.HIGHEST
VMEM_LIMIT = 48 * 2**20
PACK_LIMIT = 62 * 2**20
HALF = 48


def mm(left, right):
    return lax.dot_general(
        left, right, (((1,), (0,)), ((), ())), precision=HIGHEST, preferred_element_type=jnp.float32
    )


def mmt(left, right):
    return lax.dot_general(
        left, right, (((1,), (1,)), ((), ())), precision=HIGHEST, preferred_element_type=jnp.float32
    )


def short_mm(left, right):
    return lax.dot_general(
        left, right, (((1,), (0,)), ((), ())), preferred_element_type=jnp.float32
    )


def short_mmt(left, right):
    return lax.dot_general(
        left, right, (((1,), (1,)), ((), ())), preferred_element_type=jnp.float32
    )


def kernel_call(body, out_shape, args, specs, scratch=(), flops=0, limit=VMEM_LIMIT):
    nbytes = sum(4 * a.size for a in args) + sum(4 * o.size for o in jax.tree.leaves(out_shape))
    return pl.pallas_call(
        body,
        out_shape=out_shape,
        in_specs=specs,
        out_specs=jax.tree.map(lambda _: pl.BlockSpec(memory_space=pltpu.VMEM), out_shape),
        scratch_shapes=scratch,
        cost_estimate=pl.CostEstimate(flops=flops, bytes_accessed=nbytes, transcendentals=0),
        compiler_params=pltpu.CompilerParams(vmem_limit_bytes=limit),
    )(*args)


VM = pl.BlockSpec(memory_space=pltpu.VMEM)
SM = pl.BlockSpec(memory_space=pltpu.SMEM)


def shape(*dims):
    return jax.ShapeDtypeStruct(dims, jnp.float32)


def row_of(value, at):
    return jnp.broadcast_to(value[at : at + 1, :], value.shape)


def pack_pair(one, two):
    left = lax.broadcasted_iota(jnp.int32, one.shape, 1) < 64
    return [
        jnp.where(left, one, pltpu.roll(two, 64, 1)),
        jnp.where(left, pltpu.roll(one, 128 - HALF, 1), pltpu.roll(two, 64 - HALF, 1)),
    ]


def unpack_pair(low, high):
    early = lax.broadcasted_iota(jnp.int32, low.shape, 1) < HALF
    return (
        jnp.where(early, low, pltpu.roll(high, HALF, 1)),
        jnp.where(early, pltpu.roll(low, 64, 1), pltpu.roll(high, 64 + HALF, 1)),
    )


def inverse_factors(work):
    work = [list(pair) for pair in work]
    count = len(work)
    lanes = lax.broadcasted_iota(jnp.int32, (8, 128), 1)
    subs = lax.broadcasted_iota(jnp.int32, (8, 128), 0)
    base = jnp.where(lanes < 64, 0, 64)
    column = lanes - base
    results = []

    def place(k):
        side = 8 * k // HALF
        return side, 8 * k - side * HALF

    def spread(v, k):
        side, first = place(k)
        return [
            jnp.take_along_axis(work[v][side], base + (first + c), axis=1) for c in range(8)
        ]

    panel = spread(0, 0)
    for k in range(count):
        side, first = place(k)
        near = spread(k + 1, k) if k + 1 < count else None
        ahead = spread(k + 1, k + 1) if k + 1 < count else None
        weights = [[None] * 8 for _ in range(8)]
        inverses, lines = [], []
        scales = jnp.ones((8, 128), jnp.float32)
        for c in range(0, 8, 2):
            corner, cross, late = (
                row_of(panel[c], c),
                row_of(panel[c + 1], c),
                row_of(panel[c + 1], c + 1),
            )
            inv = 1.0 / corner
            second = corner * (1.0 / (corner * late - cross * cross))
            ratio = cross * inv
            weights[c][c + 1] = cross
            factor = panel[c] * inv
            rest = panel[c + 1] - factor * cross
            for d in range(c + 2, 8):
                weights[c][d] = row_of(panel[d], c)
                weights[c + 1][d] = row_of(panel[d], c + 1) - ratio * weights[c][d]
                panel[d] = (panel[d] - factor * weights[c][d]) - (
                    rest * weights[c + 1][d]
                ) * second
            pair = (jnp.where(subs > c, factor, 0.0), jnp.where(subs > c + 1, rest * second, 0.0))
            for e in range(2):
                inverses.append((inv, second)[e])
                scales = jnp.where(subs == c + e, inverses[-1], scales)
                line = [row_of(part, c + e) for part in work[k]]
                line[side] = line[side] + jnp.where(column == first + c + e, 1.0, 0.0)
                lines.append(line)
                work[k] = [part - pair[e] * along for part, along in zip(work[k], line)]
        if near is not None:
            for c in range(8):
                factor = near[c] * inverses[c]
                for d in range(c + 1, 8):
                    near[d] = near[d] - factor * weights[c][d]
                for d in range(8):
                    ahead[d] = ahead[d] - factor * row_of(near[c], d)
                work[k + 1] = [
                    part - factor * along for part, along in zip(work[k + 1], lines[c])
                ]
        panel = ahead
        scaled = [[part * inv for part in line] for line, inv in zip(lines, inverses)]
        for v in range(k + 2, count):
            there, at = place(v)
            for c in range(8):
                factor = jnp.take_along_axis(scaled[c][there], base + subs + at, axis=1)
                work[v] = [part - factor * along for part, along in zip(work[v], lines[c])]
        root = lax.sqrt(scales)
        unit = jnp.where(column == subs + first, 1.0, 0.0)
        own = jnp.where(column < subs + first, work[k][side], unit) * root
        other = work[k][0] * root if side else jnp.zeros((8, 128), jnp.float32)
        results.append((other, own) if side else (own, other))
    return results


def doubled_operator(value, coef):
    width = value.shape[1]
    lanes = lax.broadcasted_iota(jnp.int32, (value.shape[0], 128), 1)
    below, above = pltpu.roll(value, 1, 1), pltpu.roll(value, width - 1, 1)
    below = jnp.concatenate(
        [jnp.where(lanes == 0, 0.0, below[:, :128]), below[:, 128:]], axis=1
    )
    above = jnp.concatenate(
        [above[:, :-128], jnp.where(lanes == 127, 0.0, above[:, -128:])], axis=1
    )
    return coef * value + (below + above)


DOWN = 2.0**-13


def pack_body(modes, start_ref, base_ref, perturb_ref, out_ref, base_buf, perturb_buf, sems):
    copies = [
        pltpu.make_async_copy(source, target, sems.at[i])
        for i, (source, target) in enumerate(
            (
                (start_ref, out_ref.at[0:modes]),
                (base_ref, base_buf),
                (perturb_ref, perturb_buf),
            )
        )
    ]
    for copy in copies:
        copy.start()
    copies[1].wait()
    copies[2].wait()
    seg_count = perturb_ref.shape[0]
    rest = out_ref.shape[0] - modes - 1 - seg_count
    lines = [base_buf[...], perturb_buf[...]]
    if rest:
        lines.append(jnp.zeros((rest, out_ref.shape[1]), jnp.float32))
    out_ref[modes:, :] = jnp.concatenate(lines, axis=0)
    copies[0].wait()


def iterate_body(n_alt, chunk, seg_count, modes, width, scale_ref, *refs):
    blocks, image_refs = refs[:n_alt], refs[n_alt : n_alt + chunk]
    coef_ref, basis_ref, split_ref, gram_ref, inv_ref = refs[n_alt + chunk :]
    place = lax.axis_index("alt")
    flat = place * chunk
    freq = flat // seg_count
    first = flat - freq * seg_count
    total = n_alt * width
    for k, block in enumerate(blocks):
        source = place ^ k
        span = pl.ds(pl.multiple_of(source * width, width), width)
        start = block[0:modes, :] * (1.0 / float(total) ** 0.5)
        for i in range(chunk):
            basis_ref[i, :, span] = start
            change = block[pl.ds(modes + 1 + first + i, 1), :]
            coef_ref[i : i + 1, span] = (2.0 * scale_ref[freq]) * (
                block[modes : modes + 1, :] * (1.0 + relief * change)
            )
    split_ref[...] = jnp.zeros_like(split_ref)
    left = lax.broadcasted_iota(jnp.int32, (8, 128), 1) < 64

    def packed_row(i, at):
        return at // HALF * 128 + i * 64 + at % HALF

    def step(_, carry):
        for i in range(chunk):
            coef = coef_ref[i : i + 1, :]
            for at in range(0, modes, 16):
                image = doubled_operator(basis_ref[i, at : at + 16, :], coef)
                row = packed_row(i, at)
                for part in range(3):
                    piece = image.astype(jnp.bfloat16)
                    split_ref[part, row : row + 16, :] = piece
                    image = image - piece.astype(jnp.float32)
        gram_ref[...] = short_mmt(split_ref[0], split_ref[0]) * DOWN
        work = []
        for at in range(0, modes, 8):
            one, two = packed_row(0, at), packed_row(1, at)
            work.append(
                [
                    jnp.where(
                        left,
                        gram_ref[one : one + 8, side : side + 128],
                        gram_ref[two : two + 8, side : side + 128],
                    )
                    for side in (0, 128)
                ]
            )
        rows = inverse_factors(work)
        for at in range(0, modes, 16):
            for half in range(2):
                part = jnp.concatenate([rows[at // 8][half], rows[at // 8 + 1][half]], axis=0)
                part = part * DOWN**0.5
                here = lax.broadcasted_iota(jnp.int32, part.shape, 1) < 64
                span = slice(half * 128, half * 128 + 128)
                inv_ref[0, at : at + 16, span] = jnp.where(here, part, 0.0).astype(jnp.bfloat16)
                inv_ref[1, at : at + 16, span] = jnp.where(here, 0.0, part).astype(jnp.bfloat16)
        for i in range(chunk):
            for at in range(0, total, 256):
                basis_ref[i, :, at : at + 256] = sum(
                    short_mm(inv_ref[i], split_ref[part, :, at : at + 256]) for part in range(3)
                )
        return carry

    lax.fori_loop(0, ITERS - 1, step, 0)
    for i in range(chunk):
        for at in range(0, modes, 8):
            image_refs[i][at : at + 8, :] = doubled_operator(
                basis_ref[i, at : at + 8, :], coef_ref[i : i + 1, :]
            )


def unit_of(modes):
    rows = lax.broadcasted_iota(jnp.int32, (modes, modes), 0)
    return jnp.where(rows == lax.broadcasted_iota(jnp.int32, (modes, modes), 1), 1.0, 0.0)


def complex_mm(left, right):
    return (
        mm(left[0], right[0]) - mm(left[1], right[1]),
        mm(left[0], right[1]) + mm(left[1], right[0]),
    )


def finish_body(halves, modes, total, coef_ref, *refs):
    image_refs, basis_refs = refs[0:2], refs[2:4]
    turn_ref, inner_ref, rest_ref, gram_ref, double_ref = refs[4:]
    unit = unit_of(modes)
    gram_ref[...] = jnp.zeros_like(gram_ref)
    for i in range(2):
        image = image_refs[i][...]
        gram_ref[i, :, 0:modes] = mmt(image, image) * DOWN
    grams = [gram_ref[i, at : at + 8, :] for at in range(0, modes, 8) for i in range(2)]
    rows = inverse_factors([pack_pair(*grams[i : i + 2]) for i in range(0, len(grams), 2)])
    for k, pair in enumerate(rows):
        for i, part in enumerate(unpack_pair(*pair)):
            gram_ref[i, 8 * k : 8 * k + 8, :] = part * DOWN**0.5
    turns = []
    for i in range(2):
        inv = gram_ref[i, :, 0:modes]
        for at in range(0, total, 256):
            basis_refs[i][:, at : at + 256] = mm(inv, image_refs[i][:, at : at + 256])
    for i, ref in enumerate(basis_refs):
        for at in range(0, modes, 8):
            double_ref[at : at + 8, :] = doubled_operator(
                ref[at : at + 8, :], coef_ref[i : i + 1, :]
            )
        phase = (0.5 * phase_step) * mmt(ref[...], double_ref[...])
        square = mm(phase, phase)
        turns.append(
            (unit - 0.5 * square + mm(square, square) / 24.0, phase - mm(phase, square) / 6.0)
        )
    corr = mmt(basis_refs[1][...], basis_refs[0][...])
    inner = (mm(corr, turns[0][0]), mm(corr, turns[0][1]))
    turn = jnp.where(chain_place(halves) == 0, unit, gram_ref[0, :, 0:modes])
    turn_ref[...] = turn
    late = (mm(turns[1][0], corr), mm(turns[1][1], corr))
    rest = complex_mm(late, (mm(turns[0][0], turn), mm(turns[0][1], turn)))
    for part in range(2):
        inner_ref[part] = inner[part]
        rest_ref[part] = rest[part]


def chain_place(halves):
    return lax.axis_index("range") * halves + lax.rem(lax.axis_index("alt"), halves)


def product_body(next_ref, second_ref, rest_ref, out_ref):
    corr = mmt(next_ref[...], second_ref[...])
    for part in range(2):
        out_ref[part] = mm(corr, rest_ref[part])


def later_half(halves, bit):
    return lax.rem(chain_place(halves) // bit, 2) == 1


def pair_body(halves, bit, own_ref, other_ref, out_ref):
    later = later_half(halves, bit)
    own, other = (own_ref[0], own_ref[1]), (other_ref[0], other_ref[1])
    pairs = list(zip(own, other))
    out_ref[0], out_ref[1] = complex_mm(
        [jnp.where(later, a, b) for a, b in pairs], [jnp.where(later, b, a) for a, b in pairs]
    )


def fold(spans):
    while len(spans) > 1:
        pairs = [complex_mm(*spans[i : i + 2]) for i in range(0, len(spans) - 1, 2)]
        spans = pairs + spans[len(pairs) * 2 :]
    return spans[0]


def inside_body(halves, bits, *refs):
    turn_ref, inner_ref, out_ref = refs[len(bits) :]
    unit = unit_of(inner_ref.shape[1])
    spans = []
    for bit, ref in zip(bits, refs):
        later = later_half(halves, bit)
        spans.append((jnp.where(later, ref[0], unit), jnp.where(later, ref[1], 0.0)))
    reached = fold(spans)
    reached = (mm(turn_ref[...], reached[0]), mm(turn_ref[...], reached[1]))
    following = complex_mm((inner_ref[0], inner_ref[1]), reached)
    for part in range(2):
        out_ref[0, part] = reached[part]
        out_ref[1, part] = following[part]


def join_body(halves, group, backs, *refs):
    at = chain_place(halves) // group
    spans = []
    for back, ref in zip(backs, refs):
        missing = jnp.where(at < back, unit_of(ref.shape[1]), 0.0)
        spans.append((ref[0] + missing, ref[1]) if back else (ref[0], ref[1]))
    refs[-1][0], refs[-1][1] = fold(spans)


def group_span(halves, group, back, ref):
    there = chain_place(halves) // group >= back
    return jnp.where(there, ref[0], unit_of(ref.shape[1])), jnp.where(there, ref[1], 0.0)


def merge_body(halves, group, back, last, inside_ref, span_ref, out_ref):
    span = group_span(halves, group, back, span_ref)
    for i in range(2):
        merged = complex_mm((inside_ref[i, 0], inside_ref[i, 1]), span)
        for part in range(2):
            out_ref[i, part] = merged[part].T if last else merged[part]


def field_body(halves, group, back, n_alt, width, scale, source_ref, *refs):
    span_ref, inside_ref, first_ref, second_ref = refs[:4]
    place = lax.axis_index("alt")
    source = source_ref[place // halves]
    real, imag = source[0:1, :], source[1:2, :]
    left, right = group_span(halves, group, back, span_ref)
    came = (
        jnp.sum(left * real - right * imag, axis=1, keepdims=True),
        jnp.sum(left * imag + right * real, axis=1, keepdims=True),
    )
    rows = lax.broadcasted_iota(jnp.int32, source.shape, 0)
    amps = []
    for i in range(2):
        left, right = inside_ref[i, 0], inside_ref[i, 1]
        amp = (
            jnp.sum(left * came[0] - right * came[1], axis=0, keepdims=True),
            jnp.sum(left * came[1] + right * came[0], axis=0, keepdims=True),
        )
        amps.append(jnp.where(rows == 0, amp[0], jnp.where(rows == 1, amp[1], 0.0)))
    for k, out_ref in enumerate(refs[4:]):
        target = lax.rem(place + k, n_alt)
        span = pl.ds(pl.multiple_of(target * width, width), width)
        for i, ref in enumerate((first_ref, second_ref)):
            out_ref[i] = scale * mm(amps[i], ref[:, span])[0:2, :]


def settle_body(halves, n_alt, *refs):
    place = lax.axis_index("alt")
    out_ref = refs[n_alt]
    for k, part_ref in enumerate(refs[:n_alt]):
        source = lax.rem(place + n_alt - k, n_alt)
        chunk = part_ref.shape[0]
        freq, half = source // halves, lax.rem(source, halves)
        for i in range(chunk):
            out_ref[freq, half * chunk + i] = part_ref[i]


def local(freq_scale, base_profile, perturb, start_block, source):
    freqs = freq_scale.shape[0]
    seg_count = perturb.shape[0]
    modes, width = start_block.shape
    n_alt = lax.axis_size("alt")
    n_range = lax.axis_size("range")
    total = width * n_alt
    chunk = freqs * seg_count // n_alt
    halves = seg_count // chunk
    length = n_range * halves
    assert n_alt & (n_alt - 1) == 0 and modes == 2 * HALF
    assert chunk == 2 and halves * chunk == seg_count and halves * freqs == n_alt

    def device(freq, at):
        return at // halves * n_alt + freq * halves + at % halves

    def along_chain(value, steps):
        pairs = []
        for freq in range(freqs):
            for at in range(max(0, -steps), min(length, length - steps)):
                pairs.append((device(freq, at), device(freq, at + steps)))
        return lax.ppermute(value, ("range", "alt"), pairs)

    def around(value, k):
        return lax.ppermute(value, "alt", [(i, (i + k) % n_alt) for i in range(n_alt)])

    mine = kernel_call(
        functools.partial(pack_body, modes),
        shape(-(-(modes + 1 + seg_count) // 8) * 8, width),
        [start_block, base_profile[None, :], perturb],
        [pl.BlockSpec(memory_space=pltpu.HBM)] * 3,
        [
            pltpu.VMEM((1, width), jnp.float32),
            pltpu.VMEM((seg_count, width), jnp.float32),
            pltpu.SemaphoreType.DMA((3,)),
        ],
        limit=PACK_LIMIT,
    )
    found, bit = {0: mine}, n_alt
    while bit > 1:
        bit //= 2
        pairs = [(i, i ^ bit) for i in range(n_alt)]
        for key in list(found):
            found[key ^ bit] = lax.ppermute(found[key], "alt", pairs)
    blocks = [found[k] for k in range(n_alt)]
    flops = 2 * modes * modes * total
    image, other, coef = kernel_call(
        functools.partial(iterate_body, n_alt, chunk, seg_count, modes, width),
        [shape(modes, total)] * chunk + [shape(chunk, total)],
        [freq_scale] + blocks,
        [SM] + [VM] * n_alt,
        [
            pltpu.VMEM((chunk, modes, total), jnp.float32),
            pltpu.VMEM((3, 256, total), jnp.bfloat16),
            pltpu.VMEM((256, 256), jnp.float32),
            pltpu.VMEM((chunk, modes, 256), jnp.bfloat16),
        ],
        flops=2 * ITERS * chunk * flops,
    )
    following = along_chain(image, -1)
    first, second, turn, inner, rest = kernel_call(
        functools.partial(finish_body, halves, modes, total),
        [shape(modes, total)] * 2 + [shape(modes, modes)] + [shape(2, modes, modes)] * 2,
        [coef, image, other],
        [VM] * 3,
        [pltpu.VMEM((2, modes, 128), jnp.float32), pltpu.VMEM((modes, total), jnp.float32)],
        flops=16 * flops,
    )
    product = kernel_call(
        product_body, shape(2, modes, modes), [following, second, rest], [VM] * 3, flops=flops
    )

    group = 4
    groups = length // group
    assert groups * group == length and groups > 2

    def turned(value, size, k):
        pairs = []
        for freq in range(freqs):
            for at in range(length):
                goal = at // size * size + (at + k) % size
                pairs.append((device(freq, at), device(freq, goal)))
        return lax.ppermute(value, ("range", "alt"), pairs)

    span, beside, bits = product, [], (1, 2)
    for bit in bits:
        pairs = [
            (device(freq, at), device(freq, at ^ bit))
            for freq in range(freqs)
            for at in range(length)
        ]
        beside.append(lax.ppermute(span, ("range", "alt"), pairs))
        span = kernel_call(
            functools.partial(pair_body, halves, bit),
            shape(2, modes, modes),
            [span, beside[-1]],
            [VM] * 2,
            flops=flops,
        )

    def join(spans, backs):
        return kernel_call(
            functools.partial(join_body, halves, group, backs),
            shape(2, modes, modes),
            spans,
            [VM] * len(spans),
            flops=flops,
        )

    def from_back(backs):
        return [along_chain(span, group * back) if back else span for back in backs]

    if groups <= 4:
        backs = range(1, groups)
        came = [turned(span, length, group * back) for back in backs]
    else:
        backs = range(1, 5)
        span = join(from_back(backs), backs)
        reach = 4
        while groups > 4 * reach:
            backs = range(0, 4 * reach, reach)
            span = join(from_back(backs), backs)
            reach *= 4
        backs = range(0, groups, reach)
        came = from_back(backs)
    inside = kernel_call(
        functools.partial(inside_body, halves, bits),
        shape(2, 2, modes, modes),
        beside + [turn, inner],
        [VM] * 4,
        flops=flops,
    )
    rows = jnp.concatenate([source, jnp.zeros((freqs, 6, modes), jnp.float32)], axis=1)
    for at, back in enumerate(backs[:-1]):
        inside = kernel_call(
            functools.partial(merge_body, halves, group, back, at == len(backs) - 2),
            shape(2, 2, modes, modes),
            [inside, came[at]],
            [VM] * 2,
            flops=flops,
        )
    parts = kernel_call(
        functools.partial(
            field_body,
            halves,
            group,
            backs[-1],
            n_alt,
            width,
            (float(total) / float(modes)) ** 0.5,
        ),
        [shape(chunk, 2, width)] * n_alt,
        [rows, came[-1], inside, first, second],
        [VM] * 5,
    )
    parts = [parts[0]] + [around(parts[k], k) for k in range(1, n_alt)]
    return kernel_call(
        functools.partial(settle_body, halves, n_alt),
        shape(freqs, seg_count, 2, width),
        parts,
        [VM] * n_alt,
    )


def solution(mesh):
    in_specs = (P("freq"), P("alt"), P("range", "alt"), P(None, "alt"), P("freq", None, None))
    out_specs = P("freq", "range", None, "alt")
    return jax.shard_map(local, mesh=mesh, in_specs=in_specs, out_specs=out_specs, check_vma=False)
```

```python
import functools

import jax
import jax.numpy as jnp
from jax import lax
from jax.experimental import pallas as pl
from jax.experimental.pallas import tpu as pltpu
from jax.sharding import PartitionSpec as P

ITERS = 8

phase_step = 0.15
relief = 0.1
HIGHEST = lax.Precision.HIGHEST
VMEM_LIMIT = 48 * 2**20
HALF = 48


def mm(left, right):
    return lax.dot_general(
        left, right, (((1,), (0,)), ((), ())), precision=HIGHEST, preferred_element_type=jnp.float32
    )


def mmt(left, right):
    return lax.dot_general(
        left, right, (((1,), (1,)), ((), ())), precision=HIGHEST, preferred_element_type=jnp.float32
    )


def short_mm(left, right):
    return lax.dot_general(
        left, right, (((1,), (0,)), ((), ())), preferred_element_type=jnp.float32
    )


def short_mmt(left, right):
    return lax.dot_general(
        left, right, (((1,), (1,)), ((), ())), preferred_element_type=jnp.float32
    )


def kernel_call(body, out_shape, args, specs, scratch=(), flops=0):
    nbytes = sum(4 * a.size for a in args) + sum(4 * o.size for o in jax.tree.leaves(out_shape))
    return pl.pallas_call(
        body,
        out_shape=out_shape,
        in_specs=specs,
        out_specs=jax.tree.map(lambda _: pl.BlockSpec(memory_space=pltpu.VMEM), out_shape),
        scratch_shapes=scratch,
        cost_estimate=pl.CostEstimate(flops=flops, bytes_accessed=nbytes, transcendentals=0),
        compiler_params=pltpu.CompilerParams(vmem_limit_bytes=VMEM_LIMIT),
    )(*args)


VM = pl.BlockSpec(memory_space=pltpu.VMEM)
SM = pl.BlockSpec(memory_space=pltpu.SMEM)


def shape(*dims):
    return jax.ShapeDtypeStruct(dims, jnp.float32)


def row_of(value, at):
    return jnp.broadcast_to(value[at : at + 1, :], value.shape)


def pack_pair(one, two):
    left = lax.broadcasted_iota(jnp.int32, one.shape, 1) < 64
    return [
        jnp.where(left, one, pltpu.roll(two, 64, 1)),
        jnp.where(left, pltpu.roll(one, 128 - HALF, 1), pltpu.roll(two, 64 - HALF, 1)),
    ]


def unpack_pair(low, high):
    early = lax.broadcasted_iota(jnp.int32, low.shape, 1) < HALF
    return (
        jnp.where(early, low, pltpu.roll(high, HALF, 1)),
        jnp.where(early, pltpu.roll(low, 64, 1), pltpu.roll(high, 64 + HALF, 1)),
    )


def inverse_factors(work):
    work = [list(pair) for pair in work]
    count = len(work)
    lanes = lax.broadcasted_iota(jnp.int32, (8, 128), 1)
    subs = lax.broadcasted_iota(jnp.int32, (8, 128), 0)
    base = jnp.where(lanes < 64, 0, 64)
    column = lanes - base
    results = []

    def place(k):
        side = 8 * k // HALF
        return side, 8 * k - side * HALF

    def spread(v, k):
        side, first = place(k)
        return [
            jnp.take_along_axis(work[v][side], base + (first + c), axis=1) for c in range(8)
        ]

    panel = spread(0, 0)
    for k in range(count):
        side, first = place(k)
        near = spread(k + 1, k) if k + 1 < count else None
        ahead = spread(k + 1, k + 1) if k + 1 < count else None
        weights = [[None] * 8 for _ in range(8)]
        inverses, lines = [], []
        scales = jnp.ones((8, 128), jnp.float32)
        for c in range(0, 8, 2):
            corner, cross, late = (
                row_of(panel[c], c),
                row_of(panel[c + 1], c),
                row_of(panel[c + 1], c + 1),
            )
            inv = 1.0 / corner
            second = corner * (1.0 / (corner * late - cross * cross))
            ratio = cross * inv
            weights[c][c + 1] = cross
            factor = panel[c] * inv
            rest = panel[c + 1] - factor * cross
            for d in range(c + 2, 8):
                weights[c][d] = row_of(panel[d], c)
                weights[c + 1][d] = row_of(panel[d], c + 1) - ratio * weights[c][d]
                panel[d] = (panel[d] - factor * weights[c][d]) - (
                    rest * weights[c + 1][d]
                ) * second
            pair = (jnp.where(subs > c, factor, 0.0), jnp.where(subs > c + 1, rest * second, 0.0))
            for e in range(2):
                inverses.append((inv, second)[e])
                scales = jnp.where(subs == c + e, inverses[-1], scales)
                line = [row_of(part, c + e) for part in work[k]]
                line[side] = line[side] + jnp.where(column == first + c + e, 1.0, 0.0)
                lines.append(line)
                work[k] = [part - pair[e] * along for part, along in zip(work[k], line)]
        if near is not None:
            for c in range(8):
                factor = near[c] * inverses[c]
                for d in range(c + 1, 8):
                    near[d] = near[d] - factor * weights[c][d]
                for d in range(8):
                    ahead[d] = ahead[d] - factor * row_of(near[c], d)
                work[k + 1] = [
                    part - factor * along for part, along in zip(work[k + 1], lines[c])
                ]
        panel = ahead
        scaled = [[part * inv for part in line] for line, inv in zip(lines, inverses)]
        for v in range(k + 2, count):
            there, at = place(v)
            for c in range(8):
                factor = jnp.take_along_axis(scaled[c][there], base + subs + at, axis=1)
                work[v] = [part - factor * along for part, along in zip(work[v], lines[c])]
        root = lax.sqrt(scales)
        unit = jnp.where(column == subs + first, 1.0, 0.0)
        own = jnp.where(column < subs + first, work[k][side], unit) * root
        other = work[k][0] * root if side else jnp.zeros((8, 128), jnp.float32)
        results.append((other, own) if side else (own, other))
    return results


def doubled_operator(value, coef):
    width = value.shape[1]
    lanes = lax.broadcasted_iota(jnp.int32, (value.shape[0], 128), 1)
    below, above = pltpu.roll(value, 1, 1), pltpu.roll(value, width - 1, 1)
    below = jnp.concatenate(
        [jnp.where(lanes == 0, 0.0, below[:, :128]), below[:, 128:]], axis=1
    )
    above = jnp.concatenate(
        [above[:, :-128], jnp.where(lanes == 127, 0.0, above[:, -128:])], axis=1
    )
    return coef * value + (below + above)


DOWN = 2.0**-13


def pack_body(modes, start_ref, base_ref, perturb_ref, out_ref, base_buf, perturb_buf, sems):
    copies = [
        pltpu.make_async_copy(source, target, sems.at[i])
        for i, (source, target) in enumerate(
            (
                (start_ref, out_ref.at[0:modes]),
                (base_ref, base_buf),
                (perturb_ref, perturb_buf),
            )
        )
    ]
    for copy in copies:
        copy.start()
    copies[1].wait()
    copies[2].wait()
    seg_count = perturb_ref.shape[0]
    rest = out_ref.shape[0] - modes - 1 - seg_count
    lines = [base_buf[...], perturb_buf[...]]
    if rest:
        lines.append(jnp.zeros((rest, out_ref.shape[1]), jnp.float32))
    out_ref[modes:, :] = jnp.concatenate(lines, axis=0)
    copies[0].wait()


def iterate_body(n_alt, chunk, seg_count, modes, width, scale_ref, *refs):
    blocks, image_refs = refs[:n_alt], refs[n_alt : n_alt + chunk]
    coef_ref, basis_ref, split_ref, gram_ref, inv_ref = refs[n_alt + chunk :]
    place = lax.axis_index("alt")
    flat = place * chunk
    freq = flat // seg_count
    first = flat - freq * seg_count
    total = n_alt * width
    for k, block in enumerate(blocks):
        source = place ^ k
        span = pl.ds(pl.multiple_of(source * width, width), width)
        start = block[0:modes, :] * (1.0 / float(total) ** 0.5)
        for i in range(chunk):
            basis_ref[i, :, span] = start
            change = block[pl.ds(modes + 1 + first + i, 1), :]
            coef_ref[i : i + 1, span] = (2.0 * scale_ref[freq]) * (
                block[modes : modes + 1, :] * (1.0 + relief * change)
            )
    split_ref[...] = jnp.zeros_like(split_ref)
    left = lax.broadcasted_iota(jnp.int32, (8, 128), 1) < 64

    def packed_row(i, at):
        return at // HALF * 128 + i * 64 + at % HALF

    def step(_, carry):
        for i in range(chunk):
            coef = coef_ref[i : i + 1, :]
            for at in range(0, modes, 16):
                image = doubled_operator(basis_ref[i, at : at + 16, :], coef)
                row = packed_row(i, at)
                for part in range(3):
                    piece = image.astype(jnp.bfloat16)
                    split_ref[part, row : row + 16, :] = piece
                    image = image - piece.astype(jnp.float32)
        gram_ref[...] = short_mmt(split_ref[0], split_ref[0]) * DOWN
        work = []
        for at in range(0, modes, 8):
            one, two = packed_row(0, at), packed_row(1, at)
            work.append(
                [
                    jnp.where(
                        left,
                        gram_ref[one : one + 8, side : side + 128],
                        gram_ref[two : two + 8, side : side + 128],
                    )
                    for side in (0, 128)
                ]
            )
        rows = inverse_factors(work)
        for at in range(0, modes, 16):
            for half in range(2):
                part = jnp.concatenate([rows[at // 8][half], rows[at // 8 + 1][half]], axis=0)
                part = part * DOWN**0.5
                here = lax.broadcasted_iota(jnp.int32, part.shape, 1) < 64
                span = slice(half * 128, half * 128 + 128)
                inv_ref[0, at : at + 16, span] = jnp.where(here, part, 0.0).astype(jnp.bfloat16)
                inv_ref[1, at : at + 16, span] = jnp.where(here, 0.0, part).astype(jnp.bfloat16)
        for i in range(chunk):
            for at in range(0, total, 256):
                basis_ref[i, :, at : at + 256] = sum(
                    short_mm(inv_ref[i], split_ref[part, :, at : at + 256]) for part in range(3)
                )
        return carry

    lax.fori_loop(0, ITERS - 1, step, 0, unroll=True)
    for i in range(chunk):
        for at in range(0, modes, 8):
            image_refs[i][at : at + 8, :] = doubled_operator(
                basis_ref[i, at : at + 8, :], coef_ref[i : i + 1, :]
            )


def unit_of(modes):
    rows = lax.broadcasted_iota(jnp.int32, (modes, modes), 0)
    return jnp.where(rows == lax.broadcasted_iota(jnp.int32, (modes, modes), 1), 1.0, 0.0)


def complex_mm(left, right):
    return (
        mm(left[0], right[0]) - mm(left[1], right[1]),
        mm(left[0], right[1]) + mm(left[1], right[0]),
    )


def finish_body(halves, modes, total, coef_ref, *refs):
    image_refs, basis_refs = refs[0:2], refs[2:4]
    turn_ref, inner_ref, rest_ref, gram_ref, double_ref = refs[4:]
    unit = unit_of(modes)
    gram_ref[...] = jnp.zeros_like(gram_ref)
    for i in range(2):
        image = image_refs[i][...]
        gram_ref[i, :, 0:modes] = mmt(image, image) * DOWN
    grams = [gram_ref[i, at : at + 8, :] for at in range(0, modes, 8) for i in range(2)]
    rows = inverse_factors([pack_pair(*grams[i : i + 2]) for i in range(0, len(grams), 2)])
    for k, pair in enumerate(rows):
        for i, part in enumerate(unpack_pair(*pair)):
            gram_ref[i, 8 * k : 8 * k + 8, :] = part * DOWN**0.5
    turns = []
    for i in range(2):
        inv = gram_ref[i, :, 0:modes]
        for at in range(0, total, 256):
            basis_refs[i][:, at : at + 256] = mm(inv, image_refs[i][:, at : at + 256])
    for i, ref in enumerate(basis_refs):
        for at in range(0, modes, 8):
            double_ref[at : at + 8, :] = doubled_operator(
                ref[at : at + 8, :], coef_ref[i : i + 1, :]
            )
        phase = (0.5 * phase_step) * mmt(ref[...], double_ref[...])
        square = mm(phase, phase)
        turns.append(
            (unit - 0.5 * square + mm(square, square) / 24.0, phase - mm(phase, square) / 6.0)
        )
    corr = mmt(basis_refs[1][...], basis_refs[0][...])
    inner = (mm(corr, turns[0][0]), mm(corr, turns[0][1]))
    turn = jnp.where(chain_place(halves) == 0, unit, gram_ref[0, :, 0:modes])
    turn_ref[...] = turn
    late = (mm(turns[1][0], corr), mm(turns[1][1], corr))
    rest = complex_mm(late, (mm(turns[0][0], turn), mm(turns[0][1], turn)))
    for part in range(2):
        inner_ref[part] = inner[part]
        rest_ref[part] = rest[part]


def chain_place(halves):
    return lax.axis_index("range") * halves + lax.rem(lax.axis_index("alt"), halves)


def product_body(next_ref, second_ref, rest_ref, out_ref):
    corr = mmt(next_ref[...], second_ref[...])
    for part in range(2):
        out_ref[part] = mm(corr, rest_ref[part])


def later_half(halves, bit):
    return lax.rem(chain_place(halves) // bit, 2) == 1


def pair_body(halves, bit, own_ref, other_ref, out_ref):
    later = later_half(halves, bit)
    own, other = (own_ref[0], own_ref[1]), (other_ref[0], other_ref[1])
    pairs = list(zip(own, other))
    out_ref[0], out_ref[1] = complex_mm(
        [jnp.where(later, a, b) for a, b in pairs], [jnp.where(later, b, a) for a, b in pairs]
    )


def fold(spans):
    while len(spans) > 1:
        pairs = [complex_mm(*spans[i : i + 2]) for i in range(0, len(spans) - 1, 2)]
        spans = pairs + spans[len(pairs) * 2 :]
    return spans[0]


def inside_body(halves, bits, *refs):
    turn_ref, inner_ref, out_ref = refs[len(bits) :]
    unit = unit_of(inner_ref.shape[1])
    spans = []
    for bit, ref in zip(bits, refs):
        later = later_half(halves, bit)
        spans.append((jnp.where(later, ref[0], unit), jnp.where(later, ref[1], 0.0)))
    reached = fold(spans)
    reached = (mm(turn_ref[...], reached[0]), mm(turn_ref[...], reached[1]))
    following = complex_mm((inner_ref[0], inner_ref[1]), reached)
    for part in range(2):
        out_ref[0, part] = reached[part]
        out_ref[1, part] = following[part]


def join_body(halves, group, backs, *refs):
    at = chain_place(halves) // group
    spans = []
    for back, ref in zip(backs, refs):
        missing = jnp.where(at < back, unit_of(ref.shape[1]), 0.0)
        spans.append((ref[0] + missing, ref[1]) if back else (ref[0], ref[1]))
    refs[-1][0], refs[-1][1] = fold(spans)


def group_span(halves, group, back, ref):
    there = chain_place(halves) // group >= back
    return jnp.where(there, ref[0], unit_of(ref.shape[1])), jnp.where(there, ref[1], 0.0)


def merge_body(halves, group, back, last, inside_ref, span_ref, out_ref):
    span = group_span(halves, group, back, span_ref)
    for i in range(2):
        merged = complex_mm((inside_ref[i, 0], inside_ref[i, 1]), span)
        for part in range(2):
            out_ref[i, part] = merged[part].T if last else merged[part]


def field_body(halves, group, back, n_alt, width, scale, source_ref, *refs):
    span_ref, inside_ref, first_ref, second_ref = refs[:4]
    place = lax.axis_index("alt")
    source = source_ref[place // halves]
    real, imag = source[0:1, :], source[1:2, :]
    left, right = group_span(halves, group, back, span_ref)
    came = (
        jnp.sum(left * real - right * imag, axis=1, keepdims=True),
        jnp.sum(left * imag + right * real, axis=1, keepdims=True),
    )
    rows = lax.broadcasted_iota(jnp.int32, source.shape, 0)
    amps = []
    for i in range(2):
        left, right = inside_ref[i, 0], inside_ref[i, 1]
        amp = (
            jnp.sum(left * came[0] - right * came[1], axis=0, keepdims=True),
            jnp.sum(left * came[1] + right * came[0], axis=0, keepdims=True),
        )
        amps.append(jnp.where(rows == 0, amp[0], jnp.where(rows == 1, amp[1], 0.0)))
    for k, out_ref in enumerate(refs[4:]):
        target = lax.rem(place + k, n_alt)
        span = pl.ds(pl.multiple_of(target * width, width), width)
        for i, ref in enumerate((first_ref, second_ref)):
            out_ref[i] = scale * mm(amps[i], ref[:, span])[0:2, :]


def settle_body(halves, n_alt, *refs):
    place = lax.axis_index("alt")
    out_ref = refs[n_alt]
    for k, part_ref in enumerate(refs[:n_alt]):
        source = lax.rem(place + n_alt - k, n_alt)
        chunk = part_ref.shape[0]
        freq, half = source // halves, lax.rem(source, halves)
        for i in range(chunk):
            out_ref[freq, half * chunk + i] = part_ref[i]


def local(freq_scale, base_profile, perturb, start_block, source):
    freqs = freq_scale.shape[0]
    seg_count = perturb.shape[0]
    modes, width = start_block.shape
    n_alt = lax.axis_size("alt")
    n_range = lax.axis_size("range")
    total = width * n_alt
    chunk = freqs * seg_count // n_alt
    halves = seg_count // chunk
    length = n_range * halves
    assert n_alt & (n_alt - 1) == 0 and modes == 2 * HALF
    assert chunk == 2 and halves * chunk == seg_count and halves * freqs == n_alt

    def device(freq, at):
        return at // halves * n_alt + freq * halves + at % halves

    def along_chain(value, steps):
        pairs = []
        for freq in range(freqs):
            for at in range(max(0, -steps), min(length, length - steps)):
                pairs.append((device(freq, at), device(freq, at + steps)))
        return lax.ppermute(value, ("range", "alt"), pairs)

    def around(value, k):
        return lax.ppermute(value, "alt", [(i, (i + k) % n_alt) for i in range(n_alt)])

    mine = kernel_call(
        functools.partial(pack_body, modes),
        shape(-(-(modes + 1 + seg_count) // 8) * 8, width),
        [start_block, base_profile[None, :], perturb],
        [pl.BlockSpec(memory_space=pltpu.HBM)] * 3,
        [
            pltpu.VMEM((1, width), jnp.float32),
            pltpu.VMEM((seg_count, width), jnp.float32),
            pltpu.SemaphoreType.DMA((3,)),
        ],
    )
    found, bit = {0: mine}, n_alt
    while bit > 1:
        bit //= 2
        pairs = [(i, i ^ bit) for i in range(n_alt)]
        for key in list(found):
            found[key ^ bit] = lax.ppermute(found[key], "alt", pairs)
    blocks = [found[k] for k in range(n_alt)]
    flops = 2 * modes * modes * total
    image, other, coef = kernel_call(
        functools.partial(iterate_body, n_alt, chunk, seg_count, modes, width),
        [shape(modes, total)] * chunk + [shape(chunk, total)],
        [freq_scale] + blocks,
        [SM] + [VM] * n_alt,
        [
            pltpu.VMEM((chunk, modes, total), jnp.float32),
            pltpu.VMEM((3, 256, total), jnp.bfloat16),
            pltpu.VMEM((256, 256), jnp.float32),
            pltpu.VMEM((chunk, modes, 256), jnp.bfloat16),
        ],
        flops=2 * ITERS * chunk * flops,
    )
    following = along_chain(image, -1)
    first, second, turn, inner, rest = kernel_call(
        functools.partial(finish_body, halves, modes, total),
        [shape(modes, total)] * 2 + [shape(modes, modes)] + [shape(2, modes, modes)] * 2,
        [coef, image, other],
        [VM] * 3,
        [pltpu.VMEM((2, modes, 128), jnp.float32), pltpu.VMEM((modes, total), jnp.float32)],
        flops=16 * flops,
    )
    product = kernel_call(
        product_body, shape(2, modes, modes), [following, second, rest], [VM] * 3, flops=flops
    )

    group = 4
    groups = length // group
    assert groups * group == length and groups > 2

    def turned(value, size, k):
        pairs = []
        for freq in range(freqs):
            for at in range(length):
                goal = at // size * size + (at + k) % size
                pairs.append((device(freq, at), device(freq, goal)))
        return lax.ppermute(value, ("range", "alt"), pairs)

    span, beside, bits = product, [], (1, 2)
    for bit in bits:
        pairs = [
            (device(freq, at), device(freq, at ^ bit))
            for freq in range(freqs)
            for at in range(length)
        ]
        beside.append(lax.ppermute(span, ("range", "alt"), pairs))
        span = kernel_call(
            functools.partial(pair_body, halves, bit),
            shape(2, modes, modes),
            [span, beside[-1]],
            [VM] * 2,
            flops=flops,
        )

    def join(spans, backs):
        return kernel_call(
            functools.partial(join_body, halves, group, backs),
            shape(2, modes, modes),
            spans,
            [VM] * len(spans),
            flops=flops,
        )

    def from_back(backs):
        return [along_chain(span, group * back) if back else span for back in backs]

    if groups <= 4:
        backs = range(1, groups)
        came = [turned(span, length, group * back) for back in backs]
    else:
        backs = range(1, 5)
        span = join(from_back(backs), backs)
        reach = 4
        while groups > 4 * reach:
            backs = range(0, 4 * reach, reach)
            span = join(from_back(backs), backs)
            reach *= 4
        backs = range(0, groups, reach)
        came = from_back(backs)
    inside = kernel_call(
        functools.partial(inside_body, halves, bits),
        shape(2, 2, modes, modes),
        beside + [turn, inner],
        [VM] * 4,
        flops=flops,
    )
    rows = jnp.concatenate([source, jnp.zeros((freqs, 6, modes), jnp.float32)], axis=1)
    for at, back in enumerate(backs[:-1]):
        inside = kernel_call(
            functools.partial(merge_body, halves, group, back, at == len(backs) - 2),
            shape(2, 2, modes, modes),
            [inside, came[at]],
            [VM] * 2,
            flops=flops,
        )
    parts = kernel_call(
        functools.partial(
            field_body,
            halves,
            group,
            backs[-1],
            n_alt,
            width,
            (float(total) / float(modes)) ** 0.5,
        ),
        [shape(chunk, 2, width)] * n_alt,
        [rows, came[-1], inside, first, second],
        [VM] * 5,
    )
    parts = [parts[0]] + [around(parts[k], k) for k in range(1, n_alt)]
    return kernel_call(
        functools.partial(settle_body, halves, n_alt),
        shape(freqs, seg_count, 2, width),
        parts,
        [VM] * n_alt,
    )


def solution(mesh):
    in_specs = (P("freq"), P("alt"), P("range", "alt"), P(None, "alt"), P("freq", None, None))
    out_specs = P("freq", "range", None, "alt")
    return jax.shard_map(local, mesh=mesh, in_specs=in_specs, out_specs=out_specs, check_vma=False)
```

```python
import functools

import jax
import jax.numpy as jnp
from jax import lax
from jax.experimental import pallas as pl
from jax.experimental.pallas import tpu as pltpu
from jax.sharding import PartitionSpec as P

ITERS = 8

phase_step = 0.15
relief = 0.1
HIGHEST = lax.Precision.HIGHEST
VMEM_LIMIT = 48 * 2**20
HALF = 48


def mm(left, right):
    return lax.dot_general(
        left, right, (((1,), (0,)), ((), ())), precision=HIGHEST, preferred_element_type=jnp.float32
    )


def mmt(left, right):
    return lax.dot_general(
        left, right, (((1,), (1,)), ((), ())), precision=HIGHEST, preferred_element_type=jnp.float32
    )


def short_mm(left, right):
    return lax.dot_general(
        left, right, (((1,), (0,)), ((), ())), preferred_element_type=jnp.float32
    )


def short_mmt(left, right):
    return lax.dot_general(
        left, right, (((1,), (1,)), ((), ())), preferred_element_type=jnp.float32
    )


def kernel_call(body, out_shape, args, specs, scratch=(), flops=0):
    nbytes = sum(4 * a.size for a in args) + sum(4 * o.size for o in jax.tree.leaves(out_shape))
    return pl.pallas_call(
        body,
        out_shape=out_shape,
        in_specs=specs,
        out_specs=jax.tree.map(lambda _: pl.BlockSpec(memory_space=pltpu.VMEM), out_shape),
        scratch_shapes=scratch,
        cost_estimate=pl.CostEstimate(flops=flops, bytes_accessed=nbytes, transcendentals=0),
        compiler_params=pltpu.CompilerParams(vmem_limit_bytes=VMEM_LIMIT),
    )(*args)


VM = pl.BlockSpec(memory_space=pltpu.VMEM)
SM = pl.BlockSpec(memory_space=pltpu.SMEM)


def shape(*dims):
    return jax.ShapeDtypeStruct(dims, jnp.float32)


def row_of(value, at):
    return jnp.broadcast_to(value[at : at + 1, :], value.shape)


def pack_pair(one, two):
    left = lax.broadcasted_iota(jnp.int32, one.shape, 1) < 64
    return [
        jnp.where(left, one, pltpu.roll(two, 64, 1)),
        jnp.where(left, pltpu.roll(one, 128 - HALF, 1), pltpu.roll(two, 64 - HALF, 1)),
    ]


def unpack_pair(low, high):
    early = lax.broadcasted_iota(jnp.int32, low.shape, 1) < HALF
    return (
        jnp.where(early, low, pltpu.roll(high, HALF, 1)),
        jnp.where(early, pltpu.roll(low, 64, 1), pltpu.roll(high, 64 + HALF, 1)),
    )


def inverse_factors(work):
    work = [list(pair) for pair in work]
    count = len(work)
    lanes = lax.broadcasted_iota(jnp.int32, (8, 128), 1)
    subs = lax.broadcasted_iota(jnp.int32, (8, 128), 0)
    base = jnp.where(lanes < 64, 0, 64)
    column = lanes - base
    results = []

    def place(k):
        side = 8 * k // HALF
        return side, 8 * k - side * HALF

    def spread(v, k):
        side, first = place(k)
        return [
            jnp.take_along_axis(work[v][side], base + (first + c), axis=1) for c in range(8)
        ]

    panel = spread(0, 0)
    for k in range(count):
        side, first = place(k)
        near = spread(k + 1, k) if k + 1 < count else None
        ahead = spread(k + 1, k + 1) if k + 1 < count else None
        weights = [[None] * 8 for _ in range(8)]
        inverses, lines = [], []
        scales = jnp.ones((8, 128), jnp.float32)
        for c in range(0, 8, 2):
            corner, cross, late = (
                row_of(panel[c], c),
                row_of(panel[c + 1], c),
                row_of(panel[c + 1], c + 1),
            )
            inv = 1.0 / corner
            second = corner * (1.0 / (corner * late - cross * cross))
            ratio = cross * inv
            weights[c][c + 1] = cross
            factor = panel[c] * inv
            rest = panel[c + 1] - factor * cross
            for d in range(c + 2, 8):
                weights[c][d] = row_of(panel[d], c)
                weights[c + 1][d] = row_of(panel[d], c + 1) - ratio * weights[c][d]
                panel[d] = (panel[d] - factor * weights[c][d]) - (
                    rest * weights[c + 1][d]
                ) * second
            pair = (jnp.where(subs > c, factor, 0.0), jnp.where(subs > c + 1, rest * second, 0.0))
            for e in range(2):
                inverses.append((inv, second)[e])
                scales = jnp.where(subs == c + e, inverses[-1], scales)
                line = [row_of(part, c + e) for part in work[k]]
                line[side] = line[side] + jnp.where(column == first + c + e, 1.0, 0.0)
                lines.append(line)
                work[k] = [part - pair[e] * along for part, along in zip(work[k], line)]
        if near is not None:
            for c in range(8):
                factor = near[c] * inverses[c]
                for d in range(c + 1, 8):
                    near[d] = near[d] - factor * weights[c][d]
                for d in range(8):
                    ahead[d] = ahead[d] - factor * row_of(near[c], d)
                work[k + 1] = [
                    part - factor * along for part, along in zip(work[k + 1], lines[c])
                ]
        panel = ahead
        scaled = [[part * inv for part in line] for line, inv in zip(lines, inverses)]
        for v in range(k + 2, count):
            there, at = place(v)
            for c in range(8):
                factor = jnp.take_along_axis(scaled[c][there], base + subs + at, axis=1)
                work[v] = [part - factor * along for part, along in zip(work[v], lines[c])]
        root = lax.sqrt(scales)
        unit = jnp.where(column == subs + first, 1.0, 0.0)
        own = jnp.where(column < subs + first, work[k][side], unit) * root
        other = work[k][0] * root if side else jnp.zeros((8, 128), jnp.float32)
        results.append((other, own) if side else (own, other))
    return results


def doubled_operator(value, coef):
    width = value.shape[1]
    lanes = lax.broadcasted_iota(jnp.int32, (value.shape[0], 128), 1)
    below, above = pltpu.roll(value, 1, 1), pltpu.roll(value, width - 1, 1)
    below = jnp.concatenate(
        [jnp.where(lanes == 0, 0.0, below[:, :128]), below[:, 128:]], axis=1
    )
    above = jnp.concatenate(
        [above[:, :-128], jnp.where(lanes == 127, 0.0, above[:, -128:])], axis=1
    )
    return coef * value + (below + above)


DOWN = 2.0**-13


def iterate_body(n_alt, chunk, seg_count, modes, width, scale_ref, *refs):
    blocks, image_refs = refs[:n_alt], refs[n_alt : n_alt + chunk]
    coef_ref, basis_ref, split_ref, gram_ref, inv_ref = refs[n_alt + chunk :]
    place = lax.axis_index("alt")
    flat = place * chunk
    freq = flat // seg_count
    first = flat - freq * seg_count
    total = n_alt * width
    for k, block in enumerate(blocks):
        source = place ^ k
        span = pl.ds(pl.multiple_of(source * width, width), width)
        start = block[0:modes, :] * (1.0 / float(total) ** 0.5)
        for i in range(chunk):
            basis_ref[i, :, span] = start
            change = block[pl.ds(modes + 1 + first + i, 1), :]
            coef_ref[i : i + 1, span] = (2.0 * scale_ref[freq]) * (
                block[modes : modes + 1, :] * (1.0 + relief * change)
            )
    split_ref[...] = jnp.zeros_like(split_ref)
    left = lax.broadcasted_iota(jnp.int32, (8, 128), 1) < 64

    def packed_row(i, at):
        return at // HALF * 128 + i * 64 + at % HALF

    def step(_, carry):
        for i in range(chunk):
            coef = coef_ref[i : i + 1, :]
            for at in range(0, modes, 16):
                image = doubled_operator(basis_ref[i, at : at + 16, :], coef)
                row = packed_row(i, at)
                for part in range(3):
                    piece = image.astype(jnp.bfloat16)
                    split_ref[part, row : row + 16, :] = piece
                    image = image - piece.astype(jnp.float32)
        gram_ref[...] = short_mmt(split_ref[0], split_ref[0]) * DOWN
        work = []
        for at in range(0, modes, 8):
            one, two = packed_row(0, at), packed_row(1, at)
            work.append(
                [
                    jnp.where(
                        left,
                        gram_ref[one : one + 8, side : side + 128],
                        gram_ref[two : two + 8, side : side + 128],
                    )
                    for side in (0, 128)
                ]
            )
        rows = inverse_factors(work)
        for at in range(0, modes, 16):
            for half in range(2):
                part = jnp.concatenate([rows[at // 8][half], rows[at // 8 + 1][half]], axis=0)
                part = part * DOWN**0.5
                here = lax.broadcasted_iota(jnp.int32, part.shape, 1) < 64
                span = slice(half * 128, half * 128 + 128)
                inv_ref[0, at : at + 16, span] = jnp.where(here, part, 0.0).astype(jnp.bfloat16)
                inv_ref[1, at : at + 16, span] = jnp.where(here, 0.0, part).astype(jnp.bfloat16)
        for i in range(chunk):
            for at in range(0, total, 256):
                basis_ref[i, :, at : at + 256] = sum(
                    short_mm(inv_ref[i], split_ref[part, :, at : at + 256]) for part in range(3)
                )
        return carry

    lax.fori_loop(0, ITERS - 1, step, 0, unroll=True)
    for i in range(chunk):
        for at in range(0, modes, 8):
            image_refs[i][at : at + 8, :] = doubled_operator(
                basis_ref[i, at : at + 8, :], coef_ref[i : i + 1, :]
            )


def unit_of(modes):
    rows = lax.broadcasted_iota(jnp.int32, (modes, modes), 0)
    return jnp.where(rows == lax.broadcasted_iota(jnp.int32, (modes, modes), 1), 1.0, 0.0)


def complex_mm(left, right):
    return (
        mm(left[0], right[0]) - mm(left[1], right[1]),
        mm(left[0], right[1]) + mm(left[1], right[0]),
    )


def finish_body(halves, modes, total, coef_ref, *refs):
    image_refs, basis_refs = refs[0:2], refs[2:4]
    turn_ref, inner_ref, rest_ref, gram_ref, double_ref = refs[4:]
    unit = unit_of(modes)
    gram_ref[...] = jnp.zeros_like(gram_ref)
    for i in range(2):
        image = image_refs[i][...]
        gram_ref[i, :, 0:modes] = mmt(image, image) * DOWN
    grams = [gram_ref[i, at : at + 8, :] for at in range(0, modes, 8) for i in range(2)]
    rows = inverse_factors([pack_pair(*grams[i : i + 2]) for i in range(0, len(grams), 2)])
    for k, pair in enumerate(rows):
        for i, part in enumerate(unpack_pair(*pair)):
            gram_ref[i, 8 * k : 8 * k + 8, :] = part * DOWN**0.5
    turns = []
    for i in range(2):
        inv = gram_ref[i, :, 0:modes]
        for at in range(0, total, 256):
            basis_refs[i][:, at : at + 256] = mm(inv, image_refs[i][:, at : at + 256])
    for i, ref in enumerate(basis_refs):
        for at in range(0, modes, 8):
            double_ref[at : at + 8, :] = doubled_operator(
                ref[at : at + 8, :], coef_ref[i : i + 1, :]
            )
        phase = (0.5 * phase_step) * mmt(ref[...], double_ref[...])
        square = mm(phase, phase)
        turns.append(
            (unit - 0.5 * square + mm(square, square) / 24.0, phase - mm(phase, square) / 6.0)
        )
    corr = mmt(basis_refs[1][...], basis_refs[0][...])
    inner = (mm(corr, turns[0][0]), mm(corr, turns[0][1]))
    turn = jnp.where(chain_place(halves) == 0, unit, gram_ref[0, :, 0:modes])
    turn_ref[...] = turn
    late = (mm(turns[1][0], corr), mm(turns[1][1], corr))
    rest = complex_mm(late, (mm(turns[0][0], turn), mm(turns[0][1], turn)))
    for part in range(2):
        inner_ref[part] = inner[part]
        rest_ref[part] = rest[part]


def chain_place(halves):
    return lax.axis_index("range") * halves + lax.rem(lax.axis_index("alt"), halves)


def product_body(next_ref, second_ref, rest_ref, out_ref):
    corr = mmt(next_ref[...], second_ref[...])
    for part in range(2):
        out_ref[part] = mm(corr, rest_ref[part])


def later_half(halves, bit):
    return lax.rem(chain_place(halves) // bit, 2) == 1


def pair_body(halves, bit, own_ref, other_ref, out_ref):
    later = later_half(halves, bit)
    own, other = (own_ref[0], own_ref[1]), (other_ref[0], other_ref[1])
    pairs = list(zip(own, other))
    out_ref[0], out_ref[1] = complex_mm(
        [jnp.where(later, a, b) for a, b in pairs], [jnp.where(later, b, a) for a, b in pairs]
    )


def fold(spans):
    while len(spans) > 1:
        pairs = [complex_mm(*spans[i : i + 2]) for i in range(0, len(spans) - 1, 2)]
        spans = pairs + spans[len(pairs) * 2 :]
    return spans[0]


def inside_body(halves, bits, *refs):
    turn_ref, inner_ref, out_ref = refs[len(bits) :]
    unit = unit_of(inner_ref.shape[1])
    spans = []
    for bit, ref in zip(bits, refs):
        later = later_half(halves, bit)
        spans.append((jnp.where(later, ref[0], unit), jnp.where(later, ref[1], 0.0)))
    reached = fold(spans)
    reached = (mm(turn_ref[...], reached[0]), mm(turn_ref[...], reached[1]))
    following = complex_mm((inner_ref[0], inner_ref[1]), reached)
    for part in range(2):
        out_ref[0, part] = reached[part]
        out_ref[1, part] = following[part]


def join_body(halves, group, backs, *refs):
    at = chain_place(halves) // group
    spans = []
    for back, ref in zip(backs, refs):
        missing = jnp.where(at < back, unit_of(ref.shape[1]), 0.0)
        spans.append((ref[0] + missing, ref[1]) if back else (ref[0], ref[1]))
    refs[-1][0], refs[-1][1] = fold(spans)


def group_span(halves, group, back, ref):
    there = chain_place(halves) // group >= back
    return jnp.where(there, ref[0], unit_of(ref.shape[1])), jnp.where(there, ref[1], 0.0)


def merge_body(halves, group, back, last, inside_ref, span_ref, out_ref):
    span = group_span(halves, group, back, span_ref)
    for i in range(2):
        merged = complex_mm((inside_ref[i, 0], inside_ref[i, 1]), span)
        for part in range(2):
            out_ref[i, part] = merged[part].T if last else merged[part]


def field_body(halves, group, back, n_alt, width, scale, source_ref, *refs):
    span_ref, inside_ref, first_ref, second_ref = refs[:4]
    place = lax.axis_index("alt")
    source = source_ref[place // halves]
    real, imag = source[0:1, :], source[1:2, :]
    left, right = group_span(halves, group, back, span_ref)
    came = (
        jnp.sum(left * real - right * imag, axis=1, keepdims=True),
        jnp.sum(left * imag + right * real, axis=1, keepdims=True),
    )
    rows = lax.broadcasted_iota(jnp.int32, source.shape, 0)
    amps = []
    for i in range(2):
        left, right = inside_ref[i, 0], inside_ref[i, 1]
        amp = (
            jnp.sum(left * came[0] - right * came[1], axis=0, keepdims=True),
            jnp.sum(left * came[1] + right * came[0], axis=0, keepdims=True),
        )
        amps.append(jnp.where(rows == 0, amp[0], jnp.where(rows == 1, amp[1], 0.0)))
    for k, out_ref in enumerate(refs[4:]):
        target = lax.rem(place + k, n_alt)
        span = pl.ds(pl.multiple_of(target * width, width), width)
        for i, ref in enumerate((first_ref, second_ref)):
            out_ref[i] = scale * mm(amps[i], ref[:, span])[0:2, :]


def settle_body(halves, n_alt, *refs):
    place = lax.axis_index("alt")
    out_ref = refs[n_alt]
    for k, part_ref in enumerate(refs[:n_alt]):
        source = lax.rem(place + n_alt - k, n_alt)
        chunk = part_ref.shape[0]
        freq, half = source // halves, lax.rem(source, halves)
        for i in range(chunk):
            out_ref[freq, half * chunk + i] = part_ref[i]


def local(freq_scale, base_profile, perturb, start_block, source):
    freqs = freq_scale.shape[0]
    seg_count = perturb.shape[0]
    modes, width = start_block.shape
    n_alt = lax.axis_size("alt")
    n_range = lax.axis_size("range")
    total = width * n_alt
    chunk = freqs * seg_count // n_alt
    halves = seg_count // chunk
    length = n_range * halves
    assert n_alt & (n_alt - 1) == 0 and modes == 2 * HALF
    assert chunk == 2 and halves * chunk == seg_count and halves * freqs == n_alt

    def device(freq, at):
        return at // halves * n_alt + freq * halves + at % halves

    def along_chain(value, steps):
        pairs = []
        for freq in range(freqs):
            for at in range(max(0, -steps), min(length, length - steps)):
                pairs.append((device(freq, at), device(freq, at + steps)))
        return lax.ppermute(value, ("range", "alt"), pairs)

    def around(value, k):
        return lax.ppermute(value, "alt", [(i, (i + k) % n_alt) for i in range(n_alt)])

    filler = jnp.zeros((-(modes + 1 + seg_count) % 8, width), jnp.float32)
    mine = jnp.concatenate([start_block, base_profile[None, :], perturb, filler], axis=0)
    found, bit = {0: mine}, n_alt
    while bit > 1:
        bit //= 2
        pairs = [(i, i ^ bit) for i in range(n_alt)]
        for key in list(found):
            found[key ^ bit] = lax.ppermute(found[key], "alt", pairs)
    blocks = [found[k] for k in range(n_alt)]
    flops = 2 * modes * modes * total
    image, other, coef = kernel_call(
        functools.partial(iterate_body, n_alt, chunk, seg_count, modes, width),
        [shape(modes, total)] * chunk + [shape(chunk, total)],
        [freq_scale] + blocks,
        [SM] + [VM] * n_alt,
        [
            pltpu.VMEM((chunk, modes, total), jnp.float32),
            pltpu.VMEM((3, 256, total), jnp.bfloat16),
            pltpu.VMEM((256, 256), jnp.float32),
            pltpu.VMEM((chunk, modes, 256), jnp.bfloat16),
        ],
        flops=2 * ITERS * chunk * flops,
    )
    following = along_chain(image, -1)
    first, second, turn, inner, rest = kernel_call(
        functools.partial(finish_body, halves, modes, total),
        [shape(modes, total)] * 2 + [shape(modes, modes)] + [shape(2, modes, modes)] * 2,
        [coef, image, other],
        [VM] * 3,
        [pltpu.VMEM((2, modes, 128), jnp.float32), pltpu.VMEM((modes, total), jnp.float32)],
        flops=16 * flops,
    )
    product = kernel_call(
        product_body, shape(2, modes, modes), [following, second, rest], [VM] * 3, flops=flops
    )

    group = 4
    groups = length // group
    assert groups * group == length and groups > 2

    def turned(value, size, k):
        pairs = []
        for freq in range(freqs):
            for at in range(length):
                goal = at // size * size + (at + k) % size
                pairs.append((device(freq, at), device(freq, goal)))
        return lax.ppermute(value, ("range", "alt"), pairs)

    span, beside, bits = product, [], (1, 2)
    for bit in bits:
        pairs = [
            (device(freq, at), device(freq, at ^ bit))
            for freq in range(freqs)
            for at in range(length)
        ]
        beside.append(lax.ppermute(span, ("range", "alt"), pairs))
        span = kernel_call(
            functools.partial(pair_body, halves, bit),
            shape(2, modes, modes),
            [span, beside[-1]],
            [VM] * 2,
            flops=flops,
        )

    def join(spans, backs):
        return kernel_call(
            functools.partial(join_body, halves, group, backs),
            shape(2, modes, modes),
            spans,
            [VM] * len(spans),
            flops=flops,
        )

    def from_back(backs):
        return [along_chain(span, group * back) if back else span for back in backs]

    if groups <= 4:
        backs = range(1, groups)
        came = [turned(span, length, group * back) for back in backs]
    else:
        backs = range(1, 5)
        span = join(from_back(backs), backs)
        reach = 4
        while groups > 4 * reach:
            backs = range(0, 4 * reach, reach)
            span = join(from_back(backs), backs)
            reach *= 4
        backs = range(0, groups, reach)
        came = from_back(backs)
    inside = kernel_call(
        functools.partial(inside_body, halves, bits),
        shape(2, 2, modes, modes),
        beside + [turn, inner],
        [VM] * 4,
        flops=flops,
    )
    rows = jnp.concatenate([source, jnp.zeros((freqs, 6, modes), jnp.float32)], axis=1)
    for at, back in enumerate(backs[:-1]):
        inside = kernel_call(
            functools.partial(merge_body, halves, group, back, at == len(backs) - 2),
            shape(2, 2, modes, modes),
            [inside, came[at]],
            [VM] * 2,
            flops=flops,
        )
    parts = kernel_call(
        functools.partial(
            field_body,
            halves,
            group,
            backs[-1],
            n_alt,
            width,
            (float(total) / float(modes)) ** 0.5,
        ),
        [shape(chunk, 2, width)] * n_alt,
        [rows, came[-1], inside, first, second],
        [VM] * 5,
    )
    parts = [parts[0]] + [around(parts[k], k) for k in range(1, n_alt)]
    return kernel_call(
        functools.partial(settle_body, halves, n_alt),
        shape(freqs, seg_count, 2, width),
        parts,
        [VM] * n_alt,
    )


def solution(mesh):
    in_specs = (P("freq"), P("alt"), P("range", "alt"), P(None, "alt"), P("freq", None, None))
    out_specs = P("freq", "range", None, "alt")
    return jax.shard_map(local, mesh=mesh, in_specs=in_specs, out_specs=out_specs, check_vma=False)
```

```python
import functools

import jax
import jax.numpy as jnp
from jax import lax
from jax.experimental import pallas as pl
from jax.experimental.pallas import tpu as pltpu
from jax.sharding import PartitionSpec as P

ITERS = 8

phase_step = 0.15
relief = 0.1
HIGHEST = lax.Precision.HIGHEST
VMEM_LIMIT = 48 * 2**20
HALF = 48


def mm(left, right):
    return lax.dot_general(
        left, right, (((1,), (0,)), ((), ())), precision=HIGHEST, preferred_element_type=jnp.float32
    )


def mmt(left, right):
    return lax.dot_general(
        left, right, (((1,), (1,)), ((), ())), precision=HIGHEST, preferred_element_type=jnp.float32
    )


def short_mm(left, right):
    return lax.dot_general(
        left, right, (((1,), (0,)), ((), ())), preferred_element_type=jnp.float32
    )


def short_mmt(left, right):
    return lax.dot_general(
        left, right, (((1,), (1,)), ((), ())), preferred_element_type=jnp.float32
    )


def kernel_call(body, out_shape, args, specs, scratch=(), flops=0):
    nbytes = sum(4 * a.size for a in args) + sum(4 * o.size for o in jax.tree.leaves(out_shape))
    return pl.pallas_call(
        body,
        out_shape=out_shape,
        in_specs=specs,
        out_specs=jax.tree.map(lambda _: pl.BlockSpec(memory_space=pltpu.VMEM), out_shape),
        scratch_shapes=scratch,
        cost_estimate=pl.CostEstimate(flops=flops, bytes_accessed=nbytes, transcendentals=0),
        compiler_params=pltpu.CompilerParams(vmem_limit_bytes=VMEM_LIMIT),
    )(*args)


VM = pl.BlockSpec(memory_space=pltpu.VMEM)
SM = pl.BlockSpec(memory_space=pltpu.SMEM)


def shape(*dims):
    return jax.ShapeDtypeStruct(dims, jnp.float32)


def row_of(value, at):
    return jnp.broadcast_to(value[at : at + 1, :], value.shape)


def pack_pair(one, two):
    left = lax.broadcasted_iota(jnp.int32, one.shape, 1) < 64
    return [
        jnp.where(left, one, pltpu.roll(two, 64, 1)),
        jnp.where(left, pltpu.roll(one, 128 - HALF, 1), pltpu.roll(two, 64 - HALF, 1)),
    ]


def unpack_pair(low, high):
    early = lax.broadcasted_iota(jnp.int32, low.shape, 1) < HALF
    return (
        jnp.where(early, low, pltpu.roll(high, HALF, 1)),
        jnp.where(early, pltpu.roll(low, 64, 1), pltpu.roll(high, 64 + HALF, 1)),
    )


def inverse_factors(work):
    work = [list(pair) for pair in work]
    count = len(work)
    lanes = lax.broadcasted_iota(jnp.int32, (8, 128), 1)
    subs = lax.broadcasted_iota(jnp.int32, (8, 128), 0)
    base = jnp.where(lanes < 64, 0, 64)
    column = lanes - base
    results = []

    def place(k):
        side = 8 * k // HALF
        return side, 8 * k - side * HALF

    def spread(v, k):
        side, first = place(k)
        return [
            jnp.take_along_axis(work[v][side], base + (first + c), axis=1) for c in range(8)
        ]

    panel = spread(0, 0)
    for k in range(count):
        side, first = place(k)
        near = spread(k + 1, k) if k + 1 < count else None
        ahead = spread(k + 1, k + 1) if k + 1 < count else None
        weights = [[None] * 8 for _ in range(8)]
        inverses, lines = [], []
        scales = jnp.ones((8, 128), jnp.float32)
        for c in range(0, 8, 2):
            corner, cross, late = (
                row_of(panel[c], c),
                row_of(panel[c + 1], c),
                row_of(panel[c + 1], c + 1),
            )
            inv = 1.0 / corner
            second = corner * (1.0 / (corner * late - cross * cross))
            ratio = cross * inv
            weights[c][c + 1] = cross
            factor = panel[c] * inv
            rest = panel[c + 1] - factor * cross
            for d in range(c + 2, 8):
                weights[c][d] = row_of(panel[d], c)
                weights[c + 1][d] = row_of(panel[d], c + 1) - ratio * weights[c][d]
                panel[d] = (panel[d] - factor * weights[c][d]) - (
                    rest * weights[c + 1][d]
                ) * second
            pair = (jnp.where(subs > c, factor, 0.0), jnp.where(subs > c + 1, rest * second, 0.0))
            for e in range(2):
                inverses.append((inv, second)[e])
                scales = jnp.where(subs == c + e, inverses[-1], scales)
                line = [row_of(part, c + e) for part in work[k]]
                line[side] = line[side] + jnp.where(column == first + c + e, 1.0, 0.0)
                lines.append(line)
                work[k] = [part - pair[e] * along for part, along in zip(work[k], line)]
        if near is not None:
            for c in range(8):
                factor = near[c] * inverses[c]
                for d in range(c + 1, 8):
                    near[d] = near[d] - factor * weights[c][d]
                for d in range(8):
                    ahead[d] = ahead[d] - factor * row_of(near[c], d)
                work[k + 1] = [
                    part - factor * along for part, along in zip(work[k + 1], lines[c])
                ]
        panel = ahead
        scaled = [[part * inv for part in line] for line, inv in zip(lines, inverses)]
        for v in range(k + 2, count):
            there, at = place(v)
            for c in range(8):
                factor = jnp.take_along_axis(scaled[c][there], base + subs + at, axis=1)
                work[v] = [part - factor * along for part, along in zip(work[v], lines[c])]
        root = lax.sqrt(scales)
        unit = jnp.where(column == subs + first, 1.0, 0.0)
        own = jnp.where(column < subs + first, work[k][side], unit) * root
        other = work[k][0] * root if side else jnp.zeros((8, 128), jnp.float32)
        results.append((other, own) if side else (own, other))
    return results


def doubled_operator(value, coef):
    width = value.shape[1]
    lanes = lax.broadcasted_iota(jnp.int32, (value.shape[0], 128), 1)
    below, above = pltpu.roll(value, 1, 1), pltpu.roll(value, width - 1, 1)
    below = jnp.concatenate(
        [jnp.where(lanes == 0, 0.0, below[:, :128]), below[:, 128:]], axis=1
    )
    above = jnp.concatenate(
        [above[:, :-128], jnp.where(lanes == 127, 0.0, above[:, -128:])], axis=1
    )
    return coef * value + (below + above)


DOWN = 2.0**-13


def iterate_body(n_alt, chunk, seg_count, modes, width, scale_ref, *refs):
    blocks, image_refs = refs[:n_alt], refs[n_alt : n_alt + chunk]
    coef_ref, basis_ref, split_ref, gram_ref, inv_ref = refs[n_alt + chunk :]
    place = lax.axis_index("alt")
    flat = place * chunk
    freq = flat // seg_count
    first = flat - freq * seg_count
    total = n_alt * width
    for k, block in enumerate(blocks):
        source = place ^ k
        span = pl.ds(pl.multiple_of(source * width, width), width)
        start = block[0:modes, :] * (1.0 / float(total) ** 0.5)
        for i in range(chunk):
            basis_ref[i, :, span] = start
            change = block[pl.ds(modes + 1 + first + i, 1), :]
            coef_ref[i : i + 1, span] = (2.0 * scale_ref[freq]) * (
                block[modes : modes + 1, :] * (1.0 + relief * change)
            )
    split_ref[...] = jnp.zeros_like(split_ref)
    left = lax.broadcasted_iota(jnp.int32, (8, 128), 1) < 64

    def packed_row(i, at):
        return at // HALF * 128 + i * 64 + at % HALF

    def step(n):
        for i in range(chunk):
            coef = coef_ref[i : i + 1, :]
            for at in range(0, modes, 16):
                image = doubled_operator(basis_ref[i, at : at + 16, :], coef)
                row = packed_row(i, at)
                for part in range(3):
                    piece = image.astype(jnp.bfloat16)
                    split_ref[3 * (n % 2) + part, row : row + 16, :] = piece
                    image = image - piece.astype(jnp.float32)
        gram_ref[...] = short_mmt(split_ref[3 * (n % 2)], split_ref[3 * (n % 2)]) * DOWN
        work = []
        for at in range(0, modes, 8):
            one, two = packed_row(0, at), packed_row(1, at)
            work.append(
                [
                    jnp.where(
                        left,
                        gram_ref[one : one + 8, side : side + 128],
                        gram_ref[two : two + 8, side : side + 128],
                    )
                    for side in (0, 128)
                ]
            )
        rows = inverse_factors(work)
        for at in range(0, modes, 16):
            for half in range(2):
                part = jnp.concatenate([rows[at // 8][half], rows[at // 8 + 1][half]], axis=0)
                part = part * DOWN**0.5
                here = lax.broadcasted_iota(jnp.int32, part.shape, 1) < 64
                span = slice(half * 128, half * 128 + 128)
                inv_ref[0, at : at + 16, span] = jnp.where(here, part, 0.0).astype(jnp.bfloat16)
                inv_ref[1, at : at + 16, span] = jnp.where(here, 0.0, part).astype(jnp.bfloat16)
        for i in range(chunk):
            for at in range(0, total, 256):
                basis_ref[i, :, at : at + 256] = sum(
                    short_mm(inv_ref[i], split_ref[3 * (n % 2) + part, :, at : at + 256])
                    for part in range(3)
                )

    for n in range(ITERS - 1):
        step(n)
    for i in range(chunk):
        for at in range(0, modes, 8):
            image_refs[i][at : at + 8, :] = doubled_operator(
                basis_ref[i, at : at + 8, :], coef_ref[i : i + 1, :]
            )


def unit_of(modes):
    rows = lax.broadcasted_iota(jnp.int32, (modes, modes), 0)
    return jnp.where(rows == lax.broadcasted_iota(jnp.int32, (modes, modes), 1), 1.0, 0.0)


def complex_mm(left, right):
    return (
        mm(left[0], right[0]) - mm(left[1], right[1]),
        mm(left[0], right[1]) + mm(left[1], right[0]),
    )


def finish_body(halves, modes, total, coef_ref, *refs):
    image_refs, basis_refs = refs[0:2], refs[2:4]
    turn_ref, inner_ref, rest_ref, gram_ref, double_ref = refs[4:]
    unit = unit_of(modes)
    gram_ref[...] = jnp.zeros_like(gram_ref)
    for i in range(2):
        image = image_refs[i][...]
        gram_ref[i, :, 0:modes] = mmt(image, image) * DOWN
    grams = [gram_ref[i, at : at + 8, :] for at in range(0, modes, 8) for i in range(2)]
    rows = inverse_factors([pack_pair(*grams[i : i + 2]) for i in range(0, len(grams), 2)])
    for k, pair in enumerate(rows):
        for i, part in enumerate(unpack_pair(*pair)):
            gram_ref[i, 8 * k : 8 * k + 8, :] = part * DOWN**0.5
    turns = []
    for i in range(2):
        inv = gram_ref[i, :, 0:modes]
        for at in range(0, total, 256):
            basis_refs[i][:, at : at + 256] = mm(inv, image_refs[i][:, at : at + 256])
    for i, ref in enumerate(basis_refs):
        for at in range(0, modes, 8):
            double_ref[at : at + 8, :] = doubled_operator(
                ref[at : at + 8, :], coef_ref[i : i + 1, :]
            )
        phase = (0.5 * phase_step) * mmt(ref[...], double_ref[...])
        square = mm(phase, phase)
        turns.append(
            (unit - 0.5 * square + mm(square, square) / 24.0, phase - mm(phase, square) / 6.0)
        )
    corr = mmt(basis_refs[1][...], basis_refs[0][...])
    inner = (mm(corr, turns[0][0]), mm(corr, turns[0][1]))
    turn = jnp.where(chain_place(halves) == 0, unit, gram_ref[0, :, 0:modes])
    turn_ref[...] = turn
    late = (mm(turns[1][0], corr), mm(turns[1][1], corr))
    rest = complex_mm(late, (mm(turns[0][0], turn), mm(turns[0][1], turn)))
    for part in range(2):
        inner_ref[part] = inner[part]
        rest_ref[part] = rest[part]


def chain_place(halves):
    return lax.axis_index("range") * halves + lax.rem(lax.axis_index("alt"), halves)


def product_body(next_ref, second_ref, rest_ref, out_ref):
    corr = mmt(next_ref[...], second_ref[...])
    for part in range(2):
        out_ref[part] = mm(corr, rest_ref[part])


def later_half(halves, bit):
    return lax.rem(chain_place(halves) // bit, 2) == 1


def pair_body(halves, bit, own_ref, other_ref, out_ref):
    later = later_half(halves, bit)
    own, other = (own_ref[0], own_ref[1]), (other_ref[0], other_ref[1])
    pairs = list(zip(own, other))
    out_ref[0], out_ref[1] = complex_mm(
        [jnp.where(later, a, b) for a, b in pairs], [jnp.where(later, b, a) for a, b in pairs]
    )


def fold(spans):
    while len(spans) > 1:
        pairs = [complex_mm(*spans[i : i + 2]) for i in range(0, len(spans) - 1, 2)]
        spans = pairs + spans[len(pairs) * 2 :]
    return spans[0]


def inside_body(halves, bits, *refs):
    turn_ref, inner_ref, out_ref = refs[len(bits) :]
    unit = unit_of(inner_ref.shape[1])
    spans = []
    for bit, ref in zip(bits, refs):
        later = later_half(halves, bit)
        spans.append((jnp.where(later, ref[0], unit), jnp.where(later, ref[1], 0.0)))
    reached = fold(spans)
    reached = (mm(turn_ref[...], reached[0]), mm(turn_ref[...], reached[1]))
    following = complex_mm((inner_ref[0], inner_ref[1]), reached)
    for part in range(2):
        out_ref[0, part] = reached[part]
        out_ref[1, part] = following[part]


def join_body(halves, group, backs, *refs):
    at = chain_place(halves) // group
    spans = []
    for back, ref in zip(backs, refs):
        missing = jnp.where(at < back, unit_of(ref.shape[1]), 0.0)
        spans.append((ref[0] + missing, ref[1]) if back else (ref[0], ref[1]))
    refs[-1][0], refs[-1][1] = fold(spans)


def group_span(halves, group, back, ref):
    there = chain_place(halves) // group >= back
    return jnp.where(there, ref[0], unit_of(ref.shape[1])), jnp.where(there, ref[1], 0.0)


def merge_body(halves, group, back, last, inside_ref, span_ref, out_ref):
    span = group_span(halves, group, back, span_ref)
    for i in range(2):
        merged = complex_mm((inside_ref[i, 0], inside_ref[i, 1]), span)
        for part in range(2):
            out_ref[i, part] = merged[part].T if last else merged[part]


def field_body(halves, group, back, n_alt, width, scale, source_ref, *refs):
    span_ref, inside_ref, first_ref, second_ref = refs[:4]
    place = lax.axis_index("alt")
    source = source_ref[place // halves]
    real, imag = source[0:1, :], source[1:2, :]
    left, right = group_span(halves, group, back, span_ref)
    came = (
        jnp.sum(left * real - right * imag, axis=1, keepdims=True),
        jnp.sum(left * imag + right * real, axis=1, keepdims=True),
    )
    rows = lax.broadcasted_iota(jnp.int32, source.shape, 0)
    amps = []
    for i in range(2):
        left, right = inside_ref[i, 0], inside_ref[i, 1]
        amp = (
            jnp.sum(left * came[0] - right * came[1], axis=0, keepdims=True),
            jnp.sum(left * came[1] + right * came[0], axis=0, keepdims=True),
        )
        amps.append(jnp.where(rows == 0, amp[0], jnp.where(rows == 1, amp[1], 0.0)))
    for k, out_ref in enumerate(refs[4:]):
        target = lax.rem(place + k, n_alt)
        span = pl.ds(pl.multiple_of(target * width, width), width)
        for i, ref in enumerate((first_ref, second_ref)):
            out_ref[i] = scale * mm(amps[i], ref[:, span])[0:2, :]


def settle_body(halves, n_alt, *refs):
    place = lax.axis_index("alt")
    out_ref = refs[n_alt]
    for k, part_ref in enumerate(refs[:n_alt]):
        source = lax.rem(place + n_alt - k, n_alt)
        chunk = part_ref.shape[0]
        freq, half = source // halves, lax.rem(source, halves)
        for i in range(chunk):
            out_ref[freq, half * chunk + i] = part_ref[i]


def local(freq_scale, base_profile, perturb, start_block, source):
    freqs = freq_scale.shape[0]
    seg_count = perturb.shape[0]
    modes, width = start_block.shape
    n_alt = lax.axis_size("alt")
    n_range = lax.axis_size("range")
    total = width * n_alt
    chunk = freqs * seg_count // n_alt
    halves = seg_count // chunk
    length = n_range * halves
    assert n_alt & (n_alt - 1) == 0 and modes == 2 * HALF
    assert chunk == 2 and halves * chunk == seg_count and halves * freqs == n_alt

    def device(freq, at):
        return at // halves * n_alt + freq * halves + at % halves

    def along_chain(value, steps):
        pairs = []
        for freq in range(freqs):
            for at in range(max(0, -steps), min(length, length - steps)):
                pairs.append((device(freq, at), device(freq, at + steps)))
        return lax.ppermute(value, ("range", "alt"), pairs)

    def around(value, k):
        return lax.ppermute(value, "alt", [(i, (i + k) % n_alt) for i in range(n_alt)])

    filler = jnp.zeros((-(modes + 1 + seg_count) % 8, width), jnp.float32)
    mine = jnp.concatenate([start_block, base_profile[None, :], perturb, filler], axis=0)
    found, bit = {0: mine}, n_alt
    while bit > 1:
        bit //= 2
        pairs = [(i, i ^ bit) for i in range(n_alt)]
        for key in list(found):
            found[key ^ bit] = lax.ppermute(found[key], "alt", pairs)
    blocks = [found[k] for k in range(n_alt)]
    flops = 2 * modes * modes * total
    image, other, coef = kernel_call(
        functools.partial(iterate_body, n_alt, chunk, seg_count, modes, width),
        [shape(modes, total)] * chunk + [shape(chunk, total)],
        [freq_scale] + blocks,
        [SM] + [VM] * n_alt,
        [
            pltpu.VMEM((chunk, modes, total), jnp.float32),
            pltpu.VMEM((6, 256, total), jnp.bfloat16),
            pltpu.VMEM((256, 256), jnp.float32),
            pltpu.VMEM((chunk, modes, 256), jnp.bfloat16),
        ],
        flops=2 * ITERS * chunk * flops,
    )
    following = along_chain(image, -1)
    first, second, turn, inner, rest = kernel_call(
        functools.partial(finish_body, halves, modes, total),
        [shape(modes, total)] * 2 + [shape(modes, modes)] + [shape(2, modes, modes)] * 2,
        [coef, image, other],
        [VM] * 3,
        [pltpu.VMEM((2, modes, 128), jnp.float32), pltpu.VMEM((modes, total), jnp.float32)],
        flops=16 * flops,
    )
    product = kernel_call(
        product_body, shape(2, modes, modes), [following, second, rest], [VM] * 3, flops=flops
    )

    group = 4
    groups = length // group
    assert groups * group == length and groups > 2

    def turned(value, size, k):
        pairs = []
        for freq in range(freqs):
            for at in range(length):
                goal = at // size * size + (at + k) % size
                pairs.append((device(freq, at), device(freq, goal)))
        return lax.ppermute(value, ("range", "alt"), pairs)

    span, beside, bits = product, [], (1, 2)
    for bit in bits:
        pairs = [
            (device(freq, at), device(freq, at ^ bit))
            for freq in range(freqs)
            for at in range(length)
        ]
        beside.append(lax.ppermute(span, ("range", "alt"), pairs))
        span = kernel_call(
            functools.partial(pair_body, halves, bit),
            shape(2, modes, modes),
            [span, beside[-1]],
            [VM] * 2,
            flops=flops,
        )

    def join(spans, backs):
        return kernel_call(
            functools.partial(join_body, halves, group, backs),
            shape(2, modes, modes),
            spans,
            [VM] * len(spans),
            flops=flops,
        )

    def from_back(backs):
        return [along_chain(span, group * back) if back else span for back in backs]

    if groups <= 4:
        backs = range(1, groups)
        came = [turned(span, length, group * back) for back in backs]
    else:
        backs = range(1, 5)
        span = join(from_back(backs), backs)
        reach = 4
        while groups > 4 * reach:
            backs = range(0, 4 * reach, reach)
            span = join(from_back(backs), backs)
            reach *= 4
        backs = range(0, groups, reach)
        came = from_back(backs)
    inside = kernel_call(
        functools.partial(inside_body, halves, bits),
        shape(2, 2, modes, modes),
        beside + [turn, inner],
        [VM] * 4,
        flops=flops,
    )
    rows = jnp.concatenate([source, jnp.zeros((freqs, 6, modes), jnp.float32)], axis=1)
    for at, back in enumerate(backs[:-1]):
        inside = kernel_call(
            functools.partial(merge_body, halves, group, back, at == len(backs) - 2),
            shape(2, 2, modes, modes),
            [inside, came[at]],
            [VM] * 2,
            flops=flops,
        )
    parts = kernel_call(
        functools.partial(
            field_body,
            halves,
            group,
            backs[-1],
            n_alt,
            width,
            (float(total) / float(modes)) ** 0.5,
        ),
        [shape(chunk, 2, width)] * n_alt,
        [rows, came[-1], inside, first, second],
        [VM] * 5,
    )
    parts = [parts[0]] + [around(parts[k], k) for k in range(1, n_alt)]
    return kernel_call(
        functools.partial(settle_body, halves, n_alt),
        shape(freqs, seg_count, 2, width),
        parts,
        [VM] * n_alt,
    )


def solution(mesh):
    in_specs = (P("freq"), P("alt"), P("range", "alt"), P(None, "alt"), P("freq", None, None))
    out_specs = P("freq", "range", None, "alt")
    return jax.shard_map(local, mesh=mesh, in_specs=in_specs, out_specs=out_specs, check_vma=False)
```
